32 devices in a mesh: pole: 2 (over x), row: 8 (over z, y), col: 2 (over core).
Axes of the slice: x: 2, y: 2, z: 4, core: 2. Of those that a mesh axis runs over, the one named last changes fastest.
Arguments:
- panel: bfloat16 [4, 8, 2, 512, 128], P(('pole', 'col'), None, None, 'row'), parts along dimension 0, may hold values from -6 to 6
- tiles: bfloat16 [352, 2, 512, 512], P(('pole', 'row', 'col')), parts along dimension 0, may hold values from -0.078125 to 0.078125
- tile_slot: int32 [352], P(('pole', 'row', 'col')), parts along dimension 0, may hold values from 0 to 1
- tile_col: int32 [352], P(('pole', 'row', 'col')), parts along dimension 0, may hold values from 0 to 7
- pole_weight: float32 [4], P('pole'), parts along dimension 0, may hold values from -4 to 4
- box_orbitals: int32 [64, 256], P(('pole', 'row', 'col')), parts along dimension 0, may hold values from 0 to 8191, as said below
- box_basis: bfloat16 [64, 256, 512], P(('pole', 'row', 'col')), parts along dimension 0, may hold values from -0.375 to 0.375
- supernode_basis: bfloat16 [64, 128, 512], P(('pole', 'row', 'col')), parts along dimension 0, may hold values from -0.5 to 0.5
Outputs:
- inverse_column: float32 [32, 2, 512, 128], P(('pole', 'row'), None, 'col'), parts along dimension 0
- density: float32 [64, 512], P(('pole', 'row', 'col')), parts along dimension 0
The draws below stay inside these ranges and needn't reach their ends.
There are 2 independent parts, one for each index of `pole`. The reference program is written for one: setup_inputs(seed, part) draws one part's arguments, and reference() takes and returns one part's arrays. A program takes and returns all parts, laid end to end along the dimension named above; each array names one. Nothing has to cross between parts.
Inputs may be any that keep to these rules, and one draw needn't show every extreme that they name: `box_orbitals`: let a row g be held by device r * 2 + c where r = (g // 512) // 2 and c = (g % 512) // (512 // 2). The 2 boxes of one device take at most 64 rows (counted with repeats) held by any one device, and exactly 64 from some device.
All inputs are finite; a program needn't handle non-finite values.
Results may differ from the reference program's by a relative error of at most 0.0029.
Values may be sent and summed in bfloat16 or wider, within the bound.
A program may use at most 64 MiB of HBM per device.

```python
import jax
import jax.numpy as jnp
from jax import lax

B = 512
S = 128
PTS = 512
ORB_BOX = 256
NJP = 8
BR_DEV = 2
TILE_DEV = 11
BOX_DEV = 2
TILES = 176
NBOX = 32
N_ROW = 8
N_COL = 2


def draw_box_orbitals(key, part):
    devices = N_ROW * N_COL
    per_device = BOX_DEV * ORB_BOX
    capacity = 2 * per_device // devices
    half_rows = B // N_COL
    local_total = BR_DEV * half_rows

    def one_device(device_index):
        device_key = jax.random.fold_in(key, device_index + 7919)
        subkeys = jax.random.split(device_key, 4)
        forced = jax.random.randint(subkeys[0], (), 0, devices).astype(jnp.int32)
        others = jnp.arange((devices - 1) * capacity, dtype=jnp.int32) // capacity
        others = others + (others >= forced).astype(jnp.int32)
        others = jax.random.permutation(subkeys[1], others)[:per_device - capacity]
        sources = jnp.concatenate([jnp.full((capacity,), 1, jnp.int32) * forced, others])
        sources = jax.random.permutation(subkeys[2], sources)
        local_pick = jax.random.randint(subkeys[3], (per_device,), 0, local_total).astype(jnp.int32)
        block_row = sources // N_COL * BR_DEV + local_pick // half_rows
        return block_row * B + sources % N_COL * half_rows + local_pick % half_rows
    result = jax.vmap(one_device)(jnp.arange(devices, dtype=jnp.int32))
    return result.reshape(devices * BOX_DEV, ORB_BOX).astype(jnp.int32)


def touch_ends(array, key, smallest, largest):
    longest = array.shape.index(max(array.shape))
    spots = []
    for shift in (0, 1):
        where = [jax.random.randint(jax.random.fold_in(key, axis), (), 0, length) for axis, length in enumerate(array.shape)]
        where[longest] = (where[longest] + shift) % array.shape[longest]
        spots.append(tuple(where))
    return array.at[spots[0]].set(smallest).at[spots[1]].set(largest)


def level_of(own_key, shape, cuts, low, largest):
    loudness = 1.0
    for axis_at, blocks in cuts:
        steps = jax.random.uniform(jax.random.fold_in(jax.random.fold_in(own_key, 6), axis_at), (blocks,), jnp.float32, low / len(cuts), largest / len(cuts))
        loudness = loudness * jnp.repeat(jnp.exp(steps), shape[axis_at] // blocks).reshape((-1,) + (1,) * (len(shape) - 1 - axis_at))
    return loudness


def normal_values(stream_key, shape, spread, bound, shards=(), kind=jnp.bfloat16):
    array = spread * jax.random.normal(stream_key, shape, jnp.float32)
    if shards:
        array = array * level_of(stream_key, shape, shards, -0.22, 0.18)
    return jnp.clip(array, -bound, bound).astype(kind)


def setup_inputs(seed: int = 0, part: int = 0) -> dict:
    seeds = jax.random.split(jax.random.key(seed), 9)
    part_splits = jax.random.split(jax.random.fold_in(seeds[8], part), 9)
    panel = normal_values(part_splits[0], (N_COL, NJP, 2, B, S), 1.0, 6.0, ((0, 2), (3, 8)))
    tiles = normal_values(part_splits[1], (TILES, 2, B, B), (2 * B * TILE_DEV // BR_DEV) ** -0.5, 0.078125, ((0, 16),))
    tile_slot = touch_ends(jax.random.randint(part_splits[2], (TILES,), 0, BR_DEV), jax.random.fold_in(part_splits[2], 1), 0, BR_DEV - 1).astype(jnp.int32)
    tile_col = touch_ends(jax.random.randint(part_splits[3], (TILES,), 0, NJP), jax.random.fold_in(part_splits[3], 1), 0, NJP - 1).astype(jnp.int32)
    pole_weight = normal_values(part_splits[4], (2,), 1.0, 4.0, (), jnp.float32)
    box_orbitals = draw_box_orbitals(jax.random.fold_in(jax.random.fold_in(seeds[8], part), 71), part)
    box_basis = normal_values(part_splits[6], (NBOX, ORB_BOX, PTS), ORB_BOX ** -0.5, 0.375, ((0, 16),))
    supernode_basis = normal_values(part_splits[7], (NBOX, S, PTS), S ** -0.5, 0.5, ((0, 16),))
    return {"panel": panel, "tiles": tiles, "tile_slot": tile_slot, "tile_col": tile_col, "pole_weight": pole_weight, "box_orbitals": box_orbitals, "box_basis": box_basis, "supernode_basis": supernode_basis}


def reference(panel, tiles, tile_slot, tile_col, pole_weight, box_orbitals, box_basis, supernode_basis):
    tile_total = tiles.shape[0]

    def add_tile(column, inputs):
        tile_block, slot_row, block_col, tile_index = inputs
        device = tile_index // TILE_DEV
        block_row = ((device // N_COL) * BR_DEV + slot_row).astype(jnp.int32)
        factor = panel[device % N_COL, block_col].astype(jnp.float32)
        tile_wide = tile_block.astype(jnp.float32)
        real_part = jnp.dot(tile_wide[0], factor[0]) - jnp.dot(tile_wide[1], factor[1])
        imag_part = jnp.dot(tile_wide[0], factor[1]) + jnp.dot(tile_wide[1], factor[0])
        update = jnp.stack([real_part, imag_part], axis=0)
        column = column.at[block_row].add(update)
        return column, None

    start_column = jnp.zeros((BR_DEV * N_ROW, 2, B, S), jnp.float32)
    indices = jnp.arange(tile_total, dtype=jnp.int32)
    column, _ = lax.scan(add_tile, start_column, (tiles, tile_slot, tile_col, indices))
    inverse_column = -column
    density_rows = (pole_weight[0] * inverse_column[:, 1] + pole_weight[1] * inverse_column[:, 0]).astype(jnp.bfloat16)
    density_rows = density_rows.reshape(-1, S)
    picked = jnp.take(density_rows, box_orbitals, axis=0)
    projected = jnp.einsum("nas,nap->nsp", picked.astype(jnp.float32), box_basis.astype(jnp.float32))
    density = jnp.sum(supernode_basis.astype(jnp.float32) * projected, axis=1)
    return inverse_column, density
```

```python
import functools

import jax
import jax.numpy as jnp
from jax import lax
from jax.experimental import pallas as pl
from jax.experimental.pallas import tpu as pltpu
from jax.sharding import PartitionSpec as P

BR_DEV = 2
MESH = pl.DeviceIdType.MESH


def log2(value):
    assert value & (value - 1) == 0
    return value.bit_length() - 1


def kernel(
    rows, cols, slot_ref, tcol_ref, weight_ref, panel, tiles, orbitals, basis, super_basis,
    inv_ref, density_ref, own, near, third, last,
    tile_buf, basis_buf, super_buf, orb_buf, acc, half_in, pick_hot, basis_hot, order_buf, local_buf,
    send_rows, recv_rows, local_sem, send_sem, recv_sem, token, col_sem, orb_send, orb_recv, row_send, row_recv,
):
    lanes_y = 2
    depth_z = rows // lanes_y
    peers = rows * cols
    r = lax.axis_index("row")
    c = lax.axis_index("col")
    me = r * cols + c
    z = r // lanes_y
    y = r % lanes_y
    shard_rows = panel.shape[3]
    width = panel.shape[4]
    pieces = panel.shape[1]
    split_at = pieces // 2
    tile_count = tiles.shape[0]
    block = tiles.shape[2]
    half = block // cols
    pair = lanes_y * shard_rows
    boxes, orbs = orbitals.shape
    capacity = send_rows.shape[1]

    inner = 1 - 2 * (z // (depth_z // 2))
    corner = jnp.logical_or(z == 0, z == depth_z - 1)
    middle = jnp.logical_not(corner)
    other = r + 1 - 2 * y
    inward = r + lanes_y * inner
    outward = r - lanes_y * inner
    buffers = (own, near, third, last)
    places = (
        z,
        z + inner,
        jnp.where(corner, z + 2 * inner, z - inner),
        jnp.where(corner, z + 3 * inner, z + 2 * inner),
    )
    IN, OUT, Y = 0, 1, 2

    def spot(index):
        return {"row": index // cols, "col": index % cols}

    loads = [
        pltpu.make_async_copy(panel.at[0], own.at[y], local_sem.at[0]),
        pltpu.make_async_copy(orbitals, orb_buf.at[me], local_sem.at[4]),
        pltpu.make_async_copy(basis, basis_buf, local_sem.at[2]),
        pltpu.make_async_copy(tiles, tile_buf, local_sem.at[1]),
        pltpu.make_async_copy(super_basis, super_buf, local_sem.at[3]),
    ]
    for load in loads:
        load.start()

    barrier = pltpu.get_barrier_semaphore()
    for device in (
        {"row": other}, {"col": 1 - c}, {"row": other, "col": 1 - c}, {"row": inward},
    ):
        pl.semaphore_signal(barrier, inc=1, device_id=device, device_id_type=MESH)

    @pl.when(middle)
    def _():
        pl.semaphore_signal(barrier, inc=1, device_id={"row": outward}, device_id_type=MESH)
        pl.semaphore_wait(barrier, 5)

    @pl.when(corner)
    def _():
        pl.semaphore_wait(barrier, 4)

    def copy(link, kind, source, target, lane, p):
        row = (inward, outward, other)[link]
        src = panel.at[0, p] if source is None else buffers[source].at[lane, p]
        return pltpu.make_async_remote_copy(
            src_ref=src, dst_ref=buffers[target].at[lane, p],
            send_sem=send_sem.at[link, kind, p], recv_sem=recv_sem.at[target, lane, p],
            device_id={"row": row}, device_id_type=MESH,
        )

    def arrived(target, lane, p):
        dst = buffers[target].at[lane, p]
        pltpu.make_async_remote_copy(
            src_ref=dst, dst_ref=dst, send_sem=send_sem.at[0, 0, p], recv_sem=recv_sem.at[target, lane, p],
            device_id={"row": other}, device_id_type=MESH,
        ).wait_recv()

    def each(low, high, body):
        def run(h, carry):
            body(h)
            return carry
        lax.fori_loop(low, high, run, 0)

    corner_sends = {
        "own_in": (IN, 0, None, 2, y), "own_y": (Y, 0, None, 0, y),
        "extra": (IN, 1, 0, 2, 1 - y),
        "near_y": (Y, 1, 1, 1, y), "third_y": (Y, 2, 2, 2, y), "last_y": (Y, 3, 3, 3, y),
    }
    middle_sends = {
        "own_out": (OUT, 0, None, 1, y), "own_in": (IN, 0, None, 1, y), "own_y": (Y, 0, None, 0, y),
        "third_in": (IN, 1, 2, 3, y),
        "near_out": (OUT, 1, 1, 2, y), "near_y": (Y, 1, 1, 1, y),
        "last_out": (OUT, 2, 3, 3, y), "last_y": (Y, 2, 3, 3, y),
        "extra": (OUT, 3, 3, 3, 1 - y),
    }

    def at_corner(name, p):
        return copy(*corner_sends[name], p)

    def at_middle(name, p):
        return copy(*middle_sends[name], p)

    @pl.when(corner)
    def _():
        def go(p):
            at_corner("own_in", p).start()
            at_corner("own_y", p).start()
        each(0, pieces, go)

    @pl.when(middle)
    def _():
        def go(p):
            at_middle("own_out", p).start()
            at_middle("own_in", p).start()
            at_middle("own_y", p).start()
        each(0, pieces, go)

    acc[...] = jnp.zeros_like(acc)
    block_bits, half_bits = log2(block), log2(half)

    def split(g):
        row_block = g >> block_bits
        within = g & (block - 1)
        source = (row_block >> log2(BR_DEV)) * cols + (within >> half_bits)
        local = (row_block & (BR_DEV - 1)) * half + (within & (half - 1))
        return source, local

    def ranks(masks):
        before = lax.broadcasted_iota(jnp.int32, (orbs, orbs), 0)
        after = lax.broadcasted_iota(jnp.int32, (orbs, orbs), 1)
        upper = jnp.where(before <= after, 1.0, 0.0).astype(jnp.bfloat16)
        seen = jnp.zeros((masks[0].shape[0], 1), jnp.float32)
        result = []
        for mask in masks:
            counted = jnp.dot(mask.astype(jnp.bfloat16), upper, preferred_element_type=jnp.float32)
            result.append(counted - 1.0 + seen)
            seen = seen + jnp.sum(mask, axis=1, keepdims=True)
        return result

    def place_basis():
        loads[1].wait()
        loads[2].wait()
        masks = []
        peer_id = lax.broadcasted_iota(jnp.int32, (peers, orbs), 0)
        for n in range(boxes):
            source, _ = split(orb_buf[me, n:n + 1, :])
            masks.append(jnp.where(peer_id == source, 1.0, 0.0))
        order = ranks(masks)
        arrive = lax.broadcasted_iota(jnp.int32, (peers * capacity, orbs), 0).astype(jnp.float32)
        for n in range(boxes):
            position = jnp.sum(
                masks[n] * (order[n] + (peer_id * capacity).astype(jnp.float32)), axis=0, keepdims=True)
            hot = jnp.where(arrive == position, 1.0, 0.0).astype(jnp.bfloat16)
            basis_hot[n] = jnp.dot(hot, basis_buf[n], preferred_element_type=jnp.float32).astype(jnp.bfloat16)

    def orb_copy(k):
        return pltpu.make_async_remote_copy(
            src_ref=orbitals, dst_ref=orb_buf.at[me], send_sem=orb_send.at[k], recv_sem=orb_recv.at[k],
            device_id=spot((me + k) % peers), device_id_type=MESH,
        )

    def rank_orbitals():
        for k in range(1, peers):
            origin = (me + peers - k) % peers
            dst = orb_buf.at[origin]
            pltpu.make_async_remote_copy(
                src_ref=dst, dst_ref=dst, send_sem=orb_send.at[k], recv_sem=orb_recv.at[k],
                device_id=spot(origin), device_id_type=MESH,
            ).wait_recv()
        asked = []
        for n in range(boxes):
            g = jnp.concatenate([orb_buf[q, n:n + 1, :] for q in range(peers)], axis=0)
            source, local = split(g)
            asked.append((jnp.where(source == me, 1.0, 0.0), local.astype(jnp.float32)))
        order = ranks([a[0] for a in asked])
        for n in range(boxes):
            order_buf[n] = jnp.where(asked[n][0] > 0.5, order[n], -1.0)
            local_buf[n] = asked[n][1] + 1.0

    def place_picks(q):
        place = lax.broadcasted_iota(jnp.int32, (capacity, orbs), 0).astype(jnp.float32)
        row_id = lax.broadcasted_iota(jnp.int32, (capacity, BR_DEV * half), 1).astype(jnp.float32)
        found = jnp.zeros((capacity, 1), jnp.float32)
        for n in range(boxes):
            hit = place == order_buf[n, pl.ds(q, 1), :]
            found = found + jnp.sum(jnp.where(hit, local_buf[n, pl.ds(q, 1), :], 0.0), axis=1, keepdims=True)
        spot_rows = pl.ds(pl.multiple_of(q * capacity, capacity), capacity)
        pick_hot[spot_rows, :] = jnp.where(row_id == found - 1.0, 1.0, 0.0).astype(jnp.bfloat16)

    def product(which, t, out_rows):
        j = tcol_ref[t]
        offset = pl.multiple_of(places[which] * pair, pair)
        left = jnp.concatenate(
            [tile_buf[t, 0, out_rows, pl.ds(offset, pair)], tile_buf[t, 1, out_rows, pl.ds(offset, pair)]], axis=1)
        parts = [buffers[which][k, j] for k in range(lanes_y)]
        real = jnp.concatenate([p[0] for p in parts], axis=0)
        imag = jnp.concatenate([p[1] for p in parts], axis=0)
        right = jnp.concatenate(
            [jnp.concatenate([real, imag], axis=1), jnp.concatenate([-imag, real], axis=1)], axis=0)
        return jnp.dot(left, right, preferred_element_type=jnp.float32)

    def several(which, start, count, out_rows):
        values = [product(which, start + k, out_rows) for k in range(count)]
        for s in range(BR_DEV):
            total = jnp.where(slot_ref[start] == s, values[0], 0.0)
            for k in range(1, count):
                total = total + jnp.where(slot_ref[start + k] == s, values[k], 0.0)
            acc[s, out_rows, :] += total

    everything = pl.ds(0, block)

    def share(which, p):
        each(p * tile_count // pieces, (p + 1) * tile_count // pieces, lambda t: several(which, t, 1, everything))

    place_basis()

    def first(p):
        @pl.when(corner)
        def _():
            arrived(1, y, p)
            at_corner("near_y", p).start()
            arrived(0, 1 - y, p)
            at_corner("extra", p).start()

        @pl.when(middle)
        def _():
            arrived(2, y, p)
            at_middle("third_in", p).start()
            arrived(1, y, p)
            at_middle("near_out", p).start()
            at_middle("near_y", p).start()

            @pl.when(p == 0)
            def _():
                pl.semaphore_signal(token.at[0], inc=1, device_id={"row": inward}, device_id_type=MESH)

            @pl.when(p == pieces - 1)
            def _():
                pl.semaphore_wait(token.at[0], 1)
                pl.semaphore_signal(token.at[1], inc=1, device_id={"row": outward}, device_id_type=MESH)

    each(0, pieces, first)

    @pl.when(corner)
    def _():
        pl.semaphore_wait(token.at[1], 1)

    for k in range(1, peers):
        orb_copy(k).start()

    @pl.when(middle)
    def _():
        each(0, pieces, lambda p: arrived(0, 1 - y, p))

    loads[0].wait()
    loads[3].wait()

    def second(p):
        @pl.when(corner)
        def _():
            arrived(2, y, p)
            at_corner("third_y", p).start()

        @pl.when(middle)
        def _():
            arrived(3, y, p)
            at_middle("last_out", p).start()
            at_middle("last_y", p).start()

        share(0, p)

    each(0, pieces, second)
    each(0, pieces, lambda p: arrived(1, 1 - y, p))
    per = peers // (pieces - split_at)

    def closing(p):
        @pl.when(corner)
        def _():
            arrived(3, y, p)

            @pl.when(p >= split_at)
            def _():
                at_corner("last_y", p).start()

        @pl.when(jnp.logical_and(middle, p < split_at))
        def _():
            arrived(3, 1 - y, p)
            at_middle("extra", p).start()

        share(1, p)

        @pl.when(p == split_at - 1)
        def _():
            rank_orbitals()

        @pl.when(p >= split_at)
        def _():
            each((p - split_at) * per, (p - split_at + 1) * per, place_picks)

    each(0, pieces, closing)
    each(0, pieces, lambda p: arrived(2, 1 - y, p))
    for start in range(0, tile_count, 4):
        several(2, start, min(4, tile_count - start), everything)

    @pl.when(corner)
    def _():
        each(0, split_at, lambda p: arrived(3, 1 - y, p))
    each(split_at, pieces, lambda p: arrived(3, 1 - y, p))

    mine = pl.ds(pl.multiple_of(c * half, half), half)
    theirs = pl.ds(pl.multiple_of((1 - c) * half, half), half)
    for start in range(0, tile_count, 4):
        several(3, start, min(4, tile_count - start), theirs)
    swap = pltpu.make_async_remote_copy(
        src_ref=acc.at[:, theirs, :], dst_ref=half_in, send_sem=col_sem.at[0], recv_sem=col_sem.at[1],
        device_id={"col": 1 - c}, device_id_type=MESH,
    )
    swap.start()
    for start in range(0, tile_count, 4):
        several(3, start, min(4, tile_count - start), mine)
    swap.wait_recv()
    density_rows = []
    for s in range(BR_DEV):
        column = -(acc[s, mine, :] + half_in[s])
        real, imag = column[:, :width], column[:, width:]
        density_rows.append((weight_ref[0] * imag + weight_ref[1] * real).astype(jnp.bfloat16))
    density_rows = jnp.concatenate(density_rows, axis=0)

    group = lanes_y * cols

    def row_copy(target):
        return pltpu.make_async_remote_copy(
            src_ref=send_rows.at[target], dst_ref=recv_rows.at[me],
            send_sem=row_send.at[target], recv_sem=row_recv.at[me],
            device_id=spot(target), device_id_type=MESH,
        )

    for at_z in (places[3], places[2], places[1]):
        base = at_z * group
        hot = pick_hot[pl.ds(pl.multiple_of(base * capacity, group * capacity), group * capacity), :]
        picked = jnp.dot(hot, density_rows, preferred_element_type=jnp.float32).astype(jnp.bfloat16)
        send_rows[pl.ds(base, group)] = picked.reshape(group, capacity, width)
        for k in range(group):
            row_copy(base + k).start()
    base = z * group
    hot = pick_hot[pl.ds(pl.multiple_of(base * capacity, group * capacity), group * capacity), :]
    picked = jnp.dot(hot, density_rows, preferred_element_type=jnp.float32).astype(jnp.bfloat16)
    send_rows[pl.ds(base, group)] = picked.reshape(group, capacity, width)
    for k in range(1, group):
        row_copy(base + (me - base + k) % group).start()
    recv_rows[me] = send_rows[me]
    for s in range(BR_DEV):
        column = -(acc[s, mine, :] + half_in[s])
        inv_ref[s, 0] = column[:, :width]
        inv_ref[s, 1] = column[:, width:]
    loads[4].wait()
    for k in range(1, peers):
        origin = (me + k) % peers
        dst = recv_rows.at[origin]
        pltpu.make_async_remote_copy(
            src_ref=dst, dst_ref=dst, send_sem=row_send.at[origin], recv_sem=row_recv.at[origin],
            device_id=spot(origin), device_id_type=MESH,
        ).wait_recv()
    got = recv_rows[...].reshape(peers * capacity, width)
    for n in range(boxes):
        projected = lax.dot_general(
            got, basis_hot[n], (((0,), (0,)), ((), ())), preferred_element_type=jnp.float32)
        density_ref[n:n + 1, :] = jnp.sum(
            super_buf[n].astype(jnp.float32) * projected, axis=0, keepdims=True)

    @pl.when(corner)
    def _():
        def sent(p):
            for name in corner_sends:
                if name != "last_y":
                    at_corner(name, p).wait_send()
        each(0, pieces, sent)
        each(split_at, pieces, lambda p: at_corner("last_y", p).wait_send())

    @pl.when(middle)
    def _():
        def sent(p):
            for name in middle_sends:
                if name != "extra":
                    at_middle(name, p).wait_send()
        each(0, pieces, sent)
        each(0, split_at, lambda p: at_middle("extra", p).wait_send())

    swap.wait_send()
    for k in range(1, peers):
        orb_copy(k).wait_send()
        row_copy((me + k) % peers).wait_send()


def fused(rows, cols, panel, tiles, tile_slot, tile_col, pole_weight, box_orbitals, box_basis, supernode_basis):
    blocks, parts, shard_rows, width = panel.shape[1:]
    tile_count, _, block, _ = tiles.shape
    boxes, orbs = box_orbitals.shape
    points = box_basis.shape[2]
    half = block // cols
    peers = rows * cols
    capacity = 2 * boxes * orbs // peers
    dma = pltpu.SemaphoreType.DMA
    bf16, f32 = jnp.bfloat16, jnp.float32
    smem = pl.BlockSpec(memory_space=pltpu.SMEM)
    hbm = pl.BlockSpec(memory_space=pl.ANY)
    vmem = pl.BlockSpec(memory_space=pltpu.VMEM)
    return pl.pallas_call(
        functools.partial(kernel, rows, cols),
        name="pole_step",
        out_shape=(
            jax.ShapeDtypeStruct((BR_DEV, 2, half, width), f32),
            jax.ShapeDtypeStruct((boxes, points), f32),
        ),
        in_specs=[smem] * 3 + [hbm] * 5,
        out_specs=(vmem, vmem),
        scratch_shapes=[pltpu.VMEM((2, blocks, parts, shard_rows, width), bf16)] * 4 + [
            pltpu.VMEM(tiles.shape, bf16),
            pltpu.VMEM(box_basis.shape, bf16),
            pltpu.VMEM(supernode_basis.shape, bf16),
            pltpu.VMEM((peers, boxes, orbs), jnp.int32),
            pltpu.VMEM((BR_DEV, block, 2 * width), f32),
            pltpu.VMEM((BR_DEV, half, 2 * width), f32),
            pltpu.VMEM((peers * capacity, BR_DEV * half), bf16),
            pltpu.VMEM((boxes, peers * capacity, points), bf16),
            pltpu.VMEM((boxes, peers, orbs), f32),
            pltpu.VMEM((boxes, peers, orbs), f32),
            pltpu.VMEM((peers, capacity, width), bf16),
            pltpu.VMEM((peers, capacity, width), bf16),
            dma((5,)),
            dma((3, 4, blocks)),
            dma((4, 2, blocks)),
            pltpu.SemaphoreType.REGULAR((2,)),
            dma((2,)),
            dma((peers,)),
            dma((peers,)),
            dma((peers,)),
            dma((peers,)),
        ],
        compiler_params=pltpu.CompilerParams(
            collective_id=0, has_side_effects=True, vmem_limit_bytes=56 * 1024 * 1024),
    )(tile_slot, tile_col, pole_weight, panel, tiles, box_orbitals, box_basis, supernode_basis)


def plain(panel, tiles, tile_slot, tile_col, pole_weight, box_orbitals, box_basis, supernode_basis):
    gathered = lax.all_gather(panel, "row", axis=3, tiled=True)
    blocks = gathered[0]
    selector = (tile_col[:, None] == jnp.arange(blocks.shape[0], dtype=jnp.int32)[None, :]).astype(
        jnp.bfloat16
    )
    chosen = jnp.einsum(
        "tj,jcbs->tcbs", selector, blocks, preferred_element_type=jnp.float32
    ).astype(jnp.bfloat16)
    real_part = jnp.einsum(
        "tab,tbs->tas", tiles[:, 0], chosen[:, 0], preferred_element_type=jnp.float32
    )
    real_part = real_part - jnp.einsum(
        "tab,tbs->tas", tiles[:, 1], chosen[:, 1], preferred_element_type=jnp.float32
    )
    imag_part = jnp.einsum(
        "tab,tbs->tas", tiles[:, 0], chosen[:, 1], preferred_element_type=jnp.float32
    )
    imag_part = imag_part + jnp.einsum(
        "tab,tbs->tas", tiles[:, 1], chosen[:, 0], preferred_element_type=jnp.float32
    )
    products = jnp.stack([real_part, imag_part], axis=1)
    partial_value = jnp.stack(
        [
            jnp.sum(jnp.where((tile_slot == slot_row)[:, None, None, None], products, 0.0), axis=0)
            for slot_row in range(BR_DEV)
        ]
    )
    summed = lax.psum_scatter(partial_value, "col", scatter_dimension=2, tiled=True)
    inverse_column = -summed
    density_local = (
        pole_weight[0] * inverse_column[:, 1] + pole_weight[1] * inverse_column[:, 0]
    ).astype(jnp.bfloat16)
    columns = density_local.shape[2]
    density_local = density_local.reshape(-1, columns)
    block_width = tiles.shape[2]
    col_count = lax.axis_size("col")
    half_rows = block_width // col_count
    wanted = box_orbitals.reshape(-1)
    wanted_total = wanted.shape[0]
    block_index = wanted // block_width
    within = wanted % block_width
    source = block_index // BR_DEV * col_count + within // half_rows
    local_row = block_index % BR_DEV * half_rows + within % half_rows
    start_rows = jnp.zeros((wanted_total, columns), jnp.bfloat16)
    shards = lax.all_gather(density_local[None], ("row", "col"), axis=0, tiled=True)
    count = shards.shape[0]
    inside = (source >= 0) & (source < count)
    clipped = jnp.clip(source, 0, count - 1)
    fetched = shards[clipped, local_row]
    picked = jnp.where(inside[:, None], fetched, start_rows)
    picked = picked.reshape(box_basis.shape[0], box_basis.shape[1], columns)
    projected = jnp.einsum("nas,nap->nsp", picked, box_basis, preferred_element_type=jnp.float32)
    density = jnp.sum(supernode_basis.astype(jnp.float32) * projected, axis=1)
    return (inverse_column, density)


def solution(mesh):
    rows, cols = mesh.shape["row"], mesh.shape["col"]

    def local(panel, *rest):
        if cols == 2 and rows == 8 and panel.shape[1] % 8 == 0 and 2 * panel.shape[3] % panel.shape[4] == 0:
            return fused(rows, cols, panel, *rest)
        return plain(panel, *rest)

    return jax.shard_map(
        local,
        mesh=mesh,
        in_specs=(
            P(("pole", "col"), None, None, "row", None),
            P(("pole", "row", "col"), None, None, None),
            P(("pole", "row", "col")),
            P(("pole", "row", "col")),
            P("pole"),
            P(("pole", "row", "col"), None),
            P(("pole", "row", "col"), None, None),
            P(("pole", "row", "col"), None, None),
        ),
        out_specs=(P(("pole", "row"), None, "col", None), P(("pole", "row", "col"), None)),
        check_vma=False,
    )
```

```python
import functools

import jax
import jax.numpy as jnp
from jax import lax
from jax.experimental import pallas as pl
from jax.experimental.pallas import tpu as pltpu
from jax.sharding import PartitionSpec as P

BR_DEV = 2
MESH = pl.DeviceIdType.MESH


def log2(value):
    assert value & (value - 1) == 0
    return value.bit_length() - 1


def kernel(
    rows, cols, slot_ref, tcol_ref, weight_ref, panel, tiles, orbitals, basis, super_basis,
    inv_ref, density_ref, own, near, third, last,
    tile_buf, basis_buf, super_buf, orb_buf, acc, half_in, pick_hot, basis_hot, order_buf, local_buf,
    send_rows, recv_rows, local_sem, send_sem, recv_sem, token, col_sem, orb_send, orb_recv, row_send, row_recv,
):
    lanes_y = 2
    depth_z = rows // lanes_y
    peers = rows * cols
    r = lax.axis_index("row")
    c = lax.axis_index("col")
    me = r * cols + c
    z = r // lanes_y
    y = r % lanes_y
    shard_rows = panel.shape[3]
    width = panel.shape[4]
    pieces = recv_sem.shape[2]
    step = panel.shape[1] // pieces
    split_at = pieces // 2
    tile_count = tiles.shape[0]
    block = tiles.shape[2]
    half = block // cols
    pair = lanes_y * shard_rows
    boxes, orbs = orbitals.shape
    capacity = send_rows.shape[1]

    inner = 1 - 2 * (z // (depth_z // 2))
    corner = jnp.logical_or(z == 0, z == depth_z - 1)
    middle = jnp.logical_not(corner)
    other = r + 1 - 2 * y
    inward = r + lanes_y * inner
    outward = r - lanes_y * inner
    buffers = (own, near, third, last)
    places = (
        z,
        z + inner,
        jnp.where(corner, z + 2 * inner, z - inner),
        jnp.where(corner, z + 3 * inner, z + 2 * inner),
    )
    IN, OUT, Y = 0, 1, 2

    def spot(index):
        return {"row": index // cols, "col": index % cols}

    loads = [
        pltpu.make_async_copy(panel.at[0], own.at[y], local_sem.at[0]),
        pltpu.make_async_copy(orbitals, orb_buf.at[me], local_sem.at[4]),
        pltpu.make_async_copy(basis, basis_buf, local_sem.at[2]),
        pltpu.make_async_copy(tiles, tile_buf, local_sem.at[1]),
        pltpu.make_async_copy(super_basis, super_buf, local_sem.at[3]),
    ]
    for load in loads[:3]:
        load.start()

    barrier = pltpu.get_barrier_semaphore()
    for device in (
        {"row": other}, {"col": 1 - c}, {"row": other, "col": 1 - c}, {"row": inward},
    ):
        pl.semaphore_signal(barrier, inc=1, device_id=device, device_id_type=MESH)

    @pl.when(middle)
    def _():
        pl.semaphore_signal(barrier, inc=1, device_id={"row": outward}, device_id_type=MESH)
        pl.semaphore_wait(barrier, 5)

    @pl.when(corner)
    def _():
        pl.semaphore_wait(barrier, 4)

    loads[0].wait()

    def piece(which, lane, p):
        return buffers[which].at[lane, pl.ds(p * step, step)]

    def copy(link, kind, source, target, lane, p):
        row = (inward, outward, other)[link]
        return pltpu.make_async_remote_copy(
            src_ref=piece(source, lane, p), dst_ref=piece(target, lane, p),
            send_sem=send_sem.at[link, kind, p], recv_sem=recv_sem.at[target, lane, p],
            device_id={"row": row}, device_id_type=MESH,
        )

    def arrived(target, lane, p):
        dst = piece(target, lane, p)
        pltpu.make_async_remote_copy(
            src_ref=dst, dst_ref=dst, send_sem=send_sem.at[0, 0, p], recv_sem=recv_sem.at[target, lane, p],
            device_id={"row": other}, device_id_type=MESH,
        ).wait_recv()

    def each(low, high, body):
        def run(h, carry):
            body(h)
            return carry
        lax.fori_loop(low, high, run, 0)

    corner_sends = {
        "own_in": (IN, 0, 0, 2, y), "own_y": (Y, 0, 0, 0, y),
        "extra": (IN, 1, 0, 2, 1 - y),
        "near_y": (Y, 1, 1, 1, y), "third_y": (Y, 2, 2, 2, y), "last_y": (Y, 3, 3, 3, y),
    }
    middle_sends = {
        "own_out": (OUT, 0, 0, 1, y), "own_in": (IN, 0, 0, 1, y), "own_y": (Y, 0, 0, 0, y),
        "third_in": (IN, 1, 2, 3, y),
        "near_out": (OUT, 1, 1, 2, y), "near_y": (Y, 1, 1, 1, y),
        "last_out": (OUT, 2, 3, 3, y), "last_y": (Y, 2, 3, 3, y),
        "extra": (OUT, 3, 3, 3, 1 - y),
    }

    def at_corner(name, p):
        return copy(*corner_sends[name], p)

    def at_middle(name, p):
        return copy(*middle_sends[name], p)

    @pl.when(corner)
    def _():
        def go(p):
            at_corner("own_in", p).start()
            at_corner("own_y", p).start()
        each(0, pieces, go)

    @pl.when(middle)
    def _():
        def go(p):
            at_middle("own_out", p).start()
            at_middle("own_in", p).start()
            at_middle("own_y", p).start()
        each(0, pieces, go)

    for load in loads[3:]:
        load.start()
    acc[...] = jnp.zeros_like(acc)
    block_bits, half_bits = log2(block), log2(half)

    def split(g):
        row_block = g >> block_bits
        within = g & (block - 1)
        source = (row_block >> log2(BR_DEV)) * cols + (within >> half_bits)
        local = (row_block & (BR_DEV - 1)) * half + (within & (half - 1))
        return source, local

    def ranks(masks):
        before = lax.broadcasted_iota(jnp.int32, (orbs, orbs), 0)
        after = lax.broadcasted_iota(jnp.int32, (orbs, orbs), 1)
        upper = jnp.where(before <= after, 1.0, 0.0).astype(jnp.bfloat16)
        seen = jnp.zeros((masks[0].shape[0], 1), jnp.float32)
        result = []
        for mask in masks:
            counted = jnp.dot(mask.astype(jnp.bfloat16), upper, preferred_element_type=jnp.float32)
            result.append(counted - 1.0 + seen)
            seen = seen + jnp.sum(mask, axis=1, keepdims=True)
        return result

    def place_basis():
        loads[1].wait()
        loads[2].wait()
        masks = []
        peer_id = lax.broadcasted_iota(jnp.int32, (peers, orbs), 0)
        for n in range(boxes):
            source, _ = split(orb_buf[me, n:n + 1, :])
            masks.append(jnp.where(peer_id == source, 1.0, 0.0))
        order = ranks(masks)
        arrive = lax.broadcasted_iota(jnp.int32, (peers * capacity, orbs), 0).astype(jnp.float32)
        for n in range(boxes):
            position = jnp.sum(
                masks[n] * (order[n] + (peer_id * capacity).astype(jnp.float32)), axis=0, keepdims=True)
            hot = jnp.where(arrive == position, 1.0, 0.0).astype(jnp.bfloat16)
            basis_hot[n] = jnp.dot(hot, basis_buf[n], preferred_element_type=jnp.float32).astype(jnp.bfloat16)

    def orb_copy(k):
        return pltpu.make_async_remote_copy(
            src_ref=orbitals, dst_ref=orb_buf.at[me], send_sem=orb_send.at[k], recv_sem=orb_recv.at[k],
            device_id=spot((me + k) % peers), device_id_type=MESH,
        )

    def rank_orbitals():
        for k in range(1, peers):
            origin = (me + peers - k) % peers
            dst = orb_buf.at[origin]
            pltpu.make_async_remote_copy(
                src_ref=dst, dst_ref=dst, send_sem=orb_send.at[k], recv_sem=orb_recv.at[k],
                device_id=spot(origin), device_id_type=MESH,
            ).wait_recv()
        asked = []
        for n in range(boxes):
            g = jnp.concatenate([orb_buf[q, n:n + 1, :] for q in range(peers)], axis=0)
            source, local = split(g)
            asked.append((jnp.where(source == me, 1.0, 0.0), local.astype(jnp.float32)))
        order = ranks([a[0] for a in asked])
        for n in range(boxes):
            order_buf[n] = jnp.where(asked[n][0] > 0.5, order[n], -1.0)
            local_buf[n] = asked[n][1] + 1.0

    def place_picks(q):
        place = lax.broadcasted_iota(jnp.int32, (capacity, orbs), 0).astype(jnp.float32)
        row_id = lax.broadcasted_iota(jnp.int32, (capacity, BR_DEV * half), 1).astype(jnp.float32)
        found = jnp.zeros((capacity, 1), jnp.float32)
        for n in range(boxes):
            hit = place == order_buf[n, pl.ds(q, 1), :]
            found = found + jnp.sum(jnp.where(hit, local_buf[n, pl.ds(q, 1), :], 0.0), axis=1, keepdims=True)
        spot_rows = pl.ds(pl.multiple_of(q * capacity, capacity), capacity)
        pick_hot[spot_rows, :] = jnp.where(row_id == found - 1.0, 1.0, 0.0).astype(jnp.bfloat16)

    def product(which, t, out_rows):
        j = tcol_ref[t]
        offset = pl.multiple_of(places[which] * pair, pair)
        left = jnp.concatenate(
            [tile_buf[t, 0, out_rows, pl.ds(offset, pair)], tile_buf[t, 1, out_rows, pl.ds(offset, pair)]], axis=1)
        parts = [buffers[which][k, j] for k in range(lanes_y)]
        real = jnp.concatenate([p[0] for p in parts], axis=0)
        imag = jnp.concatenate([p[1] for p in parts], axis=0)
        right = jnp.concatenate(
            [jnp.concatenate([real, imag], axis=1), jnp.concatenate([-imag, real], axis=1)], axis=0)
        return jnp.dot(left, right, preferred_element_type=jnp.float32)

    def several(which, start, count, out_rows):
        values = [product(which, start + k, out_rows) for k in range(count)]
        for s in range(BR_DEV):
            total = jnp.where(slot_ref[start] == s, values[0], 0.0)
            for k in range(1, count):
                total = total + jnp.where(slot_ref[start + k] == s, values[k], 0.0)
            acc[s, out_rows, :] += total

    everything = pl.ds(0, block)

    def share(which, p, parts):
        each(p * tile_count // parts, (p + 1) * tile_count // parts, lambda t: several(which, t, 1, everything))

    place_basis()

    def first(p):
        @pl.when(corner)
        def _():
            arrived(1, y, p)
            at_corner("near_y", p).start()
            arrived(0, 1 - y, p)
            at_corner("extra", p).start()

        @pl.when(middle)
        def _():
            arrived(2, y, p)
            at_middle("third_in", p).start()
            arrived(1, y, p)
            at_middle("near_out", p).start()
            at_middle("near_y", p).start()

            @pl.when(p == 0)
            def _():
                pl.semaphore_signal(token.at[0], inc=1, device_id={"row": inward}, device_id_type=MESH)

            @pl.when(p == pieces - 1)
            def _():
                pl.semaphore_wait(token.at[0], 1)
                pl.semaphore_signal(token.at[1], inc=1, device_id={"row": outward}, device_id_type=MESH)

    each(0, pieces, first)

    @pl.when(corner)
    def _():
        pl.semaphore_wait(token.at[1], 1)

    for k in range(1, peers):
        orb_copy(k).start()

    @pl.when(middle)
    def _():
        each(0, pieces, lambda p: arrived(0, 1 - y, p))

    loads[3].wait()

    def second(p):
        @pl.when(corner)
        def _():
            arrived(2, y, p)
            at_corner("third_y", p).start()

        @pl.when(middle)
        def _():
            arrived(3, y, p)
            at_middle("last_out", p).start()

            @pl.when(p >= split_at)
            def _():
                at_middle("last_y", p).start()

        share(0, p, pieces)

    each(0, pieces, second)

    @pl.when(middle)
    def _():
        each(0, split_at, lambda p: at_middle("last_y", p).start())

    each(0, pieces, lambda p: arrived(1, 1 - y, p))

    def closing(p):
        share(1, p, split_at)

        @pl.when(corner)
        def _():
            arrived(3, y, p)
            at_corner("last_y", p).start()

        @pl.when(middle)
        def _():
            arrived(3, 1 - y, p + split_at)
            at_middle("extra", p + split_at).start()

    each(0, split_at, closing)
    rank_orbitals()
    each(0, peers, place_picks)
    each(0, pieces, lambda p: arrived(2, 1 - y, p))
    for start in range(0, tile_count, 4):
        several(2, start, min(4, tile_count - start), everything)

    @pl.when(corner)
    def _():
        each(split_at, pieces, lambda p: arrived(3, y, p))
        each(split_at, pieces, lambda p: arrived(3, 1 - y, p))
    each(0, split_at, lambda p: arrived(3, 1 - y, p))

    mine = pl.ds(pl.multiple_of(c * half, half), half)
    theirs = pl.ds(pl.multiple_of((1 - c) * half, half), half)
    for start in range(0, tile_count, 4):
        several(3, start, min(4, tile_count - start), theirs)
    swap = pltpu.make_async_remote_copy(
        src_ref=acc.at[:, theirs, :], dst_ref=half_in, send_sem=col_sem.at[0], recv_sem=col_sem.at[1],
        device_id={"col": 1 - c}, device_id_type=MESH,
    )
    swap.start()
    for start in range(0, tile_count, 4):
        several(3, start, min(4, tile_count - start), mine)
    swap.wait_recv()
    density_rows = []
    for s in range(BR_DEV):
        column = -(acc[s, mine, :] + half_in[s])
        real, imag = column[:, :width], column[:, width:]
        density_rows.append((weight_ref[0] * imag + weight_ref[1] * real).astype(jnp.bfloat16))
    density_rows = jnp.concatenate(density_rows, axis=0)

    group = lanes_y * cols

    def row_copy(target):
        return pltpu.make_async_remote_copy(
            src_ref=send_rows.at[target], dst_ref=recv_rows.at[me],
            send_sem=row_send.at[target], recv_sem=row_recv.at[me],
            device_id=spot(target), device_id_type=MESH,
        )

    for at_z in (places[3], places[2], places[1]):
        base = at_z * group
        hot = pick_hot[pl.ds(pl.multiple_of(base * capacity, group * capacity), group * capacity), :]
        picked = jnp.dot(hot, density_rows, preferred_element_type=jnp.float32).astype(jnp.bfloat16)
        send_rows[pl.ds(base, group)] = picked.reshape(group, capacity, width)
        for k in range(group):
            row_copy(base + k).start()
    base = z * group
    hot = pick_hot[pl.ds(pl.multiple_of(base * capacity, group * capacity), group * capacity), :]
    picked = jnp.dot(hot, density_rows, preferred_element_type=jnp.float32).astype(jnp.bfloat16)
    send_rows[pl.ds(base, group)] = picked.reshape(group, capacity, width)
    for k in range(1, group):
        row_copy(base + (me - base + k) % group).start()
    recv_rows[me] = send_rows[me]
    for s in range(BR_DEV):
        column = -(acc[s, mine, :] + half_in[s])
        inv_ref[s, 0] = column[:, :width]
        inv_ref[s, 1] = column[:, width:]
    loads[4].wait()
    for k in range(1, peers):
        origin = (me + k) % peers
        dst = recv_rows.at[origin]
        pltpu.make_async_remote_copy(
            src_ref=dst, dst_ref=dst, send_sem=row_send.at[origin], recv_sem=row_recv.at[origin],
            device_id=spot(origin), device_id_type=MESH,
        ).wait_recv()
    got = recv_rows[...].reshape(peers * capacity, width)
    for n in range(boxes):
        projected = lax.dot_general(
            got, basis_hot[n], (((0,), (0,)), ((), ())), preferred_element_type=jnp.float32)
        density_ref[n:n + 1, :] = jnp.sum(
            super_buf[n].astype(jnp.float32) * projected, axis=0, keepdims=True)

    @pl.when(corner)
    def _():
        def sent(p):
            for name in corner_sends:
                if name != "last_y":
                    at_corner(name, p).wait_send()
        each(0, pieces, sent)
        each(0, split_at, lambda p: at_corner("last_y", p).wait_send())

    @pl.when(middle)
    def _():
        def sent(p):
            for name in middle_sends:
                if name != "extra":
                    at_middle(name, p).wait_send()
        each(0, pieces, sent)
        each(split_at, pieces, lambda p: at_middle("extra", p).wait_send())

    swap.wait_send()
    for k in range(1, peers):
        orb_copy(k).wait_send()
        row_copy((me + k) % peers).wait_send()


def fused(rows, cols, panel, tiles, tile_slot, tile_col, pole_weight, box_orbitals, box_basis, supernode_basis):
    blocks, parts, shard_rows, width = panel.shape[1:]
    tile_count, _, block, _ = tiles.shape
    boxes, orbs = box_orbitals.shape
    points = box_basis.shape[2]
    half = block // cols
    peers = rows * cols
    capacity = 2 * boxes * orbs // peers
    pieces = blocks // 2
    dma = pltpu.SemaphoreType.DMA
    bf16, f32 = jnp.bfloat16, jnp.float32
    smem = pl.BlockSpec(memory_space=pltpu.SMEM)
    hbm = pl.BlockSpec(memory_space=pl.ANY)
    vmem = pl.BlockSpec(memory_space=pltpu.VMEM)
    return pl.pallas_call(
        functools.partial(kernel, rows, cols),
        name="pole_step",
        out_shape=(
            jax.ShapeDtypeStruct((BR_DEV, 2, half, width), f32),
            jax.ShapeDtypeStruct((boxes, points), f32),
        ),
        in_specs=[smem] * 3 + [hbm] * 5,
        out_specs=(vmem, vmem),
        scratch_shapes=[pltpu.VMEM((2, blocks, parts, shard_rows, width), bf16)] * 4 + [
            pltpu.VMEM(tiles.shape, bf16),
            pltpu.VMEM(box_basis.shape, bf16),
            pltpu.VMEM(supernode_basis.shape, bf16),
            pltpu.VMEM((peers, boxes, orbs), jnp.int32),
            pltpu.VMEM((BR_DEV, block, 2 * width), f32),
            pltpu.VMEM((BR_DEV, half, 2 * width), f32),
            pltpu.VMEM((peers * capacity, BR_DEV * half), bf16),
            pltpu.VMEM((boxes, peers * capacity, points), bf16),
            pltpu.VMEM((boxes, peers, orbs), f32),
            pltpu.VMEM((boxes, peers, orbs), f32),
            pltpu.VMEM((peers, capacity, width), bf16),
            pltpu.VMEM((peers, capacity, width), bf16),
            dma((5,)),
            dma((3, 4, pieces)),
            dma((4, 2, pieces)),
            pltpu.SemaphoreType.REGULAR((2,)),
            dma((2,)),
            dma((peers,)),
            dma((peers,)),
            dma((peers,)),
            dma((peers,)),
        ],
        compiler_params=pltpu.CompilerParams(
            collective_id=0, has_side_effects=True, vmem_limit_bytes=56 * 1024 * 1024),
    )(tile_slot, tile_col, pole_weight, panel, tiles, box_orbitals, box_basis, supernode_basis)


def plain(panel, tiles, tile_slot, tile_col, pole_weight, box_orbitals, box_basis, supernode_basis):
    gathered = lax.all_gather(panel, "row", axis=3, tiled=True)
    blocks = gathered[0]
    selector = (tile_col[:, None] == jnp.arange(blocks.shape[0], dtype=jnp.int32)[None, :]).astype(
        jnp.bfloat16
    )
    chosen = jnp.einsum(
        "tj,jcbs->tcbs", selector, blocks, preferred_element_type=jnp.float32
    ).astype(jnp.bfloat16)
    real_part = jnp.einsum(
        "tab,tbs->tas", tiles[:, 0], chosen[:, 0], preferred_element_type=jnp.float32
    )
    real_part = real_part - jnp.einsum(
        "tab,tbs->tas", tiles[:, 1], chosen[:, 1], preferred_element_type=jnp.float32
    )
    imag_part = jnp.einsum(
        "tab,tbs->tas", tiles[:, 0], chosen[:, 1], preferred_element_type=jnp.float32
    )
    imag_part = imag_part + jnp.einsum(
        "tab,tbs->tas", tiles[:, 1], chosen[:, 0], preferred_element_type=jnp.float32
    )
    products = jnp.stack([real_part, imag_part], axis=1)
    partial_value = jnp.stack(
        [
            jnp.sum(jnp.where((tile_slot == slot_row)[:, None, None, None], products, 0.0), axis=0)
            for slot_row in range(BR_DEV)
        ]
    )
    summed = lax.psum_scatter(partial_value, "col", scatter_dimension=2, tiled=True)
    inverse_column = -summed
    density_local = (
        pole_weight[0] * inverse_column[:, 1] + pole_weight[1] * inverse_column[:, 0]
    ).astype(jnp.bfloat16)
    columns = density_local.shape[2]
    density_local = density_local.reshape(-1, columns)
    block_width = tiles.shape[2]
    col_count = lax.axis_size("col")
    half_rows = block_width // col_count
    wanted = box_orbitals.reshape(-1)
    wanted_total = wanted.shape[0]
    block_index = wanted // block_width
    within = wanted % block_width
    source = block_index // BR_DEV * col_count + within // half_rows
    local_row = block_index % BR_DEV * half_rows + within % half_rows
    start_rows = jnp.zeros((wanted_total, columns), jnp.bfloat16)
    shards = lax.all_gather(density_local[None], ("row", "col"), axis=0, tiled=True)
    count = shards.shape[0]
    inside = (source >= 0) & (source < count)
    clipped = jnp.clip(source, 0, count - 1)
    fetched = shards[clipped, local_row]
    picked = jnp.where(inside[:, None], fetched, start_rows)
    picked = picked.reshape(box_basis.shape[0], box_basis.shape[1], columns)
    projected = jnp.einsum("nas,nap->nsp", picked, box_basis, preferred_element_type=jnp.float32)
    density = jnp.sum(supernode_basis.astype(jnp.float32) * projected, axis=1)
    return (inverse_column, density)


def solution(mesh):
    rows, cols = mesh.shape["row"], mesh.shape["col"]

    def local(panel, *rest):
        if cols == 2 and rows == 8 and panel.shape[1] % 8 == 0 and 2 * panel.shape[3] % panel.shape[4] == 0:
            return fused(rows, cols, panel, *rest)
        return plain(panel, *rest)

    return jax.shard_map(
        local,
        mesh=mesh,
        in_specs=(
            P(("pole", "col"), None, None, "row", None),
            P(("pole", "row", "col"), None, None, None),
            P(("pole", "row", "col")),
            P(("pole", "row", "col")),
            P("pole"),
            P(("pole", "row", "col"), None),
            P(("pole", "row", "col"), None, None),
            P(("pole", "row", "col"), None, None),
        ),
        out_specs=(P(("pole", "row"), None, "col", None), P(("pole", "row", "col"), None)),
        check_vma=False,
    )
```

```python
import functools

import jax
import jax.numpy as jnp
from jax import lax
from jax.experimental import pallas as pl
from jax.experimental.pallas import tpu as pltpu
from jax.sharding import PartitionSpec as P

BR_DEV = 2
MESH = pl.DeviceIdType.MESH


def log2(value):
    assert value & (value - 1) == 0
    return value.bit_length() - 1


def kernel(
    rows, cols, slot_ref, tcol_ref, weight_ref, panel, tiles, orbitals, basis, super_basis,
    inv_ref, density_ref, own, near, third, last,
    tile_buf, basis_buf, super_buf, orb_buf, acc, half_in, pick_hot, basis_hot, order_buf, local_buf,
    send_rows, recv_rows, local_sem, send_sem, recv_sem, token, col_sem, orb_send, orb_recv, row_send, row_recv,
):
    lanes_y = 2
    depth_z = rows // lanes_y
    peers = rows * cols
    r = lax.axis_index("row")
    c = lax.axis_index("col")
    me = r * cols + c
    z = r // lanes_y
    y = r % lanes_y
    shard_rows = panel.shape[3]
    width = panel.shape[4]
    pieces = recv_sem.shape[2]
    step = panel.shape[1] // pieces
    split_at = pieces // 2
    tile_count = tiles.shape[0]
    block = tiles.shape[2]
    half = block // cols
    pair = lanes_y * shard_rows
    boxes, orbs = orbitals.shape
    capacity = send_rows.shape[1]

    inner = 1 - 2 * (z // (depth_z // 2))
    corner = jnp.logical_or(z == 0, z == depth_z - 1)
    middle = jnp.logical_not(corner)
    other = r + 1 - 2 * y
    inward = r + lanes_y * inner
    outward = r - lanes_y * inner
    buffers = (own, near, third, last)
    places = (
        z,
        z + inner,
        jnp.where(corner, z + 2 * inner, z - inner),
        jnp.where(corner, z + 3 * inner, z + 2 * inner),
    )
    IN, OUT, Y = 0, 1, 2

    def spot(index):
        return {"row": index // cols, "col": index % cols}

    loads = [
        pltpu.make_async_copy(panel.at[0], own.at[y], local_sem.at[0]),
        pltpu.make_async_copy(orbitals, orb_buf.at[me], local_sem.at[4]),
        pltpu.make_async_copy(basis, basis_buf, local_sem.at[2]),
        pltpu.make_async_copy(tiles, tile_buf, local_sem.at[1]),
        pltpu.make_async_copy(super_basis, super_buf, local_sem.at[3]),
    ]
    for load in loads[:3]:
        load.start()

    barrier = pltpu.get_barrier_semaphore()
    for device in (
        {"row": other}, {"col": 1 - c}, {"row": other, "col": 1 - c}, {"row": inward},
    ):
        pl.semaphore_signal(barrier, inc=1, device_id=device, device_id_type=MESH)

    @pl.when(middle)
    def _():
        pl.semaphore_signal(barrier, inc=1, device_id={"row": outward}, device_id_type=MESH)
        pl.semaphore_wait(barrier, 5)

    @pl.when(corner)
    def _():
        pl.semaphore_wait(barrier, 4)

    loads[0].wait()

    def piece(which, lane, p):
        return buffers[which].at[lane, pl.ds(p * step, step)]

    def copy(link, kind, source, target, lane, p):
        row = (inward, outward, other)[link]
        return pltpu.make_async_remote_copy(
            src_ref=piece(source, lane, p), dst_ref=piece(target, lane, p),
            send_sem=send_sem.at[link, kind, p], recv_sem=recv_sem.at[target, lane, p],
            device_id={"row": row}, device_id_type=MESH,
        )

    def arrived(target, lane, p):
        dst = piece(target, lane, p)
        pltpu.make_async_remote_copy(
            src_ref=dst, dst_ref=dst, send_sem=send_sem.at[0, 0, p], recv_sem=recv_sem.at[target, lane, p],
            device_id={"row": other}, device_id_type=MESH,
        ).wait_recv()

    def each(low, high, body):
        def run(h, carry):
            body(h)
            return carry
        lax.fori_loop(low, high, run, 0)

    corner_sends = {
        "own_in": (IN, 0, 0, 2, y), "own_y": (Y, 0, 0, 0, y),
        "extra": (IN, 1, 0, 2, 1 - y),
        "near_y": (Y, 1, 1, 1, y), "third_y": (Y, 2, 2, 2, y), "last_y": (Y, 3, 3, 3, y),
    }
    middle_sends = {
        "own_out": (OUT, 0, 0, 1, y), "own_in": (IN, 0, 0, 1, y), "own_y": (Y, 0, 0, 0, y),
        "third_in": (IN, 1, 2, 3, y),
        "near_out": (OUT, 1, 1, 2, y), "near_y": (Y, 1, 1, 1, y),
        "last_out": (OUT, 2, 3, 3, y), "last_y": (Y, 2, 3, 3, y),
        "extra": (OUT, 3, 3, 3, 1 - y),
    }

    def at_corner(name, p):
        return copy(*corner_sends[name], p)

    def at_middle(name, p):
        return copy(*middle_sends[name], p)

    @pl.when(corner)
    def _():
        def go(p):
            at_corner("own_in", p).start()
            at_corner("own_y", p).start()
        each(0, pieces, go)

    @pl.when(middle)
    def _():
        def go(p):
            at_middle("own_out", p).start()
            at_middle("own_in", p).start()
            at_middle("own_y", p).start()
        each(0, pieces, go)

    for load in loads[3:]:
        load.start()
    acc[...] = jnp.zeros_like(acc)
    block_bits, half_bits = log2(block), log2(half)

    def split(g):
        row_block = g >> block_bits
        within = g & (block - 1)
        source = (row_block >> log2(BR_DEV)) * cols + (within >> half_bits)
        local = (row_block & (BR_DEV - 1)) * half + (within & (half - 1))
        return source, local

    def ranks(masks):
        before = lax.broadcasted_iota(jnp.int32, (orbs, orbs), 0)
        after = lax.broadcasted_iota(jnp.int32, (orbs, orbs), 1)
        upper = jnp.where(before <= after, 1.0, 0.0).astype(jnp.bfloat16)
        seen = jnp.zeros((masks[0].shape[0], 1), jnp.float32)
        result = []
        for mask in masks:
            counted = jnp.dot(mask.astype(jnp.bfloat16), upper, preferred_element_type=jnp.float32)
            result.append(counted - 1.0 + seen)
            seen = seen + jnp.sum(mask, axis=1, keepdims=True)
        return result

    def place_basis():
        loads[1].wait()
        loads[2].wait()
        masks = []
        peer_id = lax.broadcasted_iota(jnp.int32, (peers, orbs), 0)
        for n in range(boxes):
            source, _ = split(orb_buf[me, n:n + 1, :])
            masks.append(jnp.where(peer_id == source, 1.0, 0.0))
        order = ranks(masks)
        arrive = lax.broadcasted_iota(jnp.int32, (peers * capacity, orbs), 0).astype(jnp.float32)
        for n in range(boxes):
            position = jnp.sum(
                masks[n] * (order[n] + (peer_id * capacity).astype(jnp.float32)), axis=0, keepdims=True)
            hot = jnp.where(arrive == position, 1.0, 0.0).astype(jnp.bfloat16)
            basis_hot[n] = jnp.dot(hot, basis_buf[n], preferred_element_type=jnp.float32).astype(jnp.bfloat16)

    def orb_copy(k):
        return pltpu.make_async_remote_copy(
            src_ref=orbitals, dst_ref=orb_buf.at[me], send_sem=orb_send.at[k], recv_sem=orb_recv.at[k],
            device_id=spot((me + k) % peers), device_id_type=MESH,
        )

    def rank_orbitals():
        for k in range(1, peers):
            origin = (me + peers - k) % peers
            dst = orb_buf.at[origin]
            pltpu.make_async_remote_copy(
                src_ref=dst, dst_ref=dst, send_sem=orb_send.at[k], recv_sem=orb_recv.at[k],
                device_id=spot(origin), device_id_type=MESH,
            ).wait_recv()
        asked = []
        for n in range(boxes):
            g = jnp.concatenate([orb_buf[q, n:n + 1, :] for q in range(peers)], axis=0)
            source, local = split(g)
            asked.append((jnp.where(source == me, 1.0, 0.0), local.astype(jnp.float32)))
        order = ranks([a[0] for a in asked])
        for n in range(boxes):
            order_buf[n] = jnp.where(asked[n][0] > 0.5, order[n], -1.0)
            local_buf[n] = asked[n][1] + 1.0

    def place_picks(q):
        place = lax.broadcasted_iota(jnp.int32, (capacity, orbs), 0).astype(jnp.float32)
        row_id = lax.broadcasted_iota(jnp.int32, (capacity, BR_DEV * half), 1).astype(jnp.float32)
        found = jnp.zeros((capacity, 1), jnp.float32)
        for n in range(boxes):
            hit = place == order_buf[n, pl.ds(q, 1), :]
            found = found + jnp.sum(jnp.where(hit, local_buf[n, pl.ds(q, 1), :], 0.0), axis=1, keepdims=True)
        spot_rows = pl.ds(pl.multiple_of(q * capacity, capacity), capacity)
        pick_hot[spot_rows, :] = jnp.where(row_id == found - 1.0, 1.0, 0.0).astype(jnp.bfloat16)

    def product(which, t, out_rows):
        j = tcol_ref[t]
        offset = pl.multiple_of(places[which] * pair, pair)
        left = jnp.concatenate(
            [tile_buf[t, 0, out_rows, pl.ds(offset, pair)], tile_buf[t, 1, out_rows, pl.ds(offset, pair)]], axis=1)
        parts = [buffers[which][k, j] for k in range(lanes_y)]
        real = jnp.concatenate([p[0] for p in parts], axis=0)
        imag = jnp.concatenate([p[1] for p in parts], axis=0)
        right = jnp.concatenate(
            [jnp.concatenate([real, imag], axis=1), jnp.concatenate([-imag, real], axis=1)], axis=0)
        return jnp.dot(left, right, preferred_element_type=jnp.float32)

    def several(which, start, count, out_rows):
        values = [product(which, start + k, out_rows) for k in range(count)]
        for s in range(BR_DEV):
            total = jnp.where(slot_ref[start] == s, values[0], 0.0)
            for k in range(1, count):
                total = total + jnp.where(slot_ref[start + k] == s, values[k], 0.0)
            acc[s, out_rows, :] += total

    everything = pl.ds(0, block)

    def share(which, p, parts):
        each(p * tile_count // parts, (p + 1) * tile_count // parts, lambda t: several(which, t, 1, everything))

    place_basis()

    def first(p):
        @pl.when(corner)
        def _():
            arrived(1, y, p)
            at_corner("near_y", p).start()
            arrived(0, 1 - y, p)
            at_corner("extra", p).start()

        @pl.when(middle)
        def _():
            arrived(2, y, p)
            at_middle("third_in", p).start()
            arrived(1, y, p)
            at_middle("near_out", p).start()
            at_middle("near_y", p).start()

            @pl.when(p == 0)
            def _():
                pl.semaphore_signal(token.at[0], inc=1, device_id={"row": inward}, device_id_type=MESH)

            @pl.when(p == pieces - 1)
            def _():
                pl.semaphore_wait(token.at[0], 1)
                pl.semaphore_signal(token.at[1], inc=1, device_id={"row": outward}, device_id_type=MESH)

    each(0, pieces, first)

    @pl.when(corner)
    def _():
        pl.semaphore_wait(token.at[1], 1)

    for k in range(1, peers):
        orb_copy(k).start()

    @pl.when(middle)
    def _():
        each(0, pieces, lambda p: arrived(0, 1 - y, p))

    loads[3].wait()

    def second(p):
        @pl.when(corner)
        def _():
            arrived(2, y, p)
            at_corner("third_y", p).start()

        @pl.when(middle)
        def _():
            arrived(3, y, p)
            at_middle("last_out", p).start()

            @pl.when(p >= split_at)
            def _():
                at_middle("last_y", p).start()

        share(0, p, pieces)

    each(0, pieces, second)

    @pl.when(middle)
    def _():
        each(0, split_at, lambda p: at_middle("last_y", p).start())

    each(0, pieces, lambda p: arrived(1, 1 - y, p))

    def closing(p):
        share(1, p, split_at)

        @pl.when(corner)
        def _():
            arrived(3, y, p)
            at_corner("last_y", p).start()

        @pl.when(middle)
        def _():
            arrived(3, 1 - y, p + split_at)
            at_middle("extra", p + split_at).start()

    each(0, split_at, closing)
    rank_orbitals()
    each(0, peers, place_picks)
    each(0, pieces, lambda p: arrived(2, 1 - y, p))
    for start in range(0, tile_count, 4):
        several(2, start, min(4, tile_count - start), everything)

    @pl.when(corner)
    def _():
        each(split_at, pieces, lambda p: arrived(3, y, p))
        each(split_at, pieces, lambda p: arrived(3, 1 - y, p))
    each(0, split_at, lambda p: arrived(3, 1 - y, p))

    mine = pl.ds(pl.multiple_of(c * half, half), half)
    theirs = pl.ds(pl.multiple_of((1 - c) * half, half), half)
    for start in range(0, tile_count, 4):
        several(3, start, min(4, tile_count - start), theirs)
    swap = pltpu.make_async_remote_copy(
        src_ref=acc.at[:, theirs, :], dst_ref=half_in, send_sem=col_sem.at[0], recv_sem=col_sem.at[1],
        device_id={"col": 1 - c}, device_id_type=MESH,
    )
    swap.start()
    for start in range(0, tile_count, 4):
        several(3, start, min(4, tile_count - start), mine)
    swap.wait_recv()
    density_rows = []
    for s in range(BR_DEV):
        column = -(acc[s, mine, :] + half_in[s])
        real, imag = column[:, :width], column[:, width:]
        density_rows.append((weight_ref[0] * imag + weight_ref[1] * real).astype(jnp.bfloat16))
    density_rows = jnp.concatenate(density_rows, axis=0)

    group = lanes_y * cols

    def row_copy(target):
        return pltpu.make_async_remote_copy(
            src_ref=send_rows.at[target], dst_ref=recv_rows.at[me],
            send_sem=row_send.at[target], recv_sem=row_recv.at[me],
            device_id=spot(target), device_id_type=MESH,
        )

    for at_z in (places[3], places[2], places[1]):
        base = at_z * group
        hot = pick_hot[pl.ds(pl.multiple_of(base * capacity, group * capacity), group * capacity), :]
        picked = jnp.dot(hot, density_rows, preferred_element_type=jnp.float32).astype(jnp.bfloat16)
        send_rows[pl.ds(base, group)] = picked.reshape(group, capacity, width)
        for k in range(group):
            row_copy(base + k).start()
    base = z * group
    hot = pick_hot[pl.ds(pl.multiple_of(base * capacity, group * capacity), group * capacity), :]
    picked = jnp.dot(hot, density_rows, preferred_element_type=jnp.float32).astype(jnp.bfloat16)
    send_rows[pl.ds(base, group)] = picked.reshape(group, capacity, width)
    for k in range(1, group):
        row_copy(base + (me - base + k) % group).start()
    recv_rows[me] = send_rows[me]
    for s in range(BR_DEV):
        column = -(acc[s, mine, :] + half_in[s])
        inv_ref[s, 0] = column[:, :width]
        inv_ref[s, 1] = column[:, width:]
    loads[4].wait()
    for k in range(1, peers):
        origin = (me + k) % peers
        dst = recv_rows.at[origin]
        pltpu.make_async_remote_copy(
            src_ref=dst, dst_ref=dst, send_sem=row_send.at[origin], recv_sem=row_recv.at[origin],
            device_id=spot(origin), device_id_type=MESH,
        ).wait_recv()
    got = recv_rows[...].reshape(peers * capacity, width)
    for n in range(boxes):
        projected = lax.dot_general(
            got, basis_hot[n], (((0,), (0,)), ((), ())), preferred_element_type=jnp.float32)
        density_ref[n:n + 1, :] = jnp.sum(
            super_buf[n].astype(jnp.float32) * projected, axis=0, keepdims=True)

    @pl.when(corner)
    def _():
        def sent(p):
            for name in corner_sends:
                if name != "last_y":
                    at_corner(name, p).wait_send()
        each(0, pieces, sent)
        each(0, split_at, lambda p: at_corner("last_y", p).wait_send())

    @pl.when(middle)
    def _():
        def sent(p):
            for name in middle_sends:
                if name != "extra":
                    at_middle(name, p).wait_send()
        each(0, pieces, sent)
        each(split_at, pieces, lambda p: at_middle("extra", p).wait_send())

    swap.wait_send()
    for k in range(1, peers):
        orb_copy(k).wait_send()
        row_copy((me + k) % peers).wait_send()


def deliver(column, density, column_out, density_out, sem):
    copies = [
        pltpu.make_async_copy(column, column_out, sem.at[0]),
        pltpu.make_async_copy(density, density_out, sem.at[1]),
    ]
    for copy in copies:
        copy.start()
    for copy in copies:
        copy.wait()


def fused(rows, cols, panel, tiles, tile_slot, tile_col, pole_weight, box_orbitals, box_basis, supernode_basis):
    blocks, parts, shard_rows, width = panel.shape[1:]
    tile_count, _, block, _ = tiles.shape
    boxes, orbs = box_orbitals.shape
    points = box_basis.shape[2]
    half = block // cols
    peers = rows * cols
    capacity = 2 * boxes * orbs // peers
    pieces = blocks // 2
    dma = pltpu.SemaphoreType.DMA
    bf16, f32 = jnp.bfloat16, jnp.float32
    smem = pl.BlockSpec(memory_space=pltpu.SMEM)
    hbm = pl.BlockSpec(memory_space=pl.ANY)
    vmem = pl.BlockSpec(memory_space=pltpu.VMEM)
    column, density = pl.pallas_call(
        functools.partial(kernel, rows, cols),
        name="pole_step",
        out_shape=(
            pltpu.VMEM((BR_DEV, 2, half, width), f32),
            pltpu.VMEM((boxes, points), f32),
        ),
        in_specs=[smem] * 3 + [hbm] * 5,
        out_specs=(vmem, vmem),
        scratch_shapes=[pltpu.VMEM((2, blocks, parts, shard_rows, width), bf16)] * 4 + [
            pltpu.VMEM(tiles.shape, bf16),
            pltpu.VMEM(box_basis.shape, bf16),
            pltpu.VMEM(supernode_basis.shape, bf16),
            pltpu.VMEM((peers, boxes, orbs), jnp.int32),
            pltpu.VMEM((BR_DEV, block, 2 * width), f32),
            pltpu.VMEM((BR_DEV, half, 2 * width), f32),
            pltpu.VMEM((peers * capacity, BR_DEV * half), bf16),
            pltpu.VMEM((boxes, peers * capacity, points), bf16),
            pltpu.VMEM((boxes, peers, orbs), f32),
            pltpu.VMEM((boxes, peers, orbs), f32),
            pltpu.VMEM((peers, capacity, width), bf16),
            pltpu.VMEM((peers, capacity, width), bf16),
            dma((5,)),
            dma((3, 4, pieces)),
            dma((4, 2, pieces)),
            pltpu.SemaphoreType.REGULAR((2,)),
            dma((2,)),
            dma((peers,)),
            dma((peers,)),
            dma((peers,)),
            dma((peers,)),
        ],
        compiler_params=pltpu.CompilerParams(
            collective_id=0, has_side_effects=True, vmem_limit_bytes=56 * 1024 * 1024),
    )(tile_slot, tile_col, pole_weight, panel, tiles, box_orbitals, box_basis, supernode_basis)
    return pl.pallas_call(
        deliver,
        name="deliver",
        out_shape=(
            jax.ShapeDtypeStruct(column.shape, f32),
            jax.ShapeDtypeStruct(density.shape, f32),
        ),
        in_specs=[vmem] * 2,
        out_specs=(hbm, hbm),
        scratch_shapes=[dma((2,))],
        compiler_params=pltpu.CompilerParams(vmem_limit_bytes=8 * 1024 * 1024),
    )(column, density)


def plain(panel, tiles, tile_slot, tile_col, pole_weight, box_orbitals, box_basis, supernode_basis):
    gathered = lax.all_gather(panel, "row", axis=3, tiled=True)
    blocks = gathered[0]
    selector = (tile_col[:, None] == jnp.arange(blocks.shape[0], dtype=jnp.int32)[None, :]).astype(
        jnp.bfloat16
    )
    chosen = jnp.einsum(
        "tj,jcbs->tcbs", selector, blocks, preferred_element_type=jnp.float32
    ).astype(jnp.bfloat16)
    real_part = jnp.einsum(
        "tab,tbs->tas", tiles[:, 0], chosen[:, 0], preferred_element_type=jnp.float32
    )
    real_part = real_part - jnp.einsum(
        "tab,tbs->tas", tiles[:, 1], chosen[:, 1], preferred_element_type=jnp.float32
    )
    imag_part = jnp.einsum(
        "tab,tbs->tas", tiles[:, 0], chosen[:, 1], preferred_element_type=jnp.float32
    )
    imag_part = imag_part + jnp.einsum(
        "tab,tbs->tas", tiles[:, 1], chosen[:, 0], preferred_element_type=jnp.float32
    )
    products = jnp.stack([real_part, imag_part], axis=1)
    partial_value = jnp.stack(
        [
            jnp.sum(jnp.where((tile_slot == slot_row)[:, None, None, None], products, 0.0), axis=0)
            for slot_row in range(BR_DEV)
        ]
    )
    summed = lax.psum_scatter(partial_value, "col", scatter_dimension=2, tiled=True)
    inverse_column = -summed
    density_local = (
        pole_weight[0] * inverse_column[:, 1] + pole_weight[1] * inverse_column[:, 0]
    ).astype(jnp.bfloat16)
    columns = density_local.shape[2]
    density_local = density_local.reshape(-1, columns)
    block_width = tiles.shape[2]
    col_count = lax.axis_size("col")
    half_rows = block_width // col_count
    wanted = box_orbitals.reshape(-1)
    wanted_total = wanted.shape[0]
    block_index = wanted // block_width
    within = wanted % block_width
    source = block_index // BR_DEV * col_count + within // half_rows
    local_row = block_index % BR_DEV * half_rows + within % half_rows
    start_rows = jnp.zeros((wanted_total, columns), jnp.bfloat16)
    shards = lax.all_gather(density_local[None], ("row", "col"), axis=0, tiled=True)
    count = shards.shape[0]
    inside = (source >= 0) & (source < count)
    clipped = jnp.clip(source, 0, count - 1)
    fetched = shards[clipped, local_row]
    picked = jnp.where(inside[:, None], fetched, start_rows)
    picked = picked.reshape(box_basis.shape[0], box_basis.shape[1], columns)
    projected = jnp.einsum("nas,nap->nsp", picked, box_basis, preferred_element_type=jnp.float32)
    density = jnp.sum(supernode_basis.astype(jnp.float32) * projected, axis=1)
    return (inverse_column, density)


def solution(mesh):
    rows, cols = mesh.shape["row"], mesh.shape["col"]

    def local(panel, *rest):
        if cols == 2 and rows == 8 and panel.shape[1] % 8 == 0 and 2 * panel.shape[3] % panel.shape[4] == 0:
            return fused(rows, cols, panel, *rest)
        return plain(panel, *rest)

    return jax.shard_map(
        local,
        mesh=mesh,
        in_specs=(
            P(("pole", "col"), None, None, "row", None),
            P(("pole", "row", "col"), None, None, None),
            P(("pole", "row", "col")),
            P(("pole", "row", "col")),
            P("pole"),
            P(("pole", "row", "col"), None),
            P(("pole", "row", "col"), None, None),
            P(("pole", "row", "col"), None, None),
        ),
        out_specs=(P(("pole", "row"), None, "col", None), P(("pole", "row", "col"), None)),
        check_vma=False,
    )
```

```python
import functools

import jax
import jax.numpy as jnp
from jax import lax
from jax.experimental import pallas as pl
from jax.experimental.pallas import tpu as pltpu
from jax.sharding import PartitionSpec as P

BR_DEV = 2
MESH = pl.DeviceIdType.MESH


def log2(value):
    assert value & (value - 1) == 0
    return value.bit_length() - 1


def kernel(
    rows, cols, slot_ref, tcol_ref, weight_ref, panel, tiles, orbitals, basis, super_basis,
    inv_ref, density_ref, own, near, third, last,
    tile_buf, basis_buf, super_buf, orb_buf, acc, half_in, mix_out, mix_own, mix_in, pick_hot, basis_hot, order_buf, local_buf,
    send_rows, recv_rows, local_sem, send_sem, recv_sem, token, col_sem, orb_send, orb_recv, row_send, row_recv,
):
    lanes_y = 2
    depth_z = rows // lanes_y
    peers = rows * cols
    r = lax.axis_index("row")
    c = lax.axis_index("col")
    me = r * cols + c
    z = r // lanes_y
    y = r % lanes_y
    shard_rows = panel.shape[3]
    width = panel.shape[4]
    pieces = recv_sem.shape[2]
    step = panel.shape[1] // pieces
    split_at = pieces // 2
    tile_count = tiles.shape[0]
    block = tiles.shape[2]
    half = block // cols
    pair = lanes_y * shard_rows
    boxes, orbs = orbitals.shape
    capacity = send_rows.shape[1]

    inner = 1 - 2 * (z // (depth_z // 2))
    corner = jnp.logical_or(z == 0, z == depth_z - 1)
    middle = jnp.logical_not(corner)
    other = r + 1 - 2 * y
    inward = r + lanes_y * inner
    outward = r - lanes_y * inner
    buffers = (own, near, third, last)
    places = (
        z,
        z + inner,
        jnp.where(corner, z + 2 * inner, z - inner),
        jnp.where(corner, z + 3 * inner, z + 2 * inner),
    )
    IN, OUT, Y = 0, 1, 2

    def spot(index):
        return {"row": index // cols, "col": index % cols}

    loads = [
        pltpu.make_async_copy(panel.at[0], own.at[y], local_sem.at[0]),
        pltpu.make_async_copy(orbitals, orb_buf.at[me], local_sem.at[4]),
        pltpu.make_async_copy(basis, basis_buf, local_sem.at[2]),
        pltpu.make_async_copy(tiles, tile_buf, local_sem.at[1]),
        pltpu.make_async_copy(super_basis, super_buf, local_sem.at[3]),
    ]
    for load in loads[:3]:
        load.start()

    barrier = pltpu.get_barrier_semaphore()
    for device in (
        {"row": other}, {"col": 1 - c}, {"row": other, "col": 1 - c}, {"row": inward},
    ):
        pl.semaphore_signal(barrier, inc=1, device_id=device, device_id_type=MESH)

    @pl.when(middle)
    def _():
        pl.semaphore_signal(barrier, inc=1, device_id={"row": outward}, device_id_type=MESH)
        pl.semaphore_wait(barrier, 5)

    @pl.when(corner)
    def _():
        pl.semaphore_wait(barrier, 4)

    loads[0].wait()

    def piece(which, lane, p):
        return buffers[which].at[lane, pl.ds(p * step, step)]

    def copy(link, kind, source, target, lane, p):
        row = (inward, outward, other)[link]
        return pltpu.make_async_remote_copy(
            src_ref=piece(source, lane, p), dst_ref=piece(target, lane, p),
            send_sem=send_sem.at[link, kind, p], recv_sem=recv_sem.at[target, lane, p],
            device_id={"row": row}, device_id_type=MESH,
        )

    def arrived(target, lane, p):
        dst = piece(target, lane, p)
        pltpu.make_async_remote_copy(
            src_ref=dst, dst_ref=dst, send_sem=send_sem.at[0, 0, p], recv_sem=recv_sem.at[target, lane, p],
            device_id={"row": other}, device_id_type=MESH,
        ).wait_recv()

    def each(low, high, body):
        def run(h, carry):
            body(h)
            return carry
        lax.fori_loop(low, high, run, 0)

    corner_sends = {
        "own_in": (IN, 0, 0, 2, y), "own_y": (Y, 0, 0, 0, y),
        "extra": (IN, 1, 0, 2, 1 - y),
        "near_y": (Y, 1, 1, 1, y), "third_y": (Y, 2, 2, 2, y), "last_y": (Y, 3, 3, 3, y),
    }
    middle_sends = {
        "own_out": (OUT, 0, 0, 1, y), "own_in": (IN, 0, 0, 1, y), "own_y": (Y, 0, 0, 0, y),
        "third_in": (IN, 1, 2, 3, y),
        "near_out": (OUT, 1, 1, 2, y), "near_y": (Y, 1, 1, 1, y),
        "last_out": (OUT, 2, 3, 3, y), "last_y": (Y, 2, 3, 3, y),
        "extra": (OUT, 3, 3, 3, 1 - y),
    }

    def at_corner(name, p):
        return copy(*corner_sends[name], p)

    def at_middle(name, p):
        return copy(*middle_sends[name], p)

    @pl.when(corner)
    def _():
        def go(p):
            at_corner("own_in", p).start()
            at_corner("own_y", p).start()
        each(0, pieces, go)

    @pl.when(middle)
    def _():
        def go(p):
            at_middle("own_out", p).start()
            at_middle("own_in", p).start()
            at_middle("own_y", p).start()
        each(0, pieces, go)

    for load in loads[3:]:
        load.start()
    acc[...] = jnp.zeros_like(acc)
    block_bits, half_bits = log2(block), log2(half)

    def split(g):
        row_block = g >> block_bits
        within = g & (block - 1)
        source = (row_block >> log2(BR_DEV)) * cols + (within >> half_bits)
        local = (row_block & (BR_DEV - 1)) * half + (within & (half - 1))
        return source, local

    def ranks(masks):
        before = lax.broadcasted_iota(jnp.int32, (orbs, orbs), 0)
        after = lax.broadcasted_iota(jnp.int32, (orbs, orbs), 1)
        upper = jnp.where(before <= after, 1.0, 0.0).astype(jnp.bfloat16)
        seen = jnp.zeros((masks[0].shape[0], 1), jnp.float32)
        result = []
        for mask in masks:
            counted = jnp.dot(mask.astype(jnp.bfloat16), upper, preferred_element_type=jnp.float32)
            result.append(counted - 1.0 + seen)
            seen = seen + jnp.sum(mask, axis=1, keepdims=True)
        return result

    def place_basis():
        loads[1].wait()
        loads[2].wait()
        masks = []
        peer_id = lax.broadcasted_iota(jnp.int32, (peers, orbs), 0)
        for n in range(boxes):
            source, _ = split(orb_buf[me, n:n + 1, :])
            masks.append(jnp.where(peer_id == source, 1.0, 0.0))
        order = ranks(masks)
        arrive = lax.broadcasted_iota(jnp.int32, (peers * capacity, orbs), 0).astype(jnp.float32)
        for n in range(boxes):
            position = jnp.sum(
                masks[n] * (order[n] + (peer_id * capacity).astype(jnp.float32)), axis=0, keepdims=True)
            hot = jnp.where(arrive == position, 1.0, 0.0).astype(jnp.bfloat16)
            basis_hot[n] = jnp.dot(hot, basis_buf[n], preferred_element_type=jnp.float32).astype(jnp.bfloat16)

    def orb_copy(k):
        return pltpu.make_async_remote_copy(
            src_ref=orbitals, dst_ref=orb_buf.at[me], send_sem=orb_send.at[k], recv_sem=orb_recv.at[k],
            device_id=spot((me + k) % peers), device_id_type=MESH,
        )

    def rank_orbitals():
        for k in range(1, peers):
            origin = (me + peers - k) % peers
            dst = orb_buf.at[origin]
            pltpu.make_async_remote_copy(
                src_ref=dst, dst_ref=dst, send_sem=orb_send.at[k], recv_sem=orb_recv.at[k],
                device_id=spot(origin), device_id_type=MESH,
            ).wait_recv()
        asked = []
        for n in range(boxes):
            g = jnp.concatenate([orb_buf[q, n:n + 1, :] for q in range(peers)], axis=0)
            source, local = split(g)
            asked.append((jnp.where(source == me, 1.0, 0.0), local.astype(jnp.float32)))
        order = ranks([a[0] for a in asked])
        for n in range(boxes):
            order_buf[n] = jnp.where(asked[n][0] > 0.5, order[n], -1.0)
            local_buf[n] = asked[n][1] + 1.0

    def place_picks(q):
        place = lax.broadcasted_iota(jnp.int32, (capacity, orbs), 0).astype(jnp.float32)
        row_id = lax.broadcasted_iota(jnp.int32, (capacity, BR_DEV * half), 1).astype(jnp.float32)
        found = jnp.zeros((capacity, 1), jnp.float32)
        for n in range(boxes):
            hit = place == order_buf[n, pl.ds(q, 1), :]
            found = found + jnp.sum(jnp.where(hit, local_buf[n, pl.ds(q, 1), :], 0.0), axis=1, keepdims=True)
        spot_rows = pl.ds(pl.multiple_of(q * capacity, capacity), capacity)
        pick_hot[spot_rows, :] = jnp.where(row_id == found - 1.0, 1.0, 0.0).astype(jnp.bfloat16)

    def product(which, t, out_rows):
        j = tcol_ref[t]
        offset = pl.multiple_of(places[which] * pair, pair)
        left = jnp.concatenate(
            [tile_buf[t, 0, out_rows, pl.ds(offset, pair)], tile_buf[t, 1, out_rows, pl.ds(offset, pair)]], axis=1)
        parts = [buffers[which][k, j] for k in range(lanes_y)]
        real = jnp.concatenate([p[0] for p in parts], axis=0)
        imag = jnp.concatenate([p[1] for p in parts], axis=0)
        right = jnp.concatenate(
            [jnp.concatenate([real, imag], axis=1), jnp.concatenate([-imag, real], axis=1)], axis=0)
        return jnp.dot(left, right, preferred_element_type=jnp.float32)

    def several(which, start, count, out_rows):
        values = [product(which, start + k, out_rows) for k in range(count)]
        for s in range(BR_DEV):
            total = jnp.where(slot_ref[start] == s, values[0], 0.0)
            for k in range(1, count):
                total = total + jnp.where(slot_ref[start + k] == s, values[k], 0.0)
            acc[s, out_rows, :] += total

    everything = pl.ds(0, block)

    def share(which, p, parts):
        first_tile, last_tile = p * tile_count // parts, (p + 1) * tile_count // parts
        for start in range(first_tile, last_tile, 4):
            several(which, start, min(4, last_tile - start), everything)

    place_basis()

    def first(p):
        @pl.when(corner)
        def _():
            arrived(1, y, p)
            at_corner("near_y", p).start()
            arrived(0, 1 - y, p)
            at_corner("extra", p).start()

        @pl.when(middle)
        def _():
            arrived(2, y, p)
            at_middle("third_in", p).start()
            arrived(1, y, p)
            at_middle("near_out", p).start()
            at_middle("near_y", p).start()

            @pl.when(p == 0)
            def _():
                pl.semaphore_signal(token.at[0], inc=1, device_id={"row": inward}, device_id_type=MESH)

            @pl.when(p == pieces - 1)
            def _():
                pl.semaphore_wait(token.at[0], 1)
                pl.semaphore_signal(token.at[1], inc=1, device_id={"row": outward}, device_id_type=MESH)

    each(0, pieces, first)

    @pl.when(corner)
    def _():
        pl.semaphore_wait(token.at[1], 1)

    for k in range(1, peers):
        orb_copy(k).start()

    @pl.when(middle)
    def _():
        each(0, pieces, lambda p: arrived(0, 1 - y, p))

    loads[3].wait()

    def second(p):
        @pl.when(corner)
        def _():
            arrived(2, y, p)
            at_corner("third_y", p).start()

        @pl.when(middle)
        def _():
            arrived(3, y, p)
            at_middle("last_out", p).start()
            if p >= split_at:
                at_middle("last_y", p).start()

        share(0, p, pieces)

    for p in range(pieces):
        second(p)

    @pl.when(middle)
    def _():
        each(0, split_at, lambda p: at_middle("last_y", p).start())

    each(0, pieces, lambda p: arrived(1, 1 - y, p))

    def closing(p):
        share(1, p, split_at)

        @pl.when(corner)
        def _():
            arrived(3, y, p)
            at_corner("last_y", p).start()

        @pl.when(middle)
        def _():
            arrived(3, 1 - y, p + split_at)
            at_middle("extra", p + split_at).start()

    for p in range(split_at):
        closing(p)
    rank_orbitals()
    each(0, peers // 4, lambda q: [place_picks(4 * q + k) for k in range(4)])
    each(0, pieces, lambda p: arrived(2, 1 - y, p))
    share(2, 0, 1)

    @pl.when(corner)
    def _():
        each(split_at, pieces, lambda p: arrived(3, y, p))
        each(split_at, pieces, lambda p: arrived(3, 1 - y, p))
    each(0, split_at, lambda p: arrived(3, 1 - y, p))

    mine = pl.ds(pl.multiple_of(c * half, half), half)
    theirs = pl.ds(pl.multiple_of((1 - c) * half, half), half)

    def to_partner(which, src, dst):
        return pltpu.make_async_remote_copy(
            src_ref=src, dst_ref=dst, send_sem=col_sem.at[0, which], recv_sem=col_sem.at[1, which],
            device_id={"col": 1 - c}, device_id_type=MESH,
        )

    mix_swap = to_partner(0, mix_out, mix_in)
    swap = to_partner(1, acc.at[:, theirs, :], half_in)

    def mixed(s, out_rows):
        return weight_ref[0] * acc[s, out_rows, width:] + weight_ref[1] * acc[s, out_rows, :width]

    for start in range(0, tile_count, 4):
        several(3, start, min(4, tile_count - start), theirs)
    for s in range(BR_DEV):
        mix_out[s] = mixed(s, theirs)
    mix_swap.start()
    swap.start()
    for start in range(0, tile_count, 4):
        several(3, start, min(4, tile_count - start), mine)
    for s in range(BR_DEV):
        mix_own[s] = mixed(s, mine)
    mix_swap.wait_recv()
    density_rows = [(-(mix_own[s] + mix_in[s])).astype(jnp.bfloat16) for s in range(BR_DEV)]
    density_rows = jnp.concatenate(density_rows, axis=0)

    group = lanes_y * cols

    def row_copy(target):
        return pltpu.make_async_remote_copy(
            src_ref=send_rows.at[target], dst_ref=recv_rows.at[me],
            send_sem=row_send.at[target], recv_sem=row_recv.at[me],
            device_id=spot(target), device_id_type=MESH,
        )

    for at_z in (places[3], places[2], places[1]):
        base = at_z * group
        hot = pick_hot[pl.ds(pl.multiple_of(base * capacity, group * capacity), group * capacity), :]
        picked = jnp.dot(hot, density_rows, preferred_element_type=jnp.float32).astype(jnp.bfloat16)
        send_rows[pl.ds(base, group)] = picked.reshape(group, capacity, width)
        for k in range(group):
            row_copy(base + k).start()
    base = z * group
    hot = pick_hot[pl.ds(pl.multiple_of(base * capacity, group * capacity), group * capacity), :]
    picked = jnp.dot(hot, density_rows, preferred_element_type=jnp.float32).astype(jnp.bfloat16)
    send_rows[pl.ds(base, group)] = picked.reshape(group, capacity, width)
    for k in range(1, group):
        row_copy(base + (me - base + k) % group).start()
    recv_rows[me] = send_rows[me]
    swap.wait_recv()
    for s in range(BR_DEV):
        column = -(acc[s, mine, :] + half_in[s])
        inv_ref[s, 0] = column[:, :width]
        inv_ref[s, 1] = column[:, width:]
    loads[4].wait()

    @pl.when(corner)
    def _():
        def sent(p):
            for name in corner_sends:
                if name != "last_y":
                    at_corner(name, p).wait_send()
        each(0, pieces, sent)
        each(0, split_at, lambda p: at_corner("last_y", p).wait_send())

    @pl.when(middle)
    def _():
        def sent(p):
            for name in middle_sends:
                if name != "extra":
                    at_middle(name, p).wait_send()
        each(0, pieces, sent)
        each(split_at, pieces, lambda p: at_middle("extra", p).wait_send())

    mix_swap.wait_send()
    swap.wait_send()
    for k in range(1, peers):
        orb_copy(k).wait_send()

    projected = [None] * boxes
    for at_z in range(depth_z):
        if at_z == depth_z - 1:
            for k in range(1, peers):
                row_copy((me + k) % peers).wait_send()
        for origin in range(at_z * group, (at_z + 1) * group):
            @pl.when(me != origin)
            def _(origin=origin):
                dst = recv_rows.at[origin]
                pltpu.make_async_remote_copy(
                    src_ref=dst, dst_ref=dst, send_sem=row_send.at[origin], recv_sem=row_recv.at[origin],
                    device_id={"row": other}, device_id_type=MESH,
                ).wait_recv()
        got = recv_rows[at_z * group:(at_z + 1) * group].reshape(group * capacity, width)
        for n in range(boxes):
            value = lax.dot_general(
                got, basis_hot[n, at_z * group * capacity:(at_z + 1) * group * capacity, :],
                (((0,), (0,)), ((), ())), preferred_element_type=jnp.float32)
            projected[n] = value if at_z == 0 else projected[n] + value
    for n in range(boxes):
        density_ref[n:n + 1, :] = jnp.sum(
            super_buf[n].astype(jnp.float32) * projected[n], axis=0, keepdims=True)


def deliver(column, density, column_out, density_out, sem):
    copies = [
        pltpu.make_async_copy(column, column_out, sem.at[0]),
        pltpu.make_async_copy(density, density_out, sem.at[1]),
    ]
    for copy in copies:
        copy.start()
    for copy in copies:
        copy.wait()


def fused(rows, cols, panel, tiles, tile_slot, tile_col, pole_weight, box_orbitals, box_basis, supernode_basis):
    blocks, parts, shard_rows, width = panel.shape[1:]
    tile_count, _, block, _ = tiles.shape
    boxes, orbs = box_orbitals.shape
    points = box_basis.shape[2]
    half = block // cols
    peers = rows * cols
    capacity = 2 * boxes * orbs // peers
    pieces = blocks // 2
    dma = pltpu.SemaphoreType.DMA
    bf16, f32 = jnp.bfloat16, jnp.float32
    smem = pl.BlockSpec(memory_space=pltpu.SMEM)
    hbm = pl.BlockSpec(memory_space=pl.ANY)
    vmem = pl.BlockSpec(memory_space=pltpu.VMEM)
    column, density = pl.pallas_call(
        functools.partial(kernel, rows, cols),
        name="pole_step",
        out_shape=(
            pltpu.VMEM((BR_DEV, 2, half, width), f32),
            pltpu.VMEM((boxes, points), f32),
        ),
        in_specs=[smem] * 3 + [hbm] * 5,
        out_specs=(vmem, vmem),
        scratch_shapes=[pltpu.VMEM((2, blocks, parts, shard_rows, width), bf16)] * 4 + [
            pltpu.VMEM(tiles.shape, bf16),
            pltpu.VMEM(box_basis.shape, bf16),
            pltpu.VMEM(supernode_basis.shape, bf16),
            pltpu.VMEM((peers, boxes, orbs), jnp.int32),
            pltpu.VMEM((BR_DEV, block, 2 * width), f32),
            pltpu.VMEM((BR_DEV, half, 2 * width), f32),
            pltpu.VMEM((BR_DEV, half, width), f32),
            pltpu.VMEM((BR_DEV, half, width), f32),
            pltpu.VMEM((BR_DEV, half, width), f32),
            pltpu.VMEM((peers * capacity, BR_DEV * half), bf16),
            pltpu.VMEM((boxes, peers * capacity, points), bf16),
            pltpu.VMEM((boxes, peers, orbs), f32),
            pltpu.VMEM((boxes, peers, orbs), f32),
            pltpu.VMEM((peers, capacity, width), bf16),
            pltpu.VMEM((peers, capacity, width), bf16),
            dma((5,)),
            dma((3, 4, pieces)),
            dma((4, 2, pieces)),
            pltpu.SemaphoreType.REGULAR((2,)),
            dma((2, 2)),
            dma((peers,)),
            dma((peers,)),
            dma((peers,)),
            dma((peers,)),
        ],
        compiler_params=pltpu.CompilerParams(
            collective_id=0, has_side_effects=True, vmem_limit_bytes=56 * 1024 * 1024),
    )(tile_slot, tile_col, pole_weight, panel, tiles, box_orbitals, box_basis, supernode_basis)
    return pl.pallas_call(
        deliver,
        name="deliver",
        out_shape=(
            jax.ShapeDtypeStruct(column.shape, f32),
            jax.ShapeDtypeStruct(density.shape, f32),
        ),
        in_specs=[vmem] * 2,
        out_specs=(hbm, hbm),
        scratch_shapes=[dma((2,))],
        compiler_params=pltpu.CompilerParams(vmem_limit_bytes=8 * 1024 * 1024),
    )(column, density)


def plain(panel, tiles, tile_slot, tile_col, pole_weight, box_orbitals, box_basis, supernode_basis):
    gathered = lax.all_gather(panel, "row", axis=3, tiled=True)
    blocks = gathered[0]
    selector = (tile_col[:, None] == jnp.arange(blocks.shape[0], dtype=jnp.int32)[None, :]).astype(
        jnp.bfloat16
    )
    chosen = jnp.einsum(
        "tj,jcbs->tcbs", selector, blocks, preferred_element_type=jnp.float32
    ).astype(jnp.bfloat16)
    real_part = jnp.einsum(
        "tab,tbs->tas", tiles[:, 0], chosen[:, 0], preferred_element_type=jnp.float32
    )
    real_part = real_part - jnp.einsum(
        "tab,tbs->tas", tiles[:, 1], chosen[:, 1], preferred_element_type=jnp.float32
    )
    imag_part = jnp.einsum(
        "tab,tbs->tas", tiles[:, 0], chosen[:, 1], preferred_element_type=jnp.float32
    )
    imag_part = imag_part + jnp.einsum(
        "tab,tbs->tas", tiles[:, 1], chosen[:, 0], preferred_element_type=jnp.float32
    )
    products = jnp.stack([real_part, imag_part], axis=1)
    partial_value = jnp.stack(
        [
            jnp.sum(jnp.where((tile_slot == slot_row)[:, None, None, None], products, 0.0), axis=0)
            for slot_row in range(BR_DEV)
        ]
    )
    summed = lax.psum_scatter(partial_value, "col", scatter_dimension=2, tiled=True)
    inverse_column = -summed
    density_local = (
        pole_weight[0] * inverse_column[:, 1] + pole_weight[1] * inverse_column[:, 0]
    ).astype(jnp.bfloat16)
    columns = density_local.shape[2]
    density_local = density_local.reshape(-1, columns)
    block_width = tiles.shape[2]
    col_count = lax.axis_size("col")
    half_rows = block_width // col_count
    wanted = box_orbitals.reshape(-1)
    wanted_total = wanted.shape[0]
    block_index = wanted // block_width
    within = wanted % block_width
    source = block_index // BR_DEV * col_count + within // half_rows
    local_row = block_index % BR_DEV * half_rows + within % half_rows
    start_rows = jnp.zeros((wanted_total, columns), jnp.bfloat16)
    shards = lax.all_gather(density_local[None], ("row", "col"), axis=0, tiled=True)
    count = shards.shape[0]
    inside = (source >= 0) & (source < count)
    clipped = jnp.clip(source, 0, count - 1)
    fetched = shards[clipped, local_row]
    picked = jnp.where(inside[:, None], fetched, start_rows)
    picked = picked.reshape(box_basis.shape[0], box_basis.shape[1], columns)
    projected = jnp.einsum("nas,nap->nsp", picked, box_basis, preferred_element_type=jnp.float32)
    density = jnp.sum(supernode_basis.astype(jnp.float32) * projected, axis=1)
    return (inverse_column, density)


def solution(mesh):
    rows, cols = mesh.shape["row"], mesh.shape["col"]

    def local(panel, *rest):
        if cols == 2 and rows == 8 and panel.shape[1] % 8 == 0 and 2 * panel.shape[3] % panel.shape[4] == 0:
            return fused(rows, cols, panel, *rest)
        return plain(panel, *rest)

    return jax.shard_map(
        local,
        mesh=mesh,
        in_specs=(
            P(("pole", "col"), None, None, "row", None),
            P(("pole", "row", "col"), None, None, None),
            P(("pole", "row", "col")),
            P(("pole", "row", "col")),
            P("pole"),
            P(("pole", "row", "col"), None),
            P(("pole", "row", "col"), None, None),
            P(("pole", "row", "col"), None, None),
        ),
        out_specs=(P(("pole", "row"), None, "col", None), P(("pole", "row", "col"), None)),
        check_vma=False,
    )
```

```python
import functools

import jax
import jax.numpy as jnp
from jax import lax
from jax.experimental import pallas as pl
from jax.experimental.pallas import tpu as pltpu
from jax.sharding import PartitionSpec as P

BR_DEV = 2
MESH = pl.DeviceIdType.MESH


def log2(value):
    assert value & (value - 1) == 0
    return value.bit_length() - 1


def kernel(
    rows, cols, slots, tile_cols, weights, panel, tiles, orbitals, basis, super_basis,
    inv_ref, density_ref, slot_ref, tcol_ref, weight_ref, own, near, third, last,
    tile_buf, basis_buf, super_buf, orb_buf, acc, half_in, mix_out, mix_own, mix_in, pick_hot, basis_hot, order_buf, local_buf,
    send_rows, recv_rows, local_sem, send_sem, recv_sem, token, col_sem, orb_send, orb_recv, row_send, row_recv,
):
    lanes_y = 2
    depth_z = rows // lanes_y
    peers = rows * cols
    r = lax.axis_index("row")
    c = lax.axis_index("col")
    me = r * cols + c
    z = r // lanes_y
    y = r % lanes_y
    shard_rows = panel.shape[3]
    width = panel.shape[4]
    pieces = recv_sem.shape[2]
    step = panel.shape[1] // pieces
    split_at = pieces // 2
    tile_count = tiles.shape[0]
    block = tiles.shape[2]
    half = block // cols
    pair = lanes_y * shard_rows
    boxes, orbs = orbitals.shape
    capacity = send_rows.shape[1]

    inner = 1 - 2 * (z // (depth_z // 2))
    corner = jnp.logical_or(z == 0, z == depth_z - 1)
    middle = jnp.logical_not(corner)
    other = r + 1 - 2 * y
    inward = r + lanes_y * inner
    outward = r - lanes_y * inner
    buffers = (own, near, third, last)
    places = (
        z,
        z + inner,
        jnp.where(corner, z + 2 * inner, z - inner),
        jnp.where(corner, z + 3 * inner, z + 2 * inner),
    )
    IN, OUT, Y = 0, 1, 2

    def spot(index):
        return {"row": index // cols, "col": index % cols}

    loads = [
        pltpu.make_async_copy(panel.at[0], own.at[y], local_sem.at[0]),
        pltpu.make_async_copy(orbitals, orb_buf.at[me], local_sem.at[4]),
        pltpu.make_async_copy(basis, basis_buf, local_sem.at[2]),
        pltpu.make_async_copy(tiles, tile_buf, local_sem.at[1]),
        pltpu.make_async_copy(super_basis, super_buf, local_sem.at[3]),
        pltpu.make_async_copy(slots, slot_ref, local_sem.at[5]),
        pltpu.make_async_copy(tile_cols, tcol_ref, local_sem.at[6]),
        pltpu.make_async_copy(weights, weight_ref, local_sem.at[7]),
    ]
    barrier = pltpu.get_barrier_semaphore()
    for device in (
        {"row": other}, {"col": 1 - c}, {"row": other, "col": 1 - c}, {"row": inward},
    ):
        pl.semaphore_signal(barrier, inc=1, device_id=device, device_id_type=MESH)

    @pl.when(middle)
    def _():
        pl.semaphore_signal(barrier, inc=1, device_id={"row": outward}, device_id_type=MESH)

    for load in loads[:3]:
        load.start()

    @pl.when(middle)
    def _():
        pl.semaphore_wait(barrier, 5)

    @pl.when(corner)
    def _():
        pl.semaphore_wait(barrier, 4)

    loads[0].wait()

    def piece(which, lane, p):
        return buffers[which].at[lane, pl.ds(p * step, step)]

    def copy(link, kind, source, target, lane, p):
        row = (inward, outward, other)[link]
        return pltpu.make_async_remote_copy(
            src_ref=piece(source, lane, p), dst_ref=piece(target, lane, p),
            send_sem=send_sem.at[link, kind, p], recv_sem=recv_sem.at[target, lane, p],
            device_id={"row": row}, device_id_type=MESH,
        )

    def arrived(target, lane, p):
        dst = piece(target, lane, p)
        pltpu.make_async_remote_copy(
            src_ref=dst, dst_ref=dst, send_sem=send_sem.at[0, 0, p], recv_sem=recv_sem.at[target, lane, p],
            device_id={"row": other}, device_id_type=MESH,
        ).wait_recv()

    def each(low, high, body):
        def run(h, carry):
            body(h)
            return carry
        lax.fori_loop(low, high, run, 0)

    corner_sends = {
        "own_in": (IN, 0, 0, 2, y), "own_y": (Y, 0, 0, 0, y),
        "extra": (IN, 1, 0, 2, 1 - y),
        "near_y": (Y, 1, 1, 1, y), "third_y": (Y, 2, 2, 2, y), "last_y": (Y, 3, 3, 3, y),
    }
    middle_sends = {
        "own_out": (OUT, 0, 0, 1, y), "own_in": (IN, 0, 0, 1, y), "own_y": (Y, 0, 0, 0, y),
        "third_in": (IN, 1, 2, 3, y),
        "near_out": (OUT, 1, 1, 2, y), "near_y": (Y, 1, 1, 1, y),
        "last_out": (OUT, 2, 3, 3, y), "last_y": (Y, 2, 3, 3, y),
        "extra": (OUT, 3, 3, 3, 1 - y),
    }

    def at_corner(name, p):
        return copy(*corner_sends[name], p)

    def at_middle(name, p):
        return copy(*middle_sends[name], p)

    @pl.when(corner)
    def _():
        def go(p):
            at_corner("own_in", p).start()
            at_corner("own_y", p).start()
        each(0, pieces, go)

    @pl.when(middle)
    def _():
        def go(p):
            at_middle("own_out", p).start()
            at_middle("own_in", p).start()
            at_middle("own_y", p).start()
        each(0, pieces, go)

    for load in loads[3:]:
        load.start()
    acc[...] = jnp.zeros_like(acc)
    block_bits, half_bits = log2(block), log2(half)

    def split(g):
        row_block = g >> block_bits
        within = g & (block - 1)
        source = (row_block >> log2(BR_DEV)) * cols + (within >> half_bits)
        local = (row_block & (BR_DEV - 1)) * half + (within & (half - 1))
        return source, local

    def ranks(masks):
        before = lax.broadcasted_iota(jnp.int32, (orbs, orbs), 0)
        after = lax.broadcasted_iota(jnp.int32, (orbs, orbs), 1)
        upper = jnp.where(before <= after, 1.0, 0.0).astype(jnp.bfloat16)
        seen = jnp.zeros((masks[0].shape[0], 1), jnp.float32)
        result = []
        for mask in masks:
            counted = jnp.dot(mask.astype(jnp.bfloat16), upper, preferred_element_type=jnp.float32)
            result.append(counted - 1.0 + seen)
            seen = seen + jnp.sum(mask, axis=1, keepdims=True)
        return result

    def place_basis():
        loads[1].wait()
        loads[2].wait()
        masks = []
        peer_id = lax.broadcasted_iota(jnp.int32, (peers, orbs), 0)
        for n in range(boxes):
            source, _ = split(orb_buf[me, n:n + 1, :])
            masks.append(jnp.where(peer_id == source, 1.0, 0.0))
        order = ranks(masks)
        arrive = lax.broadcasted_iota(jnp.int32, (peers * capacity, orbs), 0).astype(jnp.float32)
        for n in range(boxes):
            position = jnp.sum(
                masks[n] * (order[n] + (peer_id * capacity).astype(jnp.float32)), axis=0, keepdims=True)
            hot = jnp.where(arrive == position, 1.0, 0.0).astype(jnp.bfloat16)
            basis_hot[n] = jnp.dot(hot, basis_buf[n], preferred_element_type=jnp.float32).astype(jnp.bfloat16)

    def orb_copy(k):
        return pltpu.make_async_remote_copy(
            src_ref=orbitals, dst_ref=orb_buf.at[me], send_sem=orb_send.at[k], recv_sem=orb_recv.at[k],
            device_id=spot((me + k) % peers), device_id_type=MESH,
        )

    def rank_orbitals():
        for k in range(1, peers):
            origin = (me + peers - k) % peers
            dst = orb_buf.at[origin]
            pltpu.make_async_remote_copy(
                src_ref=dst, dst_ref=dst, send_sem=orb_send.at[k], recv_sem=orb_recv.at[k],
                device_id=spot(origin), device_id_type=MESH,
            ).wait_recv()
        asked = []
        for n in range(boxes):
            g = jnp.concatenate([orb_buf[q, n:n + 1, :] for q in range(peers)], axis=0)
            source, local = split(g)
            asked.append((jnp.where(source == me, 1.0, 0.0), local.astype(jnp.float32)))
        order = ranks([a[0] for a in asked])
        for n in range(boxes):
            order_buf[n] = jnp.where(asked[n][0] > 0.5, order[n], -1.0)
            local_buf[n] = asked[n][1] + 1.0

    def place_picks(q):
        place = lax.broadcasted_iota(jnp.int32, (capacity, orbs), 0).astype(jnp.float32)
        row_id = lax.broadcasted_iota(jnp.int32, (capacity, BR_DEV * half), 1).astype(jnp.float32)
        found = jnp.zeros((capacity, 1), jnp.float32)
        for n in range(boxes):
            hit = place == order_buf[n, pl.ds(q, 1), :]
            found = found + jnp.sum(jnp.where(hit, local_buf[n, pl.ds(q, 1), :], 0.0), axis=1, keepdims=True)
        spot_rows = pl.ds(pl.multiple_of(q * capacity, capacity), capacity)
        pick_hot[spot_rows, :] = jnp.where(row_id == found - 1.0, 1.0, 0.0).astype(jnp.bfloat16)

    def product(which, t, out_rows):
        j = tcol_ref[t]
        offset = pl.multiple_of(places[which] * pair, pair)
        left = jnp.concatenate(
            [tile_buf[t, 0, out_rows, pl.ds(offset, pair)], tile_buf[t, 1, out_rows, pl.ds(offset, pair)]], axis=1)
        parts = [buffers[which][k, j] for k in range(lanes_y)]
        real = jnp.concatenate([p[0] for p in parts], axis=0)
        imag = jnp.concatenate([p[1] for p in parts], axis=0)
        right = jnp.concatenate(
            [jnp.concatenate([real, imag], axis=1), jnp.concatenate([-imag, real], axis=1)], axis=0)
        return jnp.dot(left, right, preferred_element_type=jnp.float32)

    def several(which, start, count, out_rows):
        values = [product(which, start + k, out_rows) for k in range(count)]
        for s in range(BR_DEV):
            total = jnp.where(slot_ref[start] == s, values[0], 0.0)
            for k in range(1, count):
                total = total + jnp.where(slot_ref[start + k] == s, values[k], 0.0)
            acc[s, out_rows, :] += total

    everything = pl.ds(0, block)

    def share(which, p, parts):
        first_tile, last_tile = p * tile_count // parts, (p + 1) * tile_count // parts
        for start in range(first_tile, last_tile, 4):
            several(which, start, min(4, last_tile - start), everything)

    place_basis()

    def first(p):
        @pl.when(corner)
        def _():
            arrived(1, y, p)
            at_corner("near_y", p).start()
            arrived(0, 1 - y, p)
            at_corner("extra", p).start()

        @pl.when(middle)
        def _():
            arrived(2, y, p)
            at_middle("third_in", p).start()
            arrived(1, y, p)
            at_middle("near_out", p).start()
            at_middle("near_y", p).start()

            @pl.when(p == 0)
            def _():
                pl.semaphore_signal(token.at[0], inc=1, device_id={"row": inward}, device_id_type=MESH)

            @pl.when(p == pieces - 1)
            def _():
                pl.semaphore_wait(token.at[0], 1)
                pl.semaphore_signal(token.at[1], inc=1, device_id={"row": outward}, device_id_type=MESH)

    each(0, pieces, first)

    @pl.when(corner)
    def _():
        pl.semaphore_wait(token.at[1], 1)

    for k in range(1, peers):
        orb_copy(k).start()

    @pl.when(middle)
    def _():
        each(0, pieces, lambda p: arrived(0, 1 - y, p))

    loads[3].wait()
    for load in loads[5:]:
        load.wait()

    def second(p):
        @pl.when(corner)
        def _():
            arrived(2, y, p)
            at_corner("third_y", p).start()

        @pl.when(middle)
        def _():
            arrived(3, y, p)
            at_middle("last_out", p).start()
            if p >= split_at:
                at_middle("last_y", p).start()

        share(0, p, pieces)

    for p in range(pieces):
        second(p)

    @pl.when(middle)
    def _():
        each(0, split_at, lambda p: at_middle("last_y", p).start())

    each(0, pieces, lambda p: arrived(1, 1 - y, p))

    def closing(p):
        share(1, p, split_at)

        @pl.when(corner)
        def _():
            arrived(3, y, p)
            at_corner("last_y", p).start()

        @pl.when(middle)
        def _():
            arrived(3, 1 - y, p + split_at)
            at_middle("extra", p + split_at).start()

    for p in range(split_at):
        closing(p)
    rank_orbitals()
    each(0, peers // 4, lambda q: [place_picks(4 * q + k) for k in range(4)])
    each(0, pieces, lambda p: arrived(2, 1 - y, p))
    share(2, 0, 1)

    @pl.when(corner)
    def _():
        each(split_at, pieces, lambda p: arrived(3, y, p))
        each(split_at, pieces, lambda p: arrived(3, 1 - y, p))
    each(0, split_at, lambda p: arrived(3, 1 - y, p))

    mine = pl.ds(pl.multiple_of(c * half, half), half)
    theirs = pl.ds(pl.multiple_of((1 - c) * half, half), half)

    def to_partner(which, src, dst):
        return pltpu.make_async_remote_copy(
            src_ref=src, dst_ref=dst, send_sem=col_sem.at[0, which], recv_sem=col_sem.at[1, which],
            device_id={"col": 1 - c}, device_id_type=MESH,
        )

    mix_swap = to_partner(0, mix_out, mix_in)
    swap = to_partner(1, acc.at[:, theirs, :], half_in)

    def mixed(s, out_rows):
        return weight_ref[0] * acc[s, out_rows, width:] + weight_ref[1] * acc[s, out_rows, :width]

    for start in range(0, tile_count, 4):
        several(3, start, min(4, tile_count - start), theirs)
    for s in range(BR_DEV):
        mix_out[s] = mixed(s, theirs)
    mix_swap.start()
    swap.start()
    for start in range(0, tile_count, 4):
        several(3, start, min(4, tile_count - start), mine)
    for s in range(BR_DEV):
        mix_own[s] = mixed(s, mine)
    mix_swap.wait_recv()
    density_rows = [(-(mix_own[s] + mix_in[s])).astype(jnp.bfloat16) for s in range(BR_DEV)]
    density_rows = jnp.concatenate(density_rows, axis=0)

    group = lanes_y * cols

    def row_copy(target):
        return pltpu.make_async_remote_copy(
            src_ref=send_rows.at[target], dst_ref=recv_rows.at[me],
            send_sem=row_send.at[target], recv_sem=row_recv.at[me],
            device_id=spot(target), device_id_type=MESH,
        )

    for at_z in (places[3], places[2], places[1]):
        base = at_z * group
        hot = pick_hot[pl.ds(pl.multiple_of(base * capacity, group * capacity), group * capacity), :]
        picked = jnp.dot(hot, density_rows, preferred_element_type=jnp.float32).astype(jnp.bfloat16)
        send_rows[pl.ds(base, group)] = picked.reshape(group, capacity, width)
        for k in range(group):
            row_copy(base + k).start()
    base = z * group
    hot = pick_hot[pl.ds(pl.multiple_of(base * capacity, group * capacity), group * capacity), :]
    picked = jnp.dot(hot, density_rows, preferred_element_type=jnp.float32).astype(jnp.bfloat16)
    send_rows[pl.ds(base, group)] = picked.reshape(group, capacity, width)
    for k in range(1, group):
        row_copy(base + (me - base + k) % group).start()
    recv_rows[me] = send_rows[me]
    swap.wait_recv()
    for s in range(BR_DEV):
        column = -(acc[s, mine, :] + half_in[s])
        inv_ref[s, 0] = column[:, :width]
        inv_ref[s, 1] = column[:, width:]
    loads[4].wait()

    @pl.when(corner)
    def _():
        def sent(p):
            for name in corner_sends:
                if name != "last_y":
                    at_corner(name, p).wait_send()
        each(0, pieces, sent)
        each(0, split_at, lambda p: at_corner("last_y", p).wait_send())

    @pl.when(middle)
    def _():
        def sent(p):
            for name in middle_sends:
                if name != "extra":
                    at_middle(name, p).wait_send()
        each(0, pieces, sent)
        each(split_at, pieces, lambda p: at_middle("extra", p).wait_send())

    mix_swap.wait_send()
    swap.wait_send()
    for k in range(1, peers):
        orb_copy(k).wait_send()

    projected = [None] * boxes
    for at_z in range(depth_z):
        if at_z == depth_z - 1:
            for k in range(1, peers):
                row_copy((me + k) % peers).wait_send()
        for origin in range(at_z * group, (at_z + 1) * group):
            @pl.when(me != origin)
            def _(origin=origin):
                dst = recv_rows.at[origin]
                pltpu.make_async_remote_copy(
                    src_ref=dst, dst_ref=dst, send_sem=row_send.at[origin], recv_sem=row_recv.at[origin],
                    device_id={"row": other}, device_id_type=MESH,
                ).wait_recv()
        got = recv_rows[at_z * group:(at_z + 1) * group].reshape(group * capacity, width)
        for n in range(boxes):
            value = lax.dot_general(
                got, basis_hot[n, at_z * group * capacity:(at_z + 1) * group * capacity, :],
                (((0,), (0,)), ((), ())), preferred_element_type=jnp.float32)
            projected[n] = value if at_z == 0 else projected[n] + value
    for n in range(boxes):
        density_ref[n:n + 1, :] = jnp.sum(
            super_buf[n].astype(jnp.float32) * projected[n], axis=0, keepdims=True)


def deliver(column, density, column_out, density_out, sem):
    copies = [
        pltpu.make_async_copy(column, column_out, sem.at[0]),
        pltpu.make_async_copy(density, density_out, sem.at[1]),
    ]
    for copy in copies:
        copy.start()
    for copy in copies:
        copy.wait()


def fused(rows, cols, panel, tiles, tile_slot, tile_col, pole_weight, box_orbitals, box_basis, supernode_basis):
    blocks, parts, shard_rows, width = panel.shape[1:]
    tile_count, _, block, _ = tiles.shape
    boxes, orbs = box_orbitals.shape
    points = box_basis.shape[2]
    half = block // cols
    peers = rows * cols
    capacity = 2 * boxes * orbs // peers
    pieces = blocks // 2
    dma = pltpu.SemaphoreType.DMA
    bf16, f32 = jnp.bfloat16, jnp.float32
    hbm = pl.BlockSpec(memory_space=pl.ANY)
    vmem = pl.BlockSpec(memory_space=pltpu.VMEM)
    column, density = pl.pallas_call(
        functools.partial(kernel, rows, cols),
        name="pole_step",
        out_shape=(
            pltpu.VMEM((BR_DEV, 2, half, width), f32),
            pltpu.VMEM((boxes, points), f32),
        ),
        in_specs=[hbm] * 8,
        out_specs=(vmem, vmem),
        scratch_shapes=[
            pltpu.SMEM(tile_slot.shape, jnp.int32),
            pltpu.SMEM(tile_col.shape, jnp.int32),
            pltpu.SMEM(pole_weight.shape, f32),
        ] + [pltpu.VMEM((2, blocks, parts, shard_rows, width), bf16)] * 4 + [
            pltpu.VMEM(tiles.shape, bf16),
            pltpu.VMEM(box_basis.shape, bf16),
            pltpu.VMEM(supernode_basis.shape, bf16),
            pltpu.VMEM((peers, boxes, orbs), jnp.int32),
            pltpu.VMEM((BR_DEV, block, 2 * width), f32),
            pltpu.VMEM((BR_DEV, half, 2 * width), f32),
            pltpu.VMEM((BR_DEV, half, width), f32),
            pltpu.VMEM((BR_DEV, half, width), f32),
            pltpu.VMEM((BR_DEV, half, width), f32),
            pltpu.VMEM((peers * capacity, BR_DEV * half), bf16),
            pltpu.VMEM((boxes, peers * capacity, points), bf16),
            pltpu.VMEM((boxes, peers, orbs), f32),
            pltpu.VMEM((boxes, peers, orbs), f32),
            pltpu.VMEM((peers, capacity, width), bf16),
            pltpu.VMEM((peers, capacity, width), bf16),
            dma((8,)),
            dma((3, 4, pieces)),
            dma((4, 2, pieces)),
            pltpu.SemaphoreType.REGULAR((2,)),
            dma((2, 2)),
            dma((peers,)),
            dma((peers,)),
            dma((peers,)),
            dma((peers,)),
        ],
        compiler_params=pltpu.CompilerParams(
            collective_id=0, has_side_effects=True, vmem_limit_bytes=56 * 1024 * 1024),
    )(tile_slot, tile_col, pole_weight, panel, tiles, box_orbitals, box_basis, supernode_basis)
    return pl.pallas_call(
        deliver,
        name="deliver",
        out_shape=(
            jax.ShapeDtypeStruct(column.shape, f32),
            jax.ShapeDtypeStruct(density.shape, f32),
        ),
        in_specs=[vmem] * 2,
        out_specs=(hbm, hbm),
        scratch_shapes=[dma((2,))],
        compiler_params=pltpu.CompilerParams(vmem_limit_bytes=8 * 1024 * 1024),
    )(column, density)


def plain(panel, tiles, tile_slot, tile_col, pole_weight, box_orbitals, box_basis, supernode_basis):
    gathered = lax.all_gather(panel, "row", axis=3, tiled=True)
    blocks = gathered[0]
    selector = (tile_col[:, None] == jnp.arange(blocks.shape[0], dtype=jnp.int32)[None, :]).astype(
        jnp.bfloat16
    )
    chosen = jnp.einsum(
        "tj,jcbs->tcbs", selector, blocks, preferred_element_type=jnp.float32
    ).astype(jnp.bfloat16)
    real_part = jnp.einsum(
        "tab,tbs->tas", tiles[:, 0], chosen[:, 0], preferred_element_type=jnp.float32
    )
    real_part = real_part - jnp.einsum(
        "tab,tbs->tas", tiles[:, 1], chosen[:, 1], preferred_element_type=jnp.float32
    )
    imag_part = jnp.einsum(
        "tab,tbs->tas", tiles[:, 0], chosen[:, 1], preferred_element_type=jnp.float32
    )
    imag_part = imag_part + jnp.einsum(
        "tab,tbs->tas", tiles[:, 1], chosen[:, 0], preferred_element_type=jnp.float32
    )
    products = jnp.stack([real_part, imag_part], axis=1)
    partial_value = jnp.stack(
        [
            jnp.sum(jnp.where((tile_slot == slot_row)[:, None, None, None], products, 0.0), axis=0)
            for slot_row in range(BR_DEV)
        ]
    )
    summed = lax.psum_scatter(partial_value, "col", scatter_dimension=2, tiled=True)
    inverse_column = -summed
    density_local = (
        pole_weight[0] * inverse_column[:, 1] + pole_weight[1] * inverse_column[:, 0]
    ).astype(jnp.bfloat16)
    columns = density_local.shape[2]
    density_local = density_local.reshape(-1, columns)
    block_width = tiles.shape[2]
    col_count = lax.axis_size("col")
    half_rows = block_width // col_count
    wanted = box_orbitals.reshape(-1)
    wanted_total = wanted.shape[0]
    block_index = wanted // block_width
    within = wanted % block_width
    source = block_index // BR_DEV * col_count + within // half_rows
    local_row = block_index % BR_DEV * half_rows + within % half_rows
    start_rows = jnp.zeros((wanted_total, columns), jnp.bfloat16)
    shards = lax.all_gather(density_local[None], ("row", "col"), axis=0, tiled=True)
    count = shards.shape[0]
    inside = (source >= 0) & (source < count)
    clipped = jnp.clip(source, 0, count - 1)
    fetched = shards[clipped, local_row]
    picked = jnp.where(inside[:, None], fetched, start_rows)
    picked = picked.reshape(box_basis.shape[0], box_basis.shape[1], columns)
    projected = jnp.einsum("nas,nap->nsp", picked, box_basis, preferred_element_type=jnp.float32)
    density = jnp.sum(supernode_basis.astype(jnp.float32) * projected, axis=1)
    return (inverse_column, density)


def solution(mesh):
    rows, cols = mesh.shape["row"], mesh.shape["col"]

    def local(panel, *rest):
        if cols == 2 and rows == 8 and panel.shape[1] % 8 == 0 and 2 * panel.shape[3] % panel.shape[4] == 0:
            return fused(rows, cols, panel, *rest)
        return plain(panel, *rest)

    return jax.shard_map(
        local,
        mesh=mesh,
        in_specs=(
            P(("pole", "col"), None, None, "row", None),
            P(("pole", "row", "col"), None, None, None),
            P(("pole", "row", "col")),
            P(("pole", "row", "col")),
            P("pole"),
            P(("pole", "row", "col"), None),
            P(("pole", "row", "col"), None, None),
            P(("pole", "row", "col"), None, None),
        ),
        out_specs=(P(("pole", "row"), None, "col", None), P(("pole", "row", "col"), None)),
        check_vma=False,
    )
```

```python
import functools

import jax
import jax.numpy as jnp
from jax import lax
from jax.experimental import pallas as pl
from jax.experimental.pallas import tpu as pltpu
from jax.sharding import PartitionSpec as P

BR_DEV = 2
MESH = pl.DeviceIdType.MESH


def log2(value):
    assert value & (value - 1) == 0
    return value.bit_length() - 1


def kernel(
    rows, cols, slots, tile_cols, weights, panel, tiles, orbitals, basis, super_basis,
    inv_ref, density_ref, slot_ref, tcol_ref, weight_ref, own, near, third, last,
    tile_buf, basis_buf, super_buf, orb_buf, acc, half_in, mix_out, mix_own, mix_in, pick_hot, basis_hot, order_buf, local_buf,
    send_rows, recv_rows, local_sem, send_sem, recv_sem, token, col_sem, orb_send, orb_recv, row_send, row_recv,
):
    lanes_y = 2
    depth_z = rows // lanes_y
    peers = rows * cols
    r = lax.axis_index("row")
    c = lax.axis_index("col")
    me = r * cols + c
    z = r // lanes_y
    y = r % lanes_y
    shard_rows = panel.shape[3]
    width = panel.shape[4]
    pieces = recv_sem.shape[2]
    step = panel.shape[1] // pieces
    split_at = pieces // 2
    tile_count = tiles.shape[0]
    block = tiles.shape[2]
    half = block // cols
    pair = lanes_y * shard_rows
    boxes, orbs = orbitals.shape
    capacity = send_rows.shape[1]

    inner = 1 - 2 * (z // (depth_z // 2))
    corner = jnp.logical_or(z == 0, z == depth_z - 1)
    middle = jnp.logical_not(corner)
    other = r + 1 - 2 * y
    inward = r + lanes_y * inner
    outward = r - lanes_y * inner
    buffers = (own, near, third, last)
    places = (
        z,
        z + inner,
        jnp.where(corner, z + 2 * inner, z - inner),
        jnp.where(corner, z + 3 * inner, z + 2 * inner),
    )
    IN, OUT, Y = 0, 1, 2

    def spot(index):
        return {"row": index // cols, "col": index % cols}

    loads = [
        pltpu.make_async_copy(panel.at[0], own.at[y], local_sem.at[0]),
        pltpu.make_async_copy(orbitals, orb_buf.at[c, r], local_sem.at[4]),
        pltpu.make_async_copy(basis, basis_buf, local_sem.at[2]),
        pltpu.make_async_copy(tiles, tile_buf, local_sem.at[1]),
        pltpu.make_async_copy(super_basis, super_buf, local_sem.at[3]),
        pltpu.make_async_copy(slots, slot_ref, local_sem.at[5]),
        pltpu.make_async_copy(tile_cols, tcol_ref, local_sem.at[6]),
        pltpu.make_async_copy(weights, weight_ref, local_sem.at[7]),
    ]
    barrier = pltpu.get_barrier_semaphore()
    for device in (
        {"row": other}, {"col": 1 - c}, {"row": other, "col": 1 - c}, {"row": inward},
    ):
        pl.semaphore_signal(barrier, inc=1, device_id=device, device_id_type=MESH)

    @pl.when(middle)
    def _():
        pl.semaphore_signal(barrier, inc=1, device_id={"row": outward}, device_id_type=MESH)

    for load in loads[:3]:
        load.start()

    @pl.when(middle)
    def _():
        pl.semaphore_wait(barrier, 5)

    @pl.when(corner)
    def _():
        pl.semaphore_wait(barrier, 4)

    loads[0].wait()

    def piece(which, lane, p):
        return buffers[which].at[lane, pl.ds(p * step, step)]

    def copy(link, kind, source, target, lane, p):
        row = (inward, outward, other)[link]
        return pltpu.make_async_remote_copy(
            src_ref=piece(source, lane, p), dst_ref=piece(target, lane, p),
            send_sem=send_sem.at[link, kind, p], recv_sem=recv_sem.at[target, lane, p],
            device_id={"row": row}, device_id_type=MESH,
        )

    def arrived(target, lane, p):
        dst = piece(target, lane, p)
        pltpu.make_async_remote_copy(
            src_ref=dst, dst_ref=dst, send_sem=send_sem.at[0, 0, p], recv_sem=recv_sem.at[target, lane, p],
            device_id={"row": other}, device_id_type=MESH,
        ).wait_recv()

    def each(low, high, body):
        def run(h, carry):
            body(h)
            return carry
        lax.fori_loop(low, high, run, 0)

    corner_sends = {
        "own_in": (IN, 0, 0, 2, y), "own_y": (Y, 0, 0, 0, y),
        "extra": (IN, 1, 0, 2, 1 - y),
        "near_y": (Y, 1, 1, 1, y), "third_y": (Y, 2, 2, 2, y), "last_y": (Y, 3, 3, 3, y),
    }
    middle_sends = {
        "own_out": (OUT, 0, 0, 1, y), "own_in": (IN, 0, 0, 1, y), "own_y": (Y, 0, 0, 0, y),
        "third_in": (IN, 1, 2, 3, y),
        "near_out": (OUT, 1, 1, 2, y), "near_y": (Y, 1, 1, 1, y),
        "last_out": (OUT, 2, 3, 3, y), "last_y": (Y, 2, 3, 3, y),
        "extra": (OUT, 3, 3, 3, 1 - y),
    }

    def at_corner(name, p):
        return copy(*corner_sends[name], p)

    def at_middle(name, p):
        return copy(*middle_sends[name], p)

    @pl.when(corner)
    def _():
        def go(p):
            at_corner("own_in", p).start()
            at_corner("own_y", p).start()
        each(0, pieces, go)

    @pl.when(middle)
    def _():
        def go(p):
            at_middle("own_out", p).start()
            at_middle("own_in", p).start()
            at_middle("own_y", p).start()
        each(0, pieces, go)

    for load in loads[3:]:
        load.start()
    acc[...] = jnp.zeros_like(acc)
    block_bits, half_bits = log2(block), log2(half)

    def split(g):
        row_block = g >> block_bits
        within = g & (block - 1)
        source = (row_block >> log2(BR_DEV)) * cols + (within >> half_bits)
        local = (row_block & (BR_DEV - 1)) * half + (within & (half - 1))
        return source, local

    def ranks(masks):
        before = lax.broadcasted_iota(jnp.int32, (orbs, orbs), 0)
        after = lax.broadcasted_iota(jnp.int32, (orbs, orbs), 1)
        upper = jnp.where(before <= after, 1.0, 0.0).astype(jnp.bfloat16)
        seen = jnp.zeros((masks[0].shape[0], 1), jnp.float32)
        result = []
        for mask in masks:
            counted = jnp.dot(mask.astype(jnp.bfloat16), upper, preferred_element_type=jnp.float32)
            result.append(counted - 1.0 + seen)
            seen = seen + jnp.sum(mask, axis=1, keepdims=True)
        return result

    def place_basis():
        loads[1].wait()
        loads[2].wait()
        masks = []
        peer_id = lax.broadcasted_iota(jnp.int32, (peers, orbs), 0)
        for n in range(boxes):
            source, _ = split(orb_buf[c, r, n:n + 1, :])
            masks.append(jnp.where(peer_id == source, 1.0, 0.0))
        order = ranks(masks)
        arrive = lax.broadcasted_iota(jnp.int32, (peers * capacity, orbs), 0).astype(jnp.float32)
        for n in range(boxes):
            position = jnp.sum(
                masks[n] * (order[n] + (peer_id * capacity).astype(jnp.float32)), axis=0, keepdims=True)
            hot = jnp.where(arrive == position, 1.0, 0.0).astype(jnp.bfloat16)
            basis_hot[n] = jnp.dot(hot, basis_buf[n], preferred_element_type=jnp.float32).astype(jnp.bfloat16)

    def orb_copy(k):
        return pltpu.make_async_remote_copy(
            src_ref=orbitals, dst_ref=orb_buf.at[c, r], send_sem=orb_send.at[k], recv_sem=orb_recv.at[k],
            device_id={"row": (r + k) % rows}, device_id_type=MESH,
        )

    def orb_block(col):
        return pltpu.make_async_remote_copy(
            src_ref=orb_buf.at[col], dst_ref=orb_buf.at[col], send_sem=orb_send.at[0], recv_sem=orb_recv.at[0],
            device_id={"col": 1 - c}, device_id_type=MESH,
        )

    def pass_orbitals():
        for k in range(1, rows):
            dst = orb_buf.at[c, (r + rows - k) % rows]
            pltpu.make_async_remote_copy(
                src_ref=dst, dst_ref=dst, send_sem=orb_send.at[k], recv_sem=orb_recv.at[k],
                device_id={"row": other}, device_id_type=MESH,
            ).wait_recv()
        orb_block(c).start()

    def rank_orbitals():
        orb_block(1 - c).wait_recv()
        asked = []
        for n in range(boxes):
            g = jnp.concatenate([orb_buf[q % cols, q // cols, n:n + 1, :] for q in range(peers)], axis=0)
            source, local = split(g)
            asked.append((jnp.where(source == me, 1.0, 0.0), local.astype(jnp.float32)))
        order = ranks([a[0] for a in asked])
        for n in range(boxes):
            order_buf[n] = jnp.where(asked[n][0] > 0.5, order[n], -1.0)
            local_buf[n] = asked[n][1] + 1.0

    def place_picks(q):
        place = lax.broadcasted_iota(jnp.int32, (capacity, orbs), 0).astype(jnp.float32)
        row_id = lax.broadcasted_iota(jnp.int32, (capacity, BR_DEV * half), 1).astype(jnp.float32)
        found = jnp.zeros((capacity, 1), jnp.float32)
        for n in range(boxes):
            hit = place == order_buf[n, pl.ds(q, 1), :]
            found = found + jnp.sum(jnp.where(hit, local_buf[n, pl.ds(q, 1), :], 0.0), axis=1, keepdims=True)
        spot_rows = pl.ds(pl.multiple_of(q * capacity, capacity), capacity)
        pick_hot[spot_rows, :] = jnp.where(row_id == found - 1.0, 1.0, 0.0).astype(jnp.bfloat16)

    def product(which, t, out_rows):
        j = tcol_ref[t]
        offset = pl.multiple_of(places[which] * pair, pair)
        left = jnp.concatenate(
            [tile_buf[t, 0, out_rows, pl.ds(offset, pair)], tile_buf[t, 1, out_rows, pl.ds(offset, pair)]], axis=1)
        parts = [buffers[which][k, j] for k in range(lanes_y)]
        real = jnp.concatenate([p[0] for p in parts], axis=0)
        imag = jnp.concatenate([p[1] for p in parts], axis=0)
        right = jnp.concatenate(
            [jnp.concatenate([real, imag], axis=1), jnp.concatenate([-imag, real], axis=1)], axis=0)
        return jnp.dot(left, right, preferred_element_type=jnp.float32)

    def several(which, start, count, out_rows):
        values = [product(which, start + k, out_rows) for k in range(count)]
        for s in range(BR_DEV):
            total = jnp.where(slot_ref[start] == s, values[0], 0.0)
            for k in range(1, count):
                total = total + jnp.where(slot_ref[start + k] == s, values[k], 0.0)
            acc[s, out_rows, :] += total

    everything = pl.ds(0, block)

    def share(which, p, parts):
        first_tile, last_tile = p * tile_count // parts, (p + 1) * tile_count // parts
        for start in range(first_tile, last_tile, 4):
            several(which, start, min(4, last_tile - start), everything)

    place_basis()

    def first(p):
        @pl.when(corner)
        def _():
            arrived(1, y, p)
            at_corner("near_y", p).start()
            arrived(0, 1 - y, p)
            at_corner("extra", p).start()

        @pl.when(middle)
        def _():
            arrived(2, y, p)
            at_middle("third_in", p).start()
            arrived(1, y, p)
            at_middle("near_out", p).start()
            at_middle("near_y", p).start()

            @pl.when(p == 0)
            def _():
                pl.semaphore_signal(token.at[0], inc=1, device_id={"row": inward}, device_id_type=MESH)

            @pl.when(p == pieces - 1)
            def _():
                pl.semaphore_wait(token.at[0], 1)
                pl.semaphore_signal(token.at[1], inc=1, device_id={"row": outward}, device_id_type=MESH)

    each(0, pieces, first)

    @pl.when(corner)
    def _():
        pl.semaphore_wait(token.at[1], 1)

    for k in range(1, rows):
        orb_copy(k).start()

    @pl.when(middle)
    def _():
        each(0, pieces, lambda p: arrived(0, 1 - y, p))

    loads[3].wait()
    for load in loads[5:]:
        load.wait()

    def second(p):
        @pl.when(corner)
        def _():
            arrived(2, y, p)
            at_corner("third_y", p).start()

        @pl.when(middle)
        def _():
            arrived(3, y, p)
            at_middle("last_out", p).start()
            if p >= split_at:
                at_middle("last_y", p).start()

        share(0, p, pieces)

    for p in range(pieces):
        second(p)

    @pl.when(middle)
    def _():
        each(0, split_at, lambda p: at_middle("last_y", p).start())

    each(0, pieces, lambda p: arrived(1, 1 - y, p))

    def closing(p):
        share(1, p, split_at)

        @pl.when(corner)
        def _():
            arrived(3, y, p)
            at_corner("last_y", p).start()

        @pl.when(middle)
        def _():
            arrived(3, 1 - y, p + split_at)
            at_middle("extra", p + split_at).start()

    for p in range(split_at):
        closing(p)
    pass_orbitals()

    @pl.when(middle)
    def _():
        each(0, pieces, lambda p: arrived(2, 1 - y, p))
        share(2, 0, 1)

    rank_orbitals()
    each(0, peers // 4, lambda q: [place_picks(4 * q + k) for k in range(4)])

    @pl.when(corner)
    def _():
        each(0, pieces, lambda p: arrived(2, 1 - y, p))
        share(2, 0, 1)


    @pl.when(corner)
    def _():
        each(split_at, pieces, lambda p: arrived(3, y, p))
        each(split_at, pieces, lambda p: arrived(3, 1 - y, p))
    each(0, split_at, lambda p: arrived(3, 1 - y, p))

    mine = pl.ds(pl.multiple_of(c * half, half), half)
    theirs = pl.ds(pl.multiple_of((1 - c) * half, half), half)

    def to_partner(which, src, dst):
        return pltpu.make_async_remote_copy(
            src_ref=src, dst_ref=dst, send_sem=col_sem.at[0, which], recv_sem=col_sem.at[1, which],
            device_id={"col": 1 - c}, device_id_type=MESH,
        )

    mix_swap = to_partner(0, mix_out, mix_in)
    swap = to_partner(1, acc.at[:, theirs, :], half_in)

    def mixed(s, out_rows):
        return weight_ref[0] * acc[s, out_rows, width:] + weight_ref[1] * acc[s, out_rows, :width]

    for start in range(0, tile_count, 4):
        several(3, start, min(4, tile_count - start), theirs)
    for s in range(BR_DEV):
        mix_out[s] = mixed(s, theirs)
    mix_swap.start()
    swap.start()
    for start in range(0, tile_count, 4):
        several(3, start, min(4, tile_count - start), mine)
    for s in range(BR_DEV):
        mix_own[s] = mixed(s, mine)
    mix_swap.wait_recv()
    density_rows = [(-(mix_own[s] + mix_in[s])).astype(jnp.bfloat16) for s in range(BR_DEV)]
    density_rows = jnp.concatenate(density_rows, axis=0)

    group = lanes_y * cols

    def row_copy(target):
        return pltpu.make_async_remote_copy(
            src_ref=send_rows.at[target], dst_ref=recv_rows.at[me],
            send_sem=row_send.at[target], recv_sem=row_recv.at[me],
            device_id=spot(target), device_id_type=MESH,
        )

    for k in range(depth_z - 1):
        at_z = k + jnp.where(k >= z, 1, 0)
        base = at_z * group
        hot = pick_hot[pl.ds(pl.multiple_of(base * capacity, group * capacity), group * capacity), :]
        picked = jnp.dot(hot, density_rows, preferred_element_type=jnp.float32).astype(jnp.bfloat16)
        send_rows[pl.ds(base, group)] = picked.reshape(group, capacity, width)
        for lane in range(group):
            row_copy(base + lane).start()
    base = z * group
    hot = pick_hot[pl.ds(pl.multiple_of(base * capacity, group * capacity), group * capacity), :]
    picked = jnp.dot(hot, density_rows, preferred_element_type=jnp.float32).astype(jnp.bfloat16)
    send_rows[pl.ds(base, group)] = picked.reshape(group, capacity, width)
    for k in range(1, group):
        row_copy(base + (me - base + k) % group).start()
    recv_rows[me] = send_rows[me]
    swap.wait_recv()
    for s in range(BR_DEV):
        column = -(acc[s, mine, :] + half_in[s])
        inv_ref[s, 0] = column[:, :width]
        inv_ref[s, 1] = column[:, width:]
    loads[4].wait()

    @pl.when(corner)
    def _():
        def sent(p):
            for name in corner_sends:
                if name != "last_y":
                    at_corner(name, p).wait_send()
        each(0, pieces, sent)
        each(0, split_at, lambda p: at_corner("last_y", p).wait_send())

    @pl.when(middle)
    def _():
        def sent(p):
            for name in middle_sends:
                if name != "extra":
                    at_middle(name, p).wait_send()
        each(0, pieces, sent)
        each(split_at, pieces, lambda p: at_middle("extra", p).wait_send())

    mix_swap.wait_send()
    swap.wait_send()
    for k in range(1, rows):
        orb_copy(k).wait_send()
    orb_block(c).wait_send()

    projected = [None] * boxes
    for at_z in range(depth_z):
        if at_z == depth_z - 1:
            for k in range(1, peers):
                row_copy((me + k) % peers).wait_send()
        for origin in range(at_z * group, (at_z + 1) * group):
            @pl.when(me != origin)
            def _(origin=origin):
                dst = recv_rows.at[origin]
                pltpu.make_async_remote_copy(
                    src_ref=dst, dst_ref=dst, send_sem=row_send.at[origin], recv_sem=row_recv.at[origin],
                    device_id={"row": other}, device_id_type=MESH,
                ).wait_recv()
        got = recv_rows[at_z * group:(at_z + 1) * group].reshape(group * capacity, width)
        for n in range(boxes):
            value = lax.dot_general(
                got, basis_hot[n, at_z * group * capacity:(at_z + 1) * group * capacity, :],
                (((0,), (0,)), ((), ())), preferred_element_type=jnp.float32)
            projected[n] = value if at_z == 0 else projected[n] + value
    for n in range(boxes):
        density_ref[n:n + 1, :] = jnp.sum(
            super_buf[n].astype(jnp.float32) * projected[n], axis=0, keepdims=True)


def deliver(column, density, column_out, density_out, sem):
    copies = [
        pltpu.make_async_copy(column, column_out, sem.at[0]),
        pltpu.make_async_copy(density, density_out, sem.at[1]),
    ]
    for copy in copies:
        copy.start()
    for copy in copies:
        copy.wait()


def fused(rows, cols, panel, tiles, tile_slot, tile_col, pole_weight, box_orbitals, box_basis, supernode_basis):
    blocks, parts, shard_rows, width = panel.shape[1:]
    tile_count, _, block, _ = tiles.shape
    boxes, orbs = box_orbitals.shape
    points = box_basis.shape[2]
    half = block // cols
    peers = rows * cols
    capacity = 2 * boxes * orbs // peers
    pieces = blocks // 2
    dma = pltpu.SemaphoreType.DMA
    bf16, f32 = jnp.bfloat16, jnp.float32
    hbm = pl.BlockSpec(memory_space=pl.ANY)
    vmem = pl.BlockSpec(memory_space=pltpu.VMEM)
    column, density = pl.pallas_call(
        functools.partial(kernel, rows, cols),
        name="pole_step",
        out_shape=(
            pltpu.VMEM((BR_DEV, 2, half, width), f32),
            pltpu.VMEM((boxes, points), f32),
        ),
        in_specs=[hbm] * 8,
        out_specs=(vmem, vmem),
        scratch_shapes=[
            pltpu.SMEM(tile_slot.shape, jnp.int32),
            pltpu.SMEM(tile_col.shape, jnp.int32),
            pltpu.SMEM(pole_weight.shape, f32),
        ] + [pltpu.VMEM((2, blocks, parts, shard_rows, width), bf16)] * 4 + [
            pltpu.VMEM(tiles.shape, bf16),
            pltpu.VMEM(box_basis.shape, bf16),
            pltpu.VMEM(supernode_basis.shape, bf16),
            pltpu.VMEM((cols, rows, boxes, orbs), jnp.int32),
            pltpu.VMEM((BR_DEV, block, 2 * width), f32),
            pltpu.VMEM((BR_DEV, half, 2 * width), f32),
            pltpu.VMEM((BR_DEV, half, width), f32),
            pltpu.VMEM((BR_DEV, half, width), f32),
            pltpu.VMEM((BR_DEV, half, width), f32),
            pltpu.VMEM((peers * capacity, BR_DEV * half), bf16),
            pltpu.VMEM((boxes, peers * capacity, points), bf16),
            pltpu.VMEM((boxes, peers, orbs), f32),
            pltpu.VMEM((boxes, peers, orbs), f32),
            pltpu.VMEM((peers, capacity, width), bf16),
            pltpu.VMEM((peers, capacity, width), bf16),
            dma((8,)),
            dma((3, 4, pieces)),
            dma((4, 2, pieces)),
            pltpu.SemaphoreType.REGULAR((2,)),
            dma((2, 2)),
            dma((peers,)),
            dma((peers,)),
            dma((peers,)),
            dma((peers,)),
        ],
        compiler_params=pltpu.CompilerParams(
            collective_id=0, has_side_effects=True, vmem_limit_bytes=56 * 1024 * 1024),
    )(tile_slot, tile_col, pole_weight, panel, tiles, box_orbitals, box_basis, supernode_basis)
    return pl.pallas_call(
        deliver,
        name="deliver",
        out_shape=(
            jax.ShapeDtypeStruct(column.shape, f32),
            jax.ShapeDtypeStruct(density.shape, f32),
        ),
        in_specs=[vmem] * 2,
        out_specs=(hbm, hbm),
        scratch_shapes=[dma((2,))],
        compiler_params=pltpu.CompilerParams(vmem_limit_bytes=8 * 1024 * 1024),
    )(column, density)


def plain(panel, tiles, tile_slot, tile_col, pole_weight, box_orbitals, box_basis, supernode_basis):
    gathered = lax.all_gather(panel, "row", axis=3, tiled=True)
    blocks = gathered[0]
    selector = (tile_col[:, None] == jnp.arange(blocks.shape[0], dtype=jnp.int32)[None, :]).astype(
        jnp.bfloat16
    )
    chosen = jnp.einsum(
        "tj,jcbs->tcbs", selector, blocks, preferred_element_type=jnp.float32
    ).astype(jnp.bfloat16)
    real_part = jnp.einsum(
        "tab,tbs->tas", tiles[:, 0], chosen[:, 0], preferred_element_type=jnp.float32
    )
    real_part = real_part - jnp.einsum(
        "tab,tbs->tas", tiles[:, 1], chosen[:, 1], preferred_element_type=jnp.float32
    )
    imag_part = jnp.einsum(
        "tab,tbs->tas", tiles[:, 0], chosen[:, 1], preferred_element_type=jnp.float32
    )
    imag_part = imag_part + jnp.einsum(
        "tab,tbs->tas", tiles[:, 1], chosen[:, 0], preferred_element_type=jnp.float32
    )
    products = jnp.stack([real_part, imag_part], axis=1)
    partial_value = jnp.stack(
        [
            jnp.sum(jnp.where((tile_slot == slot_row)[:, None, None, None], products, 0.0), axis=0)
            for slot_row in range(BR_DEV)
        ]
    )
    summed = lax.psum_scatter(partial_value, "col", scatter_dimension=2, tiled=True)
    inverse_column = -summed
    density_local = (
        pole_weight[0] * inverse_column[:, 1] + pole_weight[1] * inverse_column[:, 0]
    ).astype(jnp.bfloat16)
    columns = density_local.shape[2]
    density_local = density_local.reshape(-1, columns)
    block_width = tiles.shape[2]
    col_count = lax.axis_size("col")
    half_rows = block_width // col_count
    wanted = box_orbitals.reshape(-1)
    wanted_total = wanted.shape[0]
    block_index = wanted // block_width
    within = wanted % block_width
    source = block_index // BR_DEV * col_count + within // half_rows
    local_row = block_index % BR_DEV * half_rows + within % half_rows
    start_rows = jnp.zeros((wanted_total, columns), jnp.bfloat16)
    shards = lax.all_gather(density_local[None], ("row", "col"), axis=0, tiled=True)
    count = shards.shape[0]
    inside = (source >= 0) & (source < count)
    clipped = jnp.clip(source, 0, count - 1)
    fetched = shards[clipped, local_row]
    picked = jnp.where(inside[:, None], fetched, start_rows)
    picked = picked.reshape(box_basis.shape[0], box_basis.shape[1], columns)
    projected = jnp.einsum("nas,nap->nsp", picked, box_basis, preferred_element_type=jnp.float32)
    density = jnp.sum(supernode_basis.astype(jnp.float32) * projected, axis=1)
    return (inverse_column, density)


def solution(mesh):
    rows, cols = mesh.shape["row"], mesh.shape["col"]

    def local(panel, *rest):
        if cols == 2 and rows == 8 and panel.shape[1] % 8 == 0 and 2 * panel.shape[3] % panel.shape[4] == 0:
            return fused(rows, cols, panel, *rest)
        return plain(panel, *rest)

    return jax.shard_map(
        local,
        mesh=mesh,
        in_specs=(
            P(("pole", "col"), None, None, "row", None),
            P(("pole", "row", "col"), None, None, None),
            P(("pole", "row", "col")),
            P(("pole", "row", "col")),
            P("pole"),
            P(("pole", "row", "col"), None),
            P(("pole", "row", "col"), None, None),
            P(("pole", "row", "col"), None, None),
        ),
        out_specs=(P(("pole", "row"), None, "col", None), P(("pole", "row", "col"), None)),
        check_vma=False,
    )
```

```python
import functools

import jax
import jax.numpy as jnp
from jax import lax
from jax.experimental import pallas as pl
from jax.experimental.pallas import tpu as pltpu
from jax.sharding import PartitionSpec as P

BR_DEV = 2
MESH = pl.DeviceIdType.MESH


def log2(value):
    assert value & (value - 1) == 0
    return value.bit_length() - 1


def kernel(
    rows, cols, slots, tile_cols, weights, panel, tiles, orbitals, basis, super_basis,
    inv_ref, projected_ref, late_rows, late_basis, super_buf, slot_ref, tcol_ref, weight_ref, own, near, third, last,
    tile_buf, basis_buf, orb_buf, acc, half_in, mix_out, mix_own, mix_in, pick_hot, basis_hot, order_buf, local_buf,
    send_rows, recv_rows, local_sem, send_sem, recv_sem, token, col_sem, orb_send, orb_recv, row_send, row_recv,
):
    lanes_y = 2
    depth_z = rows // lanes_y
    peers = rows * cols
    r = lax.axis_index("row")
    c = lax.axis_index("col")
    me = r * cols + c
    z = r // lanes_y
    y = r % lanes_y
    shard_rows = panel.shape[3]
    width = panel.shape[4]
    pieces = recv_sem.shape[2]
    step = panel.shape[1] // pieces
    split_at = pieces // 2
    tile_count = tiles.shape[0]
    block = tiles.shape[2]
    half = block // cols
    pair = lanes_y * shard_rows
    boxes, orbs = orbitals.shape
    capacity = send_rows.shape[1]

    inner = 1 - 2 * (z // (depth_z // 2))
    corner = jnp.logical_or(z == 0, z == depth_z - 1)
    middle = jnp.logical_not(corner)
    other = r + 1 - 2 * y
    inward = r + lanes_y * inner
    outward = r - lanes_y * inner
    buffers = (own, near, third, last)
    places = (
        z,
        z + inner,
        jnp.where(corner, z + 2 * inner, z - inner),
        jnp.where(corner, z + 3 * inner, z + 2 * inner),
    )
    IN, OUT, Y = 0, 1, 2

    def spot(index):
        return {"row": index // cols, "col": index % cols}

    loads = [
        pltpu.make_async_copy(panel.at[0], own.at[y], local_sem.at[0]),
        pltpu.make_async_copy(orbitals, orb_buf.at[c, r], local_sem.at[4]),
        pltpu.make_async_copy(basis, basis_buf, local_sem.at[2]),
        pltpu.make_async_copy(tiles, tile_buf, local_sem.at[1]),
        pltpu.make_async_copy(super_basis, super_buf, local_sem.at[3]),
        pltpu.make_async_copy(slots, slot_ref, local_sem.at[5]),
        pltpu.make_async_copy(tile_cols, tcol_ref, local_sem.at[6]),
        pltpu.make_async_copy(weights, weight_ref, local_sem.at[7]),
    ]
    barrier = pltpu.get_barrier_semaphore()
    for device in (
        {"row": other}, {"col": 1 - c}, {"row": other, "col": 1 - c}, {"row": inward},
    ):
        pl.semaphore_signal(barrier, inc=1, device_id=device, device_id_type=MESH)

    @pl.when(middle)
    def _():
        pl.semaphore_signal(barrier, inc=1, device_id={"row": outward}, device_id_type=MESH)

    for load in loads[:3]:
        load.start()

    @pl.when(middle)
    def _():
        pl.semaphore_wait(barrier, 5)

    @pl.when(corner)
    def _():
        pl.semaphore_wait(barrier, 4)

    loads[0].wait()

    def piece(which, lane, p):
        return buffers[which].at[lane, pl.ds(p * step, step)]

    def copy(link, kind, source, target, lane, p):
        row = (inward, outward, other)[link]
        return pltpu.make_async_remote_copy(
            src_ref=piece(source, lane, p), dst_ref=piece(target, lane, p),
            send_sem=send_sem.at[link, kind, p], recv_sem=recv_sem.at[target, lane, p],
            device_id={"row": row}, device_id_type=MESH,
        )

    def arrived(target, lane, p):
        dst = piece(target, lane, p)
        pltpu.make_async_remote_copy(
            src_ref=dst, dst_ref=dst, send_sem=send_sem.at[0, 0, p], recv_sem=recv_sem.at[target, lane, p],
            device_id={"row": other}, device_id_type=MESH,
        ).wait_recv()

    def each(low, high, body):
        def run(h, carry):
            body(h)
            return carry
        lax.fori_loop(low, high, run, 0)

    corner_sends = {
        "own_in": (IN, 0, 0, 2, y), "own_y": (Y, 0, 0, 0, y),
        "extra": (IN, 1, 0, 2, 1 - y),
        "near_y": (Y, 1, 1, 1, y), "third_y": (Y, 2, 2, 2, y), "last_y": (Y, 3, 3, 3, y),
    }
    middle_sends = {
        "own_out": (OUT, 0, 0, 1, y), "own_in": (IN, 0, 0, 1, y), "own_y": (Y, 0, 0, 0, y),
        "third_in": (IN, 1, 2, 3, y),
        "near_out": (OUT, 1, 1, 2, y), "near_y": (Y, 1, 1, 1, y),
        "last_out": (OUT, 2, 3, 3, y), "last_y": (Y, 2, 3, 3, y),
        "extra": (OUT, 3, 3, 3, 1 - y),
    }

    def at_corner(name, p):
        return copy(*corner_sends[name], p)

    def at_middle(name, p):
        return copy(*middle_sends[name], p)

    @pl.when(corner)
    def _():
        def go(p):
            at_corner("own_in", p).start()
            at_corner("own_y", p).start()
        each(0, pieces, go)

    @pl.when(middle)
    def _():
        def go(p):
            at_middle("own_out", p).start()
            at_middle("own_in", p).start()
            at_middle("own_y", p).start()
        each(0, pieces, go)

    for load in loads[3:]:
        load.start()
    acc[...] = jnp.zeros_like(acc)
    block_bits, half_bits = log2(block), log2(half)

    def split(g):
        row_block = g >> block_bits
        within = g & (block - 1)
        source = (row_block >> log2(BR_DEV)) * cols + (within >> half_bits)
        local = (row_block & (BR_DEV - 1)) * half + (within & (half - 1))
        return source, local

    def ranks(masks):
        before = lax.broadcasted_iota(jnp.int32, (orbs, orbs), 0)
        after = lax.broadcasted_iota(jnp.int32, (orbs, orbs), 1)
        upper = jnp.where(before <= after, 1.0, 0.0).astype(jnp.bfloat16)
        seen = jnp.zeros((masks[0].shape[0], 1), jnp.float32)
        result = []
        for mask in masks:
            counted = jnp.dot(mask.astype(jnp.bfloat16), upper, preferred_element_type=jnp.float32)
            result.append(counted - 1.0 + seen)
            seen = seen + jnp.sum(mask, axis=1, keepdims=True)
        return result

    def place_basis():
        loads[1].wait()
        loads[2].wait()
        masks = []
        peer_id = lax.broadcasted_iota(jnp.int32, (peers, orbs), 0)
        for n in range(boxes):
            source, _ = split(orb_buf[c, r, n:n + 1, :])
            masks.append(jnp.where(peer_id == source, 1.0, 0.0))
        order = ranks(masks)
        arrive = lax.broadcasted_iota(jnp.int32, (peers * capacity, orbs), 0).astype(jnp.float32)
        for n in range(boxes):
            position = jnp.sum(
                masks[n] * (order[n] + (peer_id * capacity).astype(jnp.float32)), axis=0, keepdims=True)
            hot = jnp.where(arrive == position, 1.0, 0.0).astype(jnp.bfloat16)
            placed = jnp.dot(hot, basis_buf[n], preferred_element_type=jnp.float32).astype(jnp.bfloat16)
            early = basis_hot.shape[1]
            basis_hot[n] = placed[:early]
            late_basis[n] = placed[early:]

    def orb_copy(k):
        return pltpu.make_async_remote_copy(
            src_ref=orbitals, dst_ref=orb_buf.at[c, r], send_sem=orb_send.at[k], recv_sem=orb_recv.at[k],
            device_id={"row": (r + k) % rows}, device_id_type=MESH,
        )

    def orb_block(col):
        return pltpu.make_async_remote_copy(
            src_ref=orb_buf.at[col], dst_ref=orb_buf.at[col], send_sem=orb_send.at[0], recv_sem=orb_recv.at[0],
            device_id={"col": 1 - c}, device_id_type=MESH,
        )

    def pass_orbitals():
        for k in range(1, rows):
            dst = orb_buf.at[c, (r + rows - k) % rows]
            pltpu.make_async_remote_copy(
                src_ref=dst, dst_ref=dst, send_sem=orb_send.at[k], recv_sem=orb_recv.at[k],
                device_id={"row": other}, device_id_type=MESH,
            ).wait_recv()
        orb_block(c).start()

    def rank_orbitals():
        orb_block(1 - c).wait_recv()
        asked = []
        for n in range(boxes):
            g = jnp.concatenate([orb_buf[q % cols, q // cols, n:n + 1, :] for q in range(peers)], axis=0)
            source, local = split(g)
            asked.append((jnp.where(source == me, 1.0, 0.0), local.astype(jnp.float32)))
        order = ranks([a[0] for a in asked])
        for n in range(boxes):
            order_buf[n] = jnp.where(asked[n][0] > 0.5, order[n], -1.0)
            local_buf[n] = asked[n][1] + 1.0

    def place_picks(q):
        place = lax.broadcasted_iota(jnp.int32, (capacity, orbs), 0).astype(jnp.float32)
        row_id = lax.broadcasted_iota(jnp.int32, (capacity, BR_DEV * half), 1).astype(jnp.float32)
        found = jnp.zeros((capacity, 1), jnp.float32)
        for n in range(boxes):
            hit = place == order_buf[n, pl.ds(q, 1), :]
            found = found + jnp.sum(jnp.where(hit, local_buf[n, pl.ds(q, 1), :], 0.0), axis=1, keepdims=True)
        spot_rows = pl.ds(pl.multiple_of(q * capacity, capacity), capacity)
        pick_hot[spot_rows, :] = jnp.where(row_id == found - 1.0, 1.0, 0.0).astype(jnp.bfloat16)

    def product(which, t, out_rows):
        j = tcol_ref[t]
        offset = pl.multiple_of(places[which] * pair, pair)
        left = jnp.concatenate(
            [tile_buf[t, 0, out_rows, pl.ds(offset, pair)], tile_buf[t, 1, out_rows, pl.ds(offset, pair)]], axis=1)
        parts = [buffers[which][k, j] for k in range(lanes_y)]
        real = jnp.concatenate([p[0] for p in parts], axis=0)
        imag = jnp.concatenate([p[1] for p in parts], axis=0)
        right = jnp.concatenate(
            [jnp.concatenate([real, imag], axis=1), jnp.concatenate([-imag, real], axis=1)], axis=0)
        return jnp.dot(left, right, preferred_element_type=jnp.float32)

    def several(which, start, count, out_rows):
        values = [product(which, start + k, out_rows) for k in range(count)]
        for s in range(BR_DEV):
            total = jnp.where(slot_ref[start] == s, values[0], 0.0)
            for k in range(1, count):
                total = total + jnp.where(slot_ref[start + k] == s, values[k], 0.0)
            acc[s, out_rows, :] += total

    everything = pl.ds(0, block)

    def share(which, p, parts):
        first_tile, last_tile = p * tile_count // parts, (p + 1) * tile_count // parts
        for start in range(first_tile, last_tile, 4):
            several(which, start, min(4, last_tile - start), everything)

    place_basis()

    def first(p):
        @pl.when(corner)
        def _():
            arrived(1, y, p)
            at_corner("near_y", p).start()
            arrived(0, 1 - y, p)
            at_corner("extra", p).start()

        @pl.when(middle)
        def _():
            arrived(2, y, p)
            at_middle("third_in", p).start()
            arrived(1, y, p)
            at_middle("near_out", p).start()
            at_middle("near_y", p).start()

            @pl.when(p == 0)
            def _():
                pl.semaphore_signal(token.at[0], inc=1, device_id={"row": inward}, device_id_type=MESH)

            @pl.when(p == pieces - 1)
            def _():
                pl.semaphore_wait(token.at[0], 1)
                pl.semaphore_signal(token.at[1], inc=1, device_id={"row": outward}, device_id_type=MESH)

    each(0, pieces, first)

    @pl.when(corner)
    def _():
        pl.semaphore_wait(token.at[1], 1)

    for k in range(1, rows):
        orb_copy(k).start()

    @pl.when(middle)
    def _():
        each(0, pieces, lambda p: arrived(0, 1 - y, p))

    loads[3].wait()
    for load in loads[5:]:
        load.wait()

    def second(p):
        @pl.when(corner)
        def _():
            arrived(2, y, p)
            at_corner("third_y", p).start()

        @pl.when(middle)
        def _():
            arrived(3, y, p)
            at_middle("last_out", p).start()
            if p >= split_at:
                at_middle("last_y", p).start()

        share(0, p, pieces)

    for p in range(pieces):
        second(p)

    @pl.when(middle)
    def _():
        each(0, split_at, lambda p: at_middle("last_y", p).start())

    each(0, pieces, lambda p: arrived(1, 1 - y, p))

    def closing(p):
        share(1, p, split_at)

        @pl.when(corner)
        def _():
            arrived(3, y, p)
            at_corner("last_y", p).start()

        @pl.when(middle)
        def _():
            arrived(3, 1 - y, p + split_at)
            at_middle("extra", p + split_at).start()

    for p in range(split_at):
        closing(p)
    pass_orbitals()
    each(0, pieces, lambda p: arrived(2, 1 - y, p))
    share(2, 0, 1)
    rank_orbitals()
    each(0, peers // 4, lambda q: [place_picks(4 * q + k) for k in range(4)])

    @pl.when(corner)
    def _():
        each(split_at, pieces, lambda p: arrived(3, y, p))
        each(split_at, pieces, lambda p: arrived(3, 1 - y, p))
    each(0, split_at, lambda p: arrived(3, 1 - y, p))

    mine = pl.ds(pl.multiple_of(c * half, half), half)
    theirs = pl.ds(pl.multiple_of((1 - c) * half, half), half)

    def to_partner(which, src, dst):
        return pltpu.make_async_remote_copy(
            src_ref=src, dst_ref=dst, send_sem=col_sem.at[0, which], recv_sem=col_sem.at[1, which],
            device_id={"col": 1 - c}, device_id_type=MESH,
        )

    mix_swap = to_partner(0, mix_out, mix_in)
    swap = to_partner(1, acc.at[:, theirs, :], half_in)

    def mixed(s, out_rows):
        return weight_ref[0] * acc[s, out_rows, width:] + weight_ref[1] * acc[s, out_rows, :width]

    for start in range(0, tile_count, 4):
        several(3, start, min(4, tile_count - start), theirs)
    for s in range(BR_DEV):
        mix_out[s] = mixed(s, theirs)
    mix_swap.start()
    swap.start()
    for start in range(0, tile_count, 4):
        several(3, start, min(4, tile_count - start), mine)
    for s in range(BR_DEV):
        mix_own[s] = mixed(s, mine)
    mix_swap.wait_recv()
    density_rows = [(-(mix_own[s] + mix_in[s])).astype(jnp.bfloat16) for s in range(BR_DEV)]
    density_rows = jnp.concatenate(density_rows, axis=0)

    group = lanes_y * cols

    def row_copy(target):
        return pltpu.make_async_remote_copy(
            src_ref=send_rows.at[target], dst_ref=recv_rows.at[me],
            send_sem=row_send.at[target], recv_sem=row_recv.at[me],
            device_id=spot(target), device_id_type=MESH,
        )

    for k in range(depth_z - 1):
        for part in range(lanes_y if k == 0 else 1):
            count = cols if k == 0 else group
            base = (k + jnp.where(k >= z, 1, 0)) * group + part * count
            hot = pick_hot[pl.ds(pl.multiple_of(base * capacity, count * capacity), count * capacity), :]
            picked = jnp.dot(hot, density_rows, preferred_element_type=jnp.float32).astype(jnp.bfloat16)
            send_rows[pl.ds(base, count)] = picked.reshape(count, capacity, width)
            for lane in range(count):
                row_copy(base + lane).start()
    base = z * group
    hot = pick_hot[pl.ds(pl.multiple_of(base * capacity, group * capacity), group * capacity), :]
    picked = jnp.dot(hot, density_rows, preferred_element_type=jnp.float32).astype(jnp.bfloat16)
    send_rows[pl.ds(base, group)] = picked.reshape(group, capacity, width)
    for k in range(1, group):
        row_copy(base + (me - base + k) % group).start()
    recv_rows[me] = send_rows[me]
    swap.wait_recv()
    for s in range(BR_DEV):
        column = -(acc[s, mine, :] + half_in[s])
        inv_ref[s, 0] = column[:, :width]
        inv_ref[s, 1] = column[:, width:]
    loads[4].wait()

    @pl.when(corner)
    def _():
        def sent(p):
            for name in corner_sends:
                if name != "last_y":
                    at_corner(name, p).wait_send()
        each(0, pieces, sent)
        each(0, split_at, lambda p: at_corner("last_y", p).wait_send())

    @pl.when(middle)
    def _():
        def sent(p):
            for name in middle_sends:
                if name != "extra":
                    at_middle(name, p).wait_send()
        each(0, pieces, sent)
        each(split_at, pieces, lambda p: at_middle("extra", p).wait_send())

    mix_swap.wait_send()
    swap.wait_send()
    for k in range(1, rows):
        orb_copy(k).wait_send()
    orb_block(c).wait_send()

    projected = [None] * boxes
    for at_z in range(depth_z):
        if at_z == depth_z - 1:
            for k in range(1, peers):
                row_copy((me + k) % peers).wait_send()
        for origin in range(at_z * group, (at_z + 1) * group):
            @pl.when(me != origin)
            def _(origin=origin):
                dst = recv_rows.at[origin]
                pltpu.make_async_remote_copy(
                    src_ref=dst, dst_ref=dst, send_sem=row_send.at[origin], recv_sem=row_recv.at[origin],
                    device_id={"row": other}, device_id_type=MESH,
                ).wait_recv()
        if at_z == depth_z - 1:
            late_rows[...] = recv_rows[at_z * group:(at_z + 1) * group]
            continue
        got = recv_rows[at_z * group:(at_z + 1) * group].reshape(group * capacity, width)
        for n in range(boxes):
            value = lax.dot_general(
                got, basis_hot[n, at_z * group * capacity:(at_z + 1) * group * capacity, :],
                (((0,), (0,)), ((), ())), preferred_element_type=jnp.float32)
            projected[n] = value if at_z == 0 else projected[n] + value
        if at_z == depth_z - 2:
            for n in range(boxes):
                projected_ref[n] = projected[n]


def deliver(column, projected, late_rows, late_basis, super_basis, column_out, density_out, density, sem):
    column_copy = pltpu.make_async_copy(column, column_out, sem.at[0])
    column_copy.start()
    boxes, width, _ = projected.shape
    got = late_rows[...].reshape(late_basis.shape[1], width)
    for n in range(boxes):
        value = projected[n] + lax.dot_general(
            got, late_basis[n], (((0,), (0,)), ((), ())), preferred_element_type=jnp.float32)
        density[n:n + 1, :] = jnp.sum(super_basis[n].astype(jnp.float32) * value, axis=0, keepdims=True)
    density_copy = pltpu.make_async_copy(density, density_out, sem.at[1])
    density_copy.start()
    density_copy.wait()
    column_copy.wait()


def fused(rows, cols, panel, tiles, tile_slot, tile_col, pole_weight, box_orbitals, box_basis, supernode_basis):
    blocks, parts, shard_rows, width = panel.shape[1:]
    tile_count, _, block, _ = tiles.shape
    boxes, orbs = box_orbitals.shape
    points = box_basis.shape[2]
    half = block // cols
    peers = rows * cols
    capacity = 2 * boxes * orbs // peers
    pieces = blocks // 2
    dma = pltpu.SemaphoreType.DMA
    bf16, f32 = jnp.bfloat16, jnp.float32
    hbm = pl.BlockSpec(memory_space=pl.ANY)
    vmem = pl.BlockSpec(memory_space=pltpu.VMEM)
    late = 2 * cols * capacity
    results = pl.pallas_call(
        functools.partial(kernel, rows, cols),
        name="pole_step",
        out_shape=(
            pltpu.VMEM((BR_DEV, 2, half, width), f32),
            pltpu.VMEM((boxes, width, points), f32),
            pltpu.VMEM((2 * cols, capacity, width), bf16),
            pltpu.VMEM((boxes, late, points), bf16),
            pltpu.VMEM(supernode_basis.shape, bf16),
        ),
        in_specs=[hbm] * 8,
        out_specs=(vmem,) * 5,
        scratch_shapes=[
            pltpu.SMEM(tile_slot.shape, jnp.int32),
            pltpu.SMEM(tile_col.shape, jnp.int32),
            pltpu.SMEM(pole_weight.shape, f32),
        ] + [pltpu.VMEM((2, blocks, parts, shard_rows, width), bf16)] * 4 + [
            pltpu.VMEM(tiles.shape, bf16),
            pltpu.VMEM(box_basis.shape, bf16),
            pltpu.VMEM((cols, rows, boxes, orbs), jnp.int32),
            pltpu.VMEM((BR_DEV, block, 2 * width), f32),
            pltpu.VMEM((BR_DEV, half, 2 * width), f32),
            pltpu.VMEM((BR_DEV, half, width), f32),
            pltpu.VMEM((BR_DEV, half, width), f32),
            pltpu.VMEM((BR_DEV, half, width), f32),
            pltpu.VMEM((peers * capacity, BR_DEV * half), bf16),
            pltpu.VMEM((boxes, peers * capacity - late, points), bf16),
            pltpu.VMEM((boxes, peers, orbs), f32),
            pltpu.VMEM((boxes, peers, orbs), f32),
            pltpu.VMEM((peers, capacity, width), bf16),
            pltpu.VMEM((peers, capacity, width), bf16),
            dma((8,)),
            dma((3, 4, pieces)),
            dma((4, 2, pieces)),
            pltpu.SemaphoreType.REGULAR((2,)),
            dma((2, 2)),
            dma((peers,)),
            dma((peers,)),
            dma((peers,)),
            dma((peers,)),
        ],
        compiler_params=pltpu.CompilerParams(
            collective_id=0, has_side_effects=True, vmem_limit_bytes=56 * 1024 * 1024),
    )(tile_slot, tile_col, pole_weight, panel, tiles, box_orbitals, box_basis, supernode_basis)
    return pl.pallas_call(
        deliver,
        name="deliver",
        out_shape=(
            jax.ShapeDtypeStruct((BR_DEV, 2, half, width), f32),
            jax.ShapeDtypeStruct((boxes, points), f32),
        ),
        in_specs=[vmem] * 5,
        out_specs=(hbm, hbm),
        scratch_shapes=[pltpu.VMEM((boxes, points), f32), dma((2,))],
        compiler_params=pltpu.CompilerParams(vmem_limit_bytes=8 * 1024 * 1024),
    )(*results)


def plain(panel, tiles, tile_slot, tile_col, pole_weight, box_orbitals, box_basis, supernode_basis):
    gathered = lax.all_gather(panel, "row", axis=3, tiled=True)
    blocks = gathered[0]
    selector = (tile_col[:, None] == jnp.arange(blocks.shape[0], dtype=jnp.int32)[None, :]).astype(
        jnp.bfloat16
    )
    chosen = jnp.einsum(
        "tj,jcbs->tcbs", selector, blocks, preferred_element_type=jnp.float32
    ).astype(jnp.bfloat16)
    real_part = jnp.einsum(
        "tab,tbs->tas", tiles[:, 0], chosen[:, 0], preferred_element_type=jnp.float32
    )
    real_part = real_part - jnp.einsum(
        "tab,tbs->tas", tiles[:, 1], chosen[:, 1], preferred_element_type=jnp.float32
    )
    imag_part = jnp.einsum(
        "tab,tbs->tas", tiles[:, 0], chosen[:, 1], preferred_element_type=jnp.float32
    )
    imag_part = imag_part + jnp.einsum(
        "tab,tbs->tas", tiles[:, 1], chosen[:, 0], preferred_element_type=jnp.float32
    )
    products = jnp.stack([real_part, imag_part], axis=1)
    partial_value = jnp.stack(
        [
            jnp.sum(jnp.where((tile_slot == slot_row)[:, None, None, None], products, 0.0), axis=0)
            for slot_row in range(BR_DEV)
        ]
    )
    summed = lax.psum_scatter(partial_value, "col", scatter_dimension=2, tiled=True)
    inverse_column = -summed
    density_local = (
        pole_weight[0] * inverse_column[:, 1] + pole_weight[1] * inverse_column[:, 0]
    ).astype(jnp.bfloat16)
    columns = density_local.shape[2]
    density_local = density_local.reshape(-1, columns)
    block_width = tiles.shape[2]
    col_count = lax.axis_size("col")
    half_rows = block_width // col_count
    wanted = box_orbitals.reshape(-1)
    wanted_total = wanted.shape[0]
    block_index = wanted // block_width
    within = wanted % block_width
    source = block_index // BR_DEV * col_count + within // half_rows
    local_row = block_index % BR_DEV * half_rows + within % half_rows
    start_rows = jnp.zeros((wanted_total, columns), jnp.bfloat16)
    shards = lax.all_gather(density_local[None], ("row", "col"), axis=0, tiled=True)
    count = shards.shape[0]
    inside = (source >= 0) & (source < count)
    clipped = jnp.clip(source, 0, count - 1)
    fetched = shards[clipped, local_row]
    picked = jnp.where(inside[:, None], fetched, start_rows)
    picked = picked.reshape(box_basis.shape[0], box_basis.shape[1], columns)
    projected = jnp.einsum("nas,nap->nsp", picked, box_basis, preferred_element_type=jnp.float32)
    density = jnp.sum(supernode_basis.astype(jnp.float32) * projected, axis=1)
    return (inverse_column, density)


def solution(mesh):
    rows, cols = mesh.shape["row"], mesh.shape["col"]

    def local(panel, *rest):
        if cols == 2 and rows == 8 and panel.shape[1] % 8 == 0 and 2 * panel.shape[3] % panel.shape[4] == 0:
            return fused(rows, cols, panel, *rest)
        return plain(panel, *rest)

    return jax.shard_map(
        local,
        mesh=mesh,
        in_specs=(
            P(("pole", "col"), None, None, "row", None),
            P(("pole", "row", "col"), None, None, None),
            P(("pole", "row", "col")),
            P(("pole", "row", "col")),
            P("pole"),
            P(("pole", "row", "col"), None),
            P(("pole", "row", "col"), None, None),
            P(("pole", "row", "col"), None, None),
        ),
        out_specs=(P(("pole", "row"), None, "col", None), P(("pole", "row", "col"), None)),
        check_vma=False,
    )
```

```python
import functools

import jax
import jax.numpy as jnp
from jax import lax
from jax.experimental import pallas as pl
from jax.experimental.pallas import tpu as pltpu
from jax.sharding import PartitionSpec as P

BR_DEV = 2
MESH = pl.DeviceIdType.MESH


def log2(value):
    assert value & (value - 1) == 0
    return value.bit_length() - 1


def kernel(
    rows, cols, slots, tile_cols, weights, panel, tiles, orbitals, basis, super_basis,
    inv_ref, projected_ref, late_rows, late_basis, super_buf, slot_ref, tcol_ref, weight_ref, own, near, third, last,
    tile_buf, basis_buf, orb_buf, acc, half_in, mix_out, mix_own, mix_in, pick_hot, basis_hot, order_buf, local_buf,
    send_rows, recv_rows, local_sem, send_sem, recv_sem, token, col_sem, orb_send, orb_recv, row_send, row_recv,
):
    lanes_y = 2
    depth_z = rows // lanes_y
    peers = rows * cols
    r = lax.axis_index("row")
    c = lax.axis_index("col")
    me = r * cols + c
    z = r // lanes_y
    y = r % lanes_y
    shard_rows = panel.shape[3]
    width = panel.shape[4]
    pieces = recv_sem.shape[2]
    step = panel.shape[1] // pieces
    split_at = pieces // 2
    tile_count = tiles.shape[0]
    block = tiles.shape[2]
    half = block // cols
    pair = lanes_y * shard_rows
    boxes, orbs = orbitals.shape
    capacity = send_rows.shape[1]

    inner = 1 - 2 * (z // (depth_z // 2))
    corner = jnp.logical_or(z == 0, z == depth_z - 1)
    middle = jnp.logical_not(corner)
    other = r + 1 - 2 * y
    inward = r + lanes_y * inner
    outward = r - lanes_y * inner
    buffers = (own, near, third, last)
    places = (
        z,
        z + inner,
        jnp.where(corner, z + 2 * inner, z - inner),
        jnp.where(corner, z + 3 * inner, z + 2 * inner),
    )
    IN, OUT, Y = 0, 1, 2

    def spot(index):
        return {"row": index // cols, "col": index % cols}

    loads = [
        pltpu.make_async_copy(panel.at[0], own.at[y], local_sem.at[0]),
        pltpu.make_async_copy(orbitals, orb_buf.at[c, r], local_sem.at[4]),
        pltpu.make_async_copy(basis, basis_buf, local_sem.at[2]),
        pltpu.make_async_copy(tiles, tile_buf, local_sem.at[1]),
        pltpu.make_async_copy(super_basis, super_buf, local_sem.at[3]),
        pltpu.make_async_copy(slots, slot_ref, local_sem.at[5]),
        pltpu.make_async_copy(tile_cols, tcol_ref, local_sem.at[6]),
        pltpu.make_async_copy(weights, weight_ref, local_sem.at[7]),
    ]
    barrier = pltpu.get_barrier_semaphore()
    for device in (
        {"row": other}, {"col": 1 - c}, {"row": other, "col": 1 - c}, {"row": inward},
    ):
        pl.semaphore_signal(barrier, inc=1, device_id=device, device_id_type=MESH)

    @pl.when(middle)
    def _():
        pl.semaphore_signal(barrier, inc=1, device_id={"row": outward}, device_id_type=MESH)

    for load in loads[:3]:
        load.start()

    @pl.when(middle)
    def _():
        pl.semaphore_wait(barrier, 5)

    @pl.when(corner)
    def _():
        pl.semaphore_wait(barrier, 4)

    loads[0].wait()

    def piece(which, lane, p):
        return buffers[which].at[lane, pl.ds(p * step, step)]

    def copy(link, kind, source, target, lane, p):
        row = (inward, outward, other)[link]
        return pltpu.make_async_remote_copy(
            src_ref=piece(source, lane, p), dst_ref=piece(target, lane, p),
            send_sem=send_sem.at[link, kind, p], recv_sem=recv_sem.at[target, lane, p],
            device_id={"row": row}, device_id_type=MESH,
        )

    def arrived(target, lane, p):
        dst = piece(target, lane, p)
        pltpu.make_async_remote_copy(
            src_ref=dst, dst_ref=dst, send_sem=send_sem.at[0, 0, p], recv_sem=recv_sem.at[target, lane, p],
            device_id={"row": other}, device_id_type=MESH,
        ).wait_recv()

    def each(low, high, body):
        def run(h, carry):
            body(h)
            return carry
        lax.fori_loop(low, high, run, 0)

    corner_sends = {
        "own_in": (IN, 0, 0, 2, y), "own_y": (Y, 0, 0, 0, y),
        "extra": (IN, 1, 0, 2, 1 - y),
        "near_y": (Y, 1, 1, 1, y), "third_y": (Y, 2, 2, 2, y), "last_y": (Y, 3, 3, 3, y),
    }
    middle_sends = {
        "own_out": (OUT, 0, 0, 1, y), "own_in": (IN, 0, 0, 1, y), "own_y": (Y, 0, 0, 0, y),
        "third_in": (IN, 1, 2, 3, y),
        "near_out": (OUT, 1, 1, 2, y), "near_y": (Y, 1, 1, 1, y),
        "last_out": (OUT, 2, 3, 3, y), "last_y": (Y, 2, 3, 3, y),
        "extra": (OUT, 3, 3, 3, 1 - y),
    }

    def at_corner(name, p):
        return copy(*corner_sends[name], p)

    def at_middle(name, p):
        return copy(*middle_sends[name], p)

    @pl.when(corner)
    def _():
        def go(p):
            at_corner("own_in", p).start()
            at_corner("own_y", p).start()
        each(0, pieces, go)

    @pl.when(middle)
    def _():
        def go(p):
            at_middle("own_out", p).start()
            at_middle("own_in", p).start()
            at_middle("own_y", p).start()
        each(0, pieces, go)

    for load in loads[3:]:
        load.start()
    acc[...] = jnp.zeros_like(acc)
    block_bits, half_bits = log2(block), log2(half)

    def split(g):
        row_block = g >> block_bits
        within = g & (block - 1)
        source = (row_block >> log2(BR_DEV)) * cols + (within >> half_bits)
        local = (row_block & (BR_DEV - 1)) * half + (within & (half - 1))
        return source, local

    def ranks(masks):
        before = lax.broadcasted_iota(jnp.int32, (orbs, orbs), 0)
        after = lax.broadcasted_iota(jnp.int32, (orbs, orbs), 1)
        upper = jnp.where(before <= after, 1.0, 0.0).astype(jnp.bfloat16)
        seen = jnp.zeros((masks[0].shape[0], 1), jnp.float32)
        result = []
        for mask in masks:
            counted = jnp.dot(mask.astype(jnp.bfloat16), upper, preferred_element_type=jnp.float32)
            result.append(counted - 1.0 + seen)
            seen = seen + jnp.sum(mask, axis=1, keepdims=True)
        return result

    def place_basis():
        loads[1].wait()
        loads[2].wait()
        masks = []
        peer_id = lax.broadcasted_iota(jnp.int32, (peers, orbs), 0)
        for n in range(boxes):
            source, _ = split(orb_buf[c, r, n:n + 1, :])
            masks.append(jnp.where(peer_id == source, 1.0, 0.0))
        order = ranks(masks)
        arrive = lax.broadcasted_iota(jnp.int32, (peers * capacity, orbs), 0).astype(jnp.float32)
        for n in range(boxes):
            position = jnp.sum(
                masks[n] * (order[n] + (peer_id * capacity).astype(jnp.float32)), axis=0, keepdims=True)
            hot = jnp.where(arrive == position, 1.0, 0.0).astype(jnp.bfloat16)
            placed = jnp.dot(hot, basis_buf[n], preferred_element_type=jnp.float32).astype(jnp.bfloat16)
            early = basis_hot.shape[1]
            basis_hot[n] = placed[:early]
            late_basis[n] = placed[early:]

    def orb_copy(k):
        return pltpu.make_async_remote_copy(
            src_ref=orbitals, dst_ref=orb_buf.at[c, r], send_sem=orb_send.at[k], recv_sem=orb_recv.at[k],
            device_id={"row": (r + k) % rows}, device_id_type=MESH,
        )

    def orb_block(col):
        return pltpu.make_async_remote_copy(
            src_ref=orb_buf.at[col], dst_ref=orb_buf.at[col], send_sem=orb_send.at[0], recv_sem=orb_recv.at[0],
            device_id={"col": 1 - c}, device_id_type=MESH,
        )

    def pass_orbitals():
        for k in range(1, rows):
            dst = orb_buf.at[c, (r + rows - k) % rows]
            pltpu.make_async_remote_copy(
                src_ref=dst, dst_ref=dst, send_sem=orb_send.at[k], recv_sem=orb_recv.at[k],
                device_id={"row": other}, device_id_type=MESH,
            ).wait_recv()
        orb_block(c).start()

    def rank_orbitals():
        orb_block(1 - c).wait_recv()
        asked = []
        for n in range(boxes):
            g = jnp.concatenate([orb_buf[q % cols, q // cols, n:n + 1, :] for q in range(peers)], axis=0)
            source, local = split(g)
            asked.append((jnp.where(source == me, 1.0, 0.0), local.astype(jnp.float32)))
        order = ranks([a[0] for a in asked])
        for n in range(boxes):
            order_buf[n] = jnp.where(asked[n][0] > 0.5, order[n], -1.0)
            local_buf[n] = asked[n][1] + 1.0

    def place_picks(q):
        place = lax.broadcasted_iota(jnp.int32, (capacity, orbs), 0).astype(jnp.float32)
        row_id = lax.broadcasted_iota(jnp.int32, (capacity, BR_DEV * half), 1).astype(jnp.float32)
        found = jnp.zeros((capacity, 1), jnp.float32)
        for n in range(boxes):
            hit = place == order_buf[n, pl.ds(q, 1), :]
            found = found + jnp.sum(jnp.where(hit, local_buf[n, pl.ds(q, 1), :], 0.0), axis=1, keepdims=True)
        spot_rows = pl.ds(pl.multiple_of(q * capacity, capacity), capacity)
        pick_hot[spot_rows, :] = jnp.where(row_id == found - 1.0, 1.0, 0.0).astype(jnp.bfloat16)

    def product(which, t, out_rows):
        j = tcol_ref[t]
        offset = pl.multiple_of(places[which] * pair, pair)
        left = jnp.concatenate(
            [tile_buf[t, 0, out_rows, pl.ds(offset, pair)], tile_buf[t, 1, out_rows, pl.ds(offset, pair)]], axis=1)
        parts = [buffers[which][k, j] for k in range(lanes_y)]
        real = jnp.concatenate([p[0] for p in parts], axis=0)
        imag = jnp.concatenate([p[1] for p in parts], axis=0)
        right = jnp.concatenate(
            [jnp.concatenate([real, imag], axis=1), jnp.concatenate([-imag, real], axis=1)], axis=0)
        return jnp.dot(left, right, preferred_element_type=jnp.float32)

    def several(which, start, count, out_rows):
        values = [product(which, start + k, out_rows) for k in range(count)]
        for s in range(BR_DEV):
            total = jnp.where(slot_ref[start] == s, values[0], 0.0)
            for k in range(1, count):
                total = total + jnp.where(slot_ref[start + k] == s, values[k], 0.0)
            acc[s, out_rows, :] += total

    everything = pl.ds(0, block)

    def share(which, p, parts):
        first_tile, last_tile = p * tile_count // parts, (p + 1) * tile_count // parts
        for start in range(first_tile, last_tile, 4):
            several(which, start, min(4, last_tile - start), everything)

    place_basis()

    def first(p):
        @pl.when(corner)
        def _():
            arrived(1, y, p)
            at_corner("near_y", p).start()
            arrived(0, 1 - y, p)
            at_corner("extra", p).start()

        @pl.when(middle)
        def _():
            arrived(2, y, p)
            at_middle("third_in", p).start()
            arrived(1, y, p)
            at_middle("near_out", p).start()
            at_middle("near_y", p).start()

            @pl.when(p == 0)
            def _():
                pl.semaphore_signal(token.at[0], inc=1, device_id={"row": inward}, device_id_type=MESH)

            @pl.when(p == pieces - 1)
            def _():
                pl.semaphore_wait(token.at[0], 1)
                pl.semaphore_signal(token.at[1], inc=1, device_id={"row": outward}, device_id_type=MESH)

    each(0, pieces, first)

    @pl.when(corner)
    def _():
        pl.semaphore_wait(token.at[1], 1)

    for k in range(1, rows):
        orb_copy(k).start()

    @pl.when(middle)
    def _():
        each(0, pieces, lambda p: arrived(0, 1 - y, p))

    loads[3].wait()
    for load in loads[5:]:
        load.wait()

    def second(p):
        @pl.when(corner)
        def _():
            arrived(2, y, p)
            at_corner("third_y", p).start()

        @pl.when(middle)
        def _():
            arrived(3, y, p)
            at_middle("last_out", p).start()
            if p >= split_at:
                at_middle("last_y", p).start()

        share(0, p, pieces)

    for p in range(pieces):
        second(p)

    @pl.when(middle)
    def _():
        each(0, split_at, lambda p: at_middle("last_y", p).start())

    each(0, pieces, lambda p: arrived(1, 1 - y, p))

    def closing(p):
        share(1, p, split_at)

        @pl.when(corner)
        def _():
            arrived(3, y, p)
            at_corner("last_y", p).start()

        @pl.when(middle)
        def _():
            arrived(3, 1 - y, p + split_at)
            at_middle("extra", p + split_at).start()

    for p in range(split_at):
        closing(p)
    pass_orbitals()
    each(0, pieces, lambda p: arrived(2, 1 - y, p))
    share(2, 0, 1)
    rank_orbitals()
    each(0, peers // 4, lambda q: [place_picks(4 * q + k) for k in range(4)])

    @pl.when(corner)
    def _():
        each(split_at, pieces, lambda p: arrived(3, y, p))
        each(split_at, pieces, lambda p: arrived(3, 1 - y, p))
    each(0, split_at, lambda p: arrived(3, 1 - y, p))

    mine = pl.ds(pl.multiple_of(c * half, half), half)
    theirs = pl.ds(pl.multiple_of((1 - c) * half, half), half)

    def to_partner(which, src, dst):
        return pltpu.make_async_remote_copy(
            src_ref=src, dst_ref=dst, send_sem=col_sem.at[0, which], recv_sem=col_sem.at[1, which],
            device_id={"col": 1 - c}, device_id_type=MESH,
        )

    mix_swap = to_partner(0, mix_out, mix_in)
    swap = to_partner(1, acc.at[:, theirs, :], half_in)

    def mixed(s, out_rows):
        return weight_ref[0] * acc[s, out_rows, width:] + weight_ref[1] * acc[s, out_rows, :width]

    for start in range(0, tile_count, 4):
        several(3, start, min(4, tile_count - start), theirs)
    for s in range(BR_DEV):
        mix_out[s] = mixed(s, theirs)
    mix_swap.start()
    for start in range(0, tile_count, 4):
        several(3, start, min(4, tile_count - start), mine)
    for s in range(BR_DEV):
        mix_own[s] = mixed(s, mine)
    mix_swap.wait_recv()
    density_rows = [(-(mix_own[s] + mix_in[s])).astype(jnp.bfloat16) for s in range(BR_DEV)]
    density_rows = jnp.concatenate(density_rows, axis=0)

    group = lanes_y * cols

    def row_copy(target):
        return pltpu.make_async_remote_copy(
            src_ref=send_rows.at[target], dst_ref=recv_rows.at[me],
            send_sem=row_send.at[target], recv_sem=row_recv.at[me],
            device_id=spot(target), device_id_type=MESH,
        )

    for k in range(depth_z - 1):
        for part in range(lanes_y if k == 0 else 1):
            count = cols if k == 0 else group
            base = (k + jnp.where(k >= z, 1, 0)) * group + part * count
            hot = pick_hot[pl.ds(pl.multiple_of(base * capacity, count * capacity), count * capacity), :]
            picked = jnp.dot(hot, density_rows, preferred_element_type=jnp.float32).astype(jnp.bfloat16)
            send_rows[pl.ds(base, count)] = picked.reshape(count, capacity, width)
            for lane in range(count):
                row_copy(base + lane).start()
    base = z * group
    hot = pick_hot[pl.ds(pl.multiple_of(base * capacity, group * capacity), group * capacity), :]
    picked = jnp.dot(hot, density_rows, preferred_element_type=jnp.float32).astype(jnp.bfloat16)
    send_rows[pl.ds(base, group)] = picked.reshape(group, capacity, width)
    for k in range(1, group):
        row_copy(base + (me - base + k) % group).start()
    swap.start()
    recv_rows[me] = send_rows[me]
    swap.wait_recv()
    for s in range(BR_DEV):
        column = -(acc[s, mine, :] + half_in[s])
        inv_ref[s, 0] = column[:, :width]
        inv_ref[s, 1] = column[:, width:]
    loads[4].wait()

    @pl.when(corner)
    def _():
        def sent(p):
            for name in corner_sends:
                if name != "last_y":
                    at_corner(name, p).wait_send()
        each(0, pieces, sent)
        each(0, split_at, lambda p: at_corner("last_y", p).wait_send())

    @pl.when(middle)
    def _():
        def sent(p):
            for name in middle_sends:
                if name != "extra":
                    at_middle(name, p).wait_send()
        each(0, pieces, sent)
        each(split_at, pieces, lambda p: at_middle("extra", p).wait_send())

    mix_swap.wait_send()
    swap.wait_send()
    for k in range(1, rows):
        orb_copy(k).wait_send()
    orb_block(c).wait_send()

    projected = [None] * boxes
    for at_z in range(depth_z):
        if at_z == depth_z - 1:
            for k in range(1, peers):
                row_copy((me + k) % peers).wait_send()
        for origin in range(at_z * group, (at_z + 1) * group):
            @pl.when(me != origin)
            def _(origin=origin):
                dst = recv_rows.at[origin]
                pltpu.make_async_remote_copy(
                    src_ref=dst, dst_ref=dst, send_sem=row_send.at[origin], recv_sem=row_recv.at[origin],
                    device_id={"row": other}, device_id_type=MESH,
                ).wait_recv()
        if at_z == depth_z - 1:
            late_rows[...] = recv_rows[at_z * group:(at_z + 1) * group]
            continue
        got = recv_rows[at_z * group:(at_z + 1) * group].reshape(group * capacity, width)
        for n in range(boxes):
            value = lax.dot_general(
                got, basis_hot[n, at_z * group * capacity:(at_z + 1) * group * capacity, :],
                (((0,), (0,)), ((), ())), preferred_element_type=jnp.float32)
            projected[n] = value if at_z == 0 else projected[n] + value
        if at_z == depth_z - 2:
            for n in range(boxes):
                projected_ref[n] = projected[n]


def deliver(column, projected, late_rows, late_basis, super_basis, column_out, density_out, density, sem):
    column_copy = pltpu.make_async_copy(column, column_out, sem.at[0])
    column_copy.start()
    boxes, width, _ = projected.shape
    got = late_rows[...].reshape(late_basis.shape[1], width)
    for n in range(boxes):
        value = projected[n] + lax.dot_general(
            got, late_basis[n], (((0,), (0,)), ((), ())), preferred_element_type=jnp.float32)
        density[n:n + 1, :] = jnp.sum(super_basis[n].astype(jnp.float32) * value, axis=0, keepdims=True)
    density_copy = pltpu.make_async_copy(density, density_out, sem.at[1])
    density_copy.start()
    density_copy.wait()
    column_copy.wait()


def fused(rows, cols, panel, tiles, tile_slot, tile_col, pole_weight, box_orbitals, box_basis, supernode_basis):
    blocks, parts, shard_rows, width = panel.shape[1:]
    tile_count, _, block, _ = tiles.shape
    boxes, orbs = box_orbitals.shape
    points = box_basis.shape[2]
    half = block // cols
    peers = rows * cols
    capacity = 2 * boxes * orbs // peers
    pieces = blocks // 2
    dma = pltpu.SemaphoreType.DMA
    bf16, f32 = jnp.bfloat16, jnp.float32
    hbm = pl.BlockSpec(memory_space=pl.ANY)
    vmem = pl.BlockSpec(memory_space=pltpu.VMEM)
    late = 2 * cols * capacity
    results = pl.pallas_call(
        functools.partial(kernel, rows, cols),
        name="pole_step",
        out_shape=(
            pltpu.VMEM((BR_DEV, 2, half, width), f32),
            pltpu.VMEM((boxes, width, points), f32),
            pltpu.VMEM((2 * cols, capacity, width), bf16),
            pltpu.VMEM((boxes, late, points), bf16),
            pltpu.VMEM(supernode_basis.shape, bf16),
        ),
        in_specs=[hbm] * 8,
        out_specs=(vmem,) * 5,
        scratch_shapes=[
            pltpu.SMEM(tile_slot.shape, jnp.int32),
            pltpu.SMEM(tile_col.shape, jnp.int32),
            pltpu.SMEM(pole_weight.shape, f32),
        ] + [pltpu.VMEM((2, blocks, parts, shard_rows, width), bf16)] * 4 + [
            pltpu.VMEM(tiles.shape, bf16),
            pltpu.VMEM(box_basis.shape, bf16),
            pltpu.VMEM((cols, rows, boxes, orbs), jnp.int32),
            pltpu.VMEM((BR_DEV, block, 2 * width), f32),
            pltpu.VMEM((BR_DEV, half, 2 * width), f32),
            pltpu.VMEM((BR_DEV, half, width), f32),
            pltpu.VMEM((BR_DEV, half, width), f32),
            pltpu.VMEM((BR_DEV, half, width), f32),
            pltpu.VMEM((peers * capacity, BR_DEV * half), bf16),
            pltpu.VMEM((boxes, peers * capacity - late, points), bf16),
            pltpu.VMEM((boxes, peers, orbs), f32),
            pltpu.VMEM((boxes, peers, orbs), f32),
            pltpu.VMEM((peers, capacity, width), bf16),
            pltpu.VMEM((peers, capacity, width), bf16),
            dma((8,)),
            dma((3, 4, pieces)),
            dma((4, 2, pieces)),
            pltpu.SemaphoreType.REGULAR((2,)),
            dma((2, 2)),
            dma((peers,)),
            dma((peers,)),
            dma((peers,)),
            dma((peers,)),
        ],
        compiler_params=pltpu.CompilerParams(
            collective_id=0, has_side_effects=True, vmem_limit_bytes=56 * 1024 * 1024),
    )(tile_slot, tile_col, pole_weight, panel, tiles, box_orbitals, box_basis, supernode_basis)
    return pl.pallas_call(
        deliver,
        name="deliver",
        out_shape=(
            jax.ShapeDtypeStruct((BR_DEV, 2, half, width), f32),
            jax.ShapeDtypeStruct((boxes, points), f32),
        ),
        in_specs=[vmem] * 5,
        out_specs=(hbm, hbm),
        scratch_shapes=[pltpu.VMEM((boxes, points), f32), dma((2,))],
        compiler_params=pltpu.CompilerParams(vmem_limit_bytes=8 * 1024 * 1024),
    )(*results)


def plain(panel, tiles, tile_slot, tile_col, pole_weight, box_orbitals, box_basis, supernode_basis):
    gathered = lax.all_gather(panel, "row", axis=3, tiled=True)
    blocks = gathered[0]
    selector = (tile_col[:, None] == jnp.arange(blocks.shape[0], dtype=jnp.int32)[None, :]).astype(
        jnp.bfloat16
    )
    chosen = jnp.einsum(
        "tj,jcbs->tcbs", selector, blocks, preferred_element_type=jnp.float32
    ).astype(jnp.bfloat16)
    real_part = jnp.einsum(
        "tab,tbs->tas", tiles[:, 0], chosen[:, 0], preferred_element_type=jnp.float32
    )
    real_part = real_part - jnp.einsum(
        "tab,tbs->tas", tiles[:, 1], chosen[:, 1], preferred_element_type=jnp.float32
    )
    imag_part = jnp.einsum(
        "tab,tbs->tas", tiles[:, 0], chosen[:, 1], preferred_element_type=jnp.float32
    )
    imag_part = imag_part + jnp.einsum(
        "tab,tbs->tas", tiles[:, 1], chosen[:, 0], preferred_element_type=jnp.float32
    )
    products = jnp.stack([real_part, imag_part], axis=1)
    partial_value = jnp.stack(
        [
            jnp.sum(jnp.where((tile_slot == slot_row)[:, None, None, None], products, 0.0), axis=0)
            for slot_row in range(BR_DEV)
        ]
    )
    summed = lax.psum_scatter(partial_value, "col", scatter_dimension=2, tiled=True)
    inverse_column = -summed
    density_local = (
        pole_weight[0] * inverse_column[:, 1] + pole_weight[1] * inverse_column[:, 0]
    ).astype(jnp.bfloat16)
    columns = density_local.shape[2]
    density_local = density_local.reshape(-1, columns)
    block_width = tiles.shape[2]
    col_count = lax.axis_size("col")
    half_rows = block_width // col_count
    wanted = box_orbitals.reshape(-1)
    wanted_total = wanted.shape[0]
    block_index = wanted // block_width
    within = wanted % block_width
    source = block_index // BR_DEV * col_count + within // half_rows
    local_row = block_index % BR_DEV * half_rows + within % half_rows
    start_rows = jnp.zeros((wanted_total, columns), jnp.bfloat16)
    shards = lax.all_gather(density_local[None], ("row", "col"), axis=0, tiled=True)
    count = shards.shape[0]
    inside = (source >= 0) & (source < count)
    clipped = jnp.clip(source, 0, count - 1)
    fetched = shards[clipped, local_row]
    picked = jnp.where(inside[:, None], fetched, start_rows)
    picked = picked.reshape(box_basis.shape[0], box_basis.shape[1], columns)
    projected = jnp.einsum("nas,nap->nsp", picked, box_basis, preferred_element_type=jnp.float32)
    density = jnp.sum(supernode_basis.astype(jnp.float32) * projected, axis=1)
    return (inverse_column, density)


def solution(mesh):
    rows, cols = mesh.shape["row"], mesh.shape["col"]

    def local(panel, *rest):
        if cols == 2 and rows == 8 and panel.shape[1] % 8 == 0 and 2 * panel.shape[3] % panel.shape[4] == 0:
            return fused(rows, cols, panel, *rest)
        return plain(panel, *rest)

    return jax.shard_map(
        local,
        mesh=mesh,
        in_specs=(
            P(("pole", "col"), None, None, "row", None),
            P(("pole", "row", "col"), None, None, None),
            P(("pole", "row", "col")),
            P(("pole", "row", "col")),
            P("pole"),
            P(("pole", "row", "col"), None),
            P(("pole", "row", "col"), None, None),
            P(("pole", "row", "col"), None, None),
        ),
        out_specs=(P(("pole", "row"), None, "col", None), P(("pole", "row", "col"), None)),
        check_vma=False,
    )
```

```python
import functools

import jax
import jax.numpy as jnp
from jax import lax
from jax.experimental import pallas as pl
from jax.experimental.pallas import tpu as pltpu
from jax.sharding import PartitionSpec as P

BR_DEV = 2
MESH = pl.DeviceIdType.MESH


def log2(value):
    assert value & (value - 1) == 0
    return value.bit_length() - 1


def kernel(
    rows, cols, slots, tile_cols, weights, panel, tiles, orbitals, basis, super_basis,
    inv_ref, projected_ref, late_rows, late_basis, super_buf, slot_ref, tcol_ref, weight_ref, own, near, third, last,
    tile_buf, basis_buf, orb_buf, acc, half_in, mix_out, mix_own, mix_in, pick_hot, basis_hot, order_buf, local_buf,
    send_rows, recv_rows, local_sem, send_sem, recv_sem, token, col_sem, orb_send, orb_recv, row_send, row_recv,
):
    lanes_y = 2
    depth_z = rows // lanes_y
    peers = rows * cols
    r = lax.axis_index("row")
    c = lax.axis_index("col")
    me = r * cols + c
    z = r // lanes_y
    y = r % lanes_y
    shard_rows = panel.shape[3]
    width = panel.shape[4]
    pieces = recv_sem.shape[2]
    step = panel.shape[1] // pieces
    split_at = pieces // 2
    tile_count = tiles.shape[0]
    block = tiles.shape[2]
    half = block // cols
    pair = lanes_y * shard_rows
    boxes, orbs = orbitals.shape
    capacity = send_rows.shape[1]

    inner = 1 - 2 * (z // (depth_z // 2))
    corner = jnp.logical_or(z == 0, z == depth_z - 1)
    middle = jnp.logical_not(corner)
    other = r + 1 - 2 * y
    inward = r + lanes_y * inner
    outward = r - lanes_y * inner
    buffers = (own, near, third, last)
    places = (
        z,
        z + inner,
        jnp.where(corner, z + 2 * inner, z - inner),
        jnp.where(corner, z + 3 * inner, z + 2 * inner),
    )
    IN, OUT, Y = 0, 1, 2

    def spot(index):
        return {"row": index // cols, "col": index % cols}

    loads = [
        pltpu.make_async_copy(panel.at[0], own.at[y], local_sem.at[0]),
        pltpu.make_async_copy(orbitals, orb_buf.at[c, r], local_sem.at[4]),
        pltpu.make_async_copy(basis, basis_buf, local_sem.at[2]),
        pltpu.make_async_copy(tiles, tile_buf, local_sem.at[1]),
        pltpu.make_async_copy(super_basis, super_buf, local_sem.at[3]),
        pltpu.make_async_copy(slots, slot_ref, local_sem.at[5]),
        pltpu.make_async_copy(tile_cols, tcol_ref, local_sem.at[6]),
        pltpu.make_async_copy(weights, weight_ref, local_sem.at[7]),
    ]
    barrier = pltpu.get_barrier_semaphore()
    for device in (
        {"row": other}, {"col": 1 - c}, {"row": other, "col": 1 - c}, {"row": inward},
    ):
        pl.semaphore_signal(barrier, inc=1, device_id=device, device_id_type=MESH)

    @pl.when(middle)
    def _():
        pl.semaphore_signal(barrier, inc=1, device_id={"row": outward}, device_id_type=MESH)

    for load in loads[:3]:
        load.start()

    @pl.when(middle)
    def _():
        pl.semaphore_wait(barrier, 5)

    @pl.when(corner)
    def _():
        pl.semaphore_wait(barrier, 4)

    loads[0].wait()

    def piece(which, lane, p):
        return buffers[which].at[lane, pl.ds(p * step, step)]

    def copy(link, kind, source, target, lane, p):
        row = (inward, outward, other)[link]
        return pltpu.make_async_remote_copy(
            src_ref=piece(source, lane, p), dst_ref=piece(target, lane, p),
            send_sem=send_sem.at[link, kind, p], recv_sem=recv_sem.at[target, lane, p],
            device_id={"row": row}, device_id_type=MESH,
        )

    def arrived(target, lane, p):
        dst = piece(target, lane, p)
        pltpu.make_async_remote_copy(
            src_ref=dst, dst_ref=dst, send_sem=send_sem.at[0, 0, p], recv_sem=recv_sem.at[target, lane, p],
            device_id={"row": other}, device_id_type=MESH,
        ).wait_recv()

    def each(low, high, body):
        def run(h, carry):
            body(h)
            return carry
        lax.fori_loop(low, high, run, 0)

    corner_sends = {
        "own_in": (IN, 0, 0, 2, y), "own_y": (Y, 0, 0, 0, y),
        "extra": (IN, 1, 0, 2, 1 - y),
        "near_y": (Y, 1, 1, 1, y), "third_y": (Y, 2, 2, 2, y), "last_y": (Y, 3, 3, 3, y),
    }
    middle_sends = {
        "own_out": (OUT, 0, 0, 1, y), "own_in": (IN, 0, 0, 1, y), "own_y": (Y, 0, 0, 0, y),
        "third_in": (IN, 1, 2, 3, y),
        "near_out": (OUT, 1, 1, 2, y), "near_y": (Y, 1, 1, 1, y),
        "last_out": (OUT, 2, 3, 3, y), "last_y": (Y, 2, 3, 3, y),
        "extra": (OUT, 3, 3, 3, 1 - y),
    }

    def at_corner(name, p):
        return copy(*corner_sends[name], p)

    def at_middle(name, p):
        return copy(*middle_sends[name], p)

    @pl.when(corner)
    def _():
        def go(p):
            at_corner("own_in", p).start()
            at_corner("own_y", p).start()
        each(0, pieces, go)

    @pl.when(middle)
    def _():
        def go(p):
            at_middle("own_out", p).start()
            at_middle("own_in", p).start()
            at_middle("own_y", p).start()
        each(0, pieces, go)

    for load in loads[3:]:
        load.start()
    acc[...] = jnp.zeros_like(acc)
    block_bits, half_bits = log2(block), log2(half)

    def split(g):
        row_block = g >> block_bits
        within = g & (block - 1)
        source = (row_block >> log2(BR_DEV)) * cols + (within >> half_bits)
        local = (row_block & (BR_DEV - 1)) * half + (within & (half - 1))
        return source, local

    def ranks(masks):
        before = lax.broadcasted_iota(jnp.int32, (orbs, orbs), 0)
        after = lax.broadcasted_iota(jnp.int32, (orbs, orbs), 1)
        upper = jnp.where(before <= after, 1.0, 0.0).astype(jnp.bfloat16)
        seen = jnp.zeros((masks[0].shape[0], 1), jnp.float32)
        result = []
        for mask in masks:
            counted = jnp.dot(mask.astype(jnp.bfloat16), upper, preferred_element_type=jnp.float32)
            result.append(counted - 1.0 + seen)
            seen = seen + jnp.sum(mask, axis=1, keepdims=True)
        return result

    def place_basis():
        loads[1].wait()
        loads[2].wait()
        masks = []
        peer_id = lax.broadcasted_iota(jnp.int32, (peers, orbs), 0)
        for n in range(boxes):
            source, _ = split(orb_buf[c, r, n:n + 1, :])
            masks.append(jnp.where(peer_id == source, 1.0, 0.0))
        order = ranks(masks)
        arrive = lax.broadcasted_iota(jnp.int32, (peers * capacity, orbs), 0).astype(jnp.float32)
        for n in range(boxes):
            position = jnp.sum(
                masks[n] * (order[n] + (peer_id * capacity).astype(jnp.float32)), axis=0, keepdims=True)
            hot = jnp.where(arrive == position, 1.0, 0.0).astype(jnp.bfloat16)
            placed = jnp.dot(hot, basis_buf[n], preferred_element_type=jnp.float32).astype(jnp.bfloat16)
            early = basis_hot.shape[1]
            basis_hot[n] = placed[:early]
            late_basis[n] = placed[early:]

    def orb_copy(k):
        return pltpu.make_async_remote_copy(
            src_ref=orbitals, dst_ref=orb_buf.at[c, r], send_sem=orb_send.at[k], recv_sem=orb_recv.at[k],
            device_id={"row": (r + k) % rows}, device_id_type=MESH,
        )

    def orb_block(col):
        return pltpu.make_async_remote_copy(
            src_ref=orb_buf.at[col], dst_ref=orb_buf.at[col], send_sem=orb_send.at[0], recv_sem=orb_recv.at[0],
            device_id={"col": 1 - c}, device_id_type=MESH,
        )

    def pass_orbitals():
        for k in range(1, rows):
            dst = orb_buf.at[c, (r + rows - k) % rows]
            pltpu.make_async_remote_copy(
                src_ref=dst, dst_ref=dst, send_sem=orb_send.at[k], recv_sem=orb_recv.at[k],
                device_id={"row": other}, device_id_type=MESH,
            ).wait_recv()
        orb_block(c).start()

    def rank_orbitals():
        orb_block(1 - c).wait_recv()
        asked = []
        for n in range(boxes):
            g = jnp.concatenate([orb_buf[q % cols, q // cols, n:n + 1, :] for q in range(peers)], axis=0)
            source, local = split(g)
            asked.append((jnp.where(source == me, 1.0, 0.0), local.astype(jnp.float32)))
        order = ranks([a[0] for a in asked])
        for n in range(boxes):
            order_buf[n] = jnp.where(asked[n][0] > 0.5, order[n], -1.0)
            local_buf[n] = asked[n][1] + 1.0

    def place_picks(q):
        place = lax.broadcasted_iota(jnp.int32, (capacity, orbs), 0).astype(jnp.float32)
        row_id = lax.broadcasted_iota(jnp.int32, (capacity, BR_DEV * half), 1).astype(jnp.float32)
        found = jnp.zeros((capacity, 1), jnp.float32)
        for n in range(boxes):
            hit = place == order_buf[n, pl.ds(q, 1), :]
            found = found + jnp.sum(jnp.where(hit, local_buf[n, pl.ds(q, 1), :], 0.0), axis=1, keepdims=True)
        spot_rows = pl.ds(pl.multiple_of(q * capacity, capacity), capacity)
        pick_hot[spot_rows, :] = jnp.where(row_id == found - 1.0, 1.0, 0.0).astype(jnp.bfloat16)

    def product(which, t, out_rows):
        j = tcol_ref[t]
        offset = pl.multiple_of(places[which] * pair, pair)
        left = jnp.concatenate(
            [tile_buf[t, 0, out_rows, pl.ds(offset, pair)], tile_buf[t, 1, out_rows, pl.ds(offset, pair)]], axis=1)
        parts = [buffers[which][k, j] for k in range(lanes_y)]
        real = jnp.concatenate([p[0] for p in parts], axis=0)
        imag = jnp.concatenate([p[1] for p in parts], axis=0)
        right = jnp.concatenate(
            [jnp.concatenate([real, imag], axis=1), jnp.concatenate([-imag, real], axis=1)], axis=0)
        return jnp.dot(left, right, preferred_element_type=jnp.float32)

    def several(which, start, count, out_rows):
        values = [product(which, start + k, out_rows) for k in range(count)]
        for s in range(BR_DEV):
            total = jnp.where(slot_ref[start] == s, values[0], 0.0)
            for k in range(1, count):
                total = total + jnp.where(slot_ref[start + k] == s, values[k], 0.0)
            acc[s, out_rows, :] += total

    everything = pl.ds(0, block)

    def share(which, p, parts):
        first_tile, last_tile = p * tile_count // parts, (p + 1) * tile_count // parts
        for start in range(first_tile, last_tile, 4):
            several(which, start, min(4, last_tile - start), everything)

    place_basis()

    def first(p):
        @pl.when(corner)
        def _():
            arrived(1, y, p)
            at_corner("near_y", p).start()
            arrived(0, 1 - y, p)
            at_corner("extra", p).start()

        @pl.when(middle)
        def _():
            arrived(2, y, p)
            at_middle("third_in", p).start()
            arrived(1, y, p)
            at_middle("near_out", p).start()
            at_middle("near_y", p).start()

            @pl.when(p == 0)
            def _():
                pl.semaphore_signal(token.at[0], inc=1, device_id={"row": inward}, device_id_type=MESH)

            @pl.when(p == pieces - 1)
            def _():
                pl.semaphore_wait(token.at[0], 1)
                pl.semaphore_signal(token.at[1], inc=1, device_id={"row": outward}, device_id_type=MESH)

    each(0, pieces, first)

    @pl.when(corner)
    def _():
        pl.semaphore_wait(token.at[1], 1)

    for k in range(1, rows):
        orb_copy(k).start()

    @pl.when(middle)
    def _():
        each(0, pieces, lambda p: arrived(0, 1 - y, p))

    loads[3].wait()
    for load in loads[5:]:
        load.wait()

    def second(p):
        @pl.when(corner)
        def _():
            arrived(2, y, p)
            at_corner("third_y", p).start()

        @pl.when(middle)
        def _():
            arrived(3, y, p)
            at_middle("last_out", p).start()
            if p >= split_at:
                at_middle("last_y", p).start()

        share(0, p, pieces)

    for p in range(pieces):
        second(p)

    @pl.when(middle)
    def _():
        each(0, split_at, lambda p: at_middle("last_y", p).start())

    each(0, pieces, lambda p: arrived(1, 1 - y, p))

    def closing(p):
        share(1, p, split_at)

        @pl.when(corner)
        def _():
            arrived(3, y, p)
            at_corner("last_y", p).start()

        @pl.when(middle)
        def _():
            arrived(3, 1 - y, p + split_at)
            at_middle("extra", p + split_at).start()

    for p in range(split_at):
        closing(p)
    pass_orbitals()
    each(0, pieces, lambda p: arrived(2, 1 - y, p))
    share(2, 0, 1)
    rank_orbitals()
    each(0, peers // 4, lambda q: [place_picks(4 * q + k) for k in range(4)])

    @pl.when(corner)
    def _():
        each(split_at, pieces, lambda p: arrived(3, y, p))
        each(split_at, pieces, lambda p: arrived(3, 1 - y, p))
    each(0, split_at, lambda p: arrived(3, 1 - y, p))

    mine = pl.ds(pl.multiple_of(c * half, half), half)
    theirs = pl.ds(pl.multiple_of((1 - c) * half, half), half)

    def to_partner(which, src, dst):
        return pltpu.make_async_remote_copy(
            src_ref=src, dst_ref=dst, send_sem=col_sem.at[0, which], recv_sem=col_sem.at[1, which],
            device_id={"col": 1 - c}, device_id_type=MESH,
        )

    mix_swap = to_partner(0, mix_out, mix_in)
    swap = to_partner(1, acc.at[:, theirs, :], half_in)

    def mixed(s, out_rows):
        return weight_ref[0] * acc[s, out_rows, width:] + weight_ref[1] * acc[s, out_rows, :width]

    for start in range(0, tile_count, 4):
        several(3, start, min(4, tile_count - start), theirs)
    for s in range(BR_DEV):
        mix_out[s] = mixed(s, theirs)
    mix_swap.start()
    for start in range(0, tile_count, 4):
        several(3, start, min(4, tile_count - start), mine)
    for s in range(BR_DEV):
        mix_own[s] = mixed(s, mine)
    mix_swap.wait_recv()
    density_rows = [(-(mix_own[s] + mix_in[s])).astype(jnp.bfloat16) for s in range(BR_DEV)]
    density_rows = jnp.concatenate(density_rows, axis=0)

    group = lanes_y * cols

    def row_copy(target):
        return pltpu.make_async_remote_copy(
            src_ref=send_rows.at[target], dst_ref=recv_rows.at[me],
            send_sem=row_send.at[target], recv_sem=row_recv.at[me],
            device_id=spot(target), device_id_type=MESH,
        )

    for k in range(depth_z - 1):
        for part in range(lanes_y):
            count = cols
            base = (k + jnp.where(k >= z, 1, 0)) * group + part * count
            hot = pick_hot[pl.ds(pl.multiple_of(base * capacity, count * capacity), count * capacity), :]
            picked = jnp.dot(hot, density_rows, preferred_element_type=jnp.float32).astype(jnp.bfloat16)
            send_rows[pl.ds(base, count)] = picked.reshape(count, capacity, width)
            for lane in range(count):
                row_copy(base + lane).start()
    base = z * group
    hot = pick_hot[pl.ds(pl.multiple_of(base * capacity, group * capacity), group * capacity), :]
    picked = jnp.dot(hot, density_rows, preferred_element_type=jnp.float32).astype(jnp.bfloat16)
    send_rows[pl.ds(base, group)] = picked.reshape(group, capacity, width)
    for k in range(1, group):
        row_copy(base + (me - base + k) % group).start()
    swap.start()
    recv_rows[me] = send_rows[me]
    swap.wait_recv()
    for s in range(BR_DEV):
        column = -(acc[s, mine, :] + half_in[s])
        inv_ref[s, 0] = column[:, :width]
        inv_ref[s, 1] = column[:, width:]
    loads[4].wait()

    @pl.when(corner)
    def _():
        def sent(p):
            for name in corner_sends:
                if name != "last_y":
                    at_corner(name, p).wait_send()
        each(0, pieces, sent)
        each(0, split_at, lambda p: at_corner("last_y", p).wait_send())

    @pl.when(middle)
    def _():
        def sent(p):
            for name in middle_sends:
                if name != "extra":
                    at_middle(name, p).wait_send()
        each(0, pieces, sent)
        each(split_at, pieces, lambda p: at_middle("extra", p).wait_send())

    mix_swap.wait_send()
    swap.wait_send()
    for k in range(1, rows):
        orb_copy(k).wait_send()
    orb_block(c).wait_send()

    projected = [None] * boxes
    for at_z in range(depth_z):
        if at_z == depth_z - 1:
            for k in range(1, peers):
                row_copy((me + k) % peers).wait_send()
        for origin in range(at_z * group, (at_z + 1) * group):
            @pl.when(me != origin)
            def _(origin=origin):
                dst = recv_rows.at[origin]
                pltpu.make_async_remote_copy(
                    src_ref=dst, dst_ref=dst, send_sem=row_send.at[origin], recv_sem=row_recv.at[origin],
                    device_id={"row": other}, device_id_type=MESH,
                ).wait_recv()
        if at_z == depth_z - 1:
            late_rows[...] = recv_rows[at_z * group:(at_z + 1) * group]
            continue
        got = recv_rows[at_z * group:(at_z + 1) * group].reshape(group * capacity, width)
        for n in range(boxes):
            value = lax.dot_general(
                got, basis_hot[n, at_z * group * capacity:(at_z + 1) * group * capacity, :],
                (((0,), (0,)), ((), ())), preferred_element_type=jnp.float32)
            projected[n] = value if at_z == 0 else projected[n] + value
        if at_z == depth_z - 2:
            for n in range(boxes):
                projected_ref[n] = projected[n]


def deliver(column, projected, late_rows, late_basis, super_basis, column_out, density_out, density, sem):
    column_copy = pltpu.make_async_copy(column, column_out, sem.at[0])
    column_copy.start()
    boxes, width, _ = projected.shape
    got = late_rows[...].reshape(late_basis.shape[1], width)
    for n in range(boxes):
        value = projected[n] + lax.dot_general(
            got, late_basis[n], (((0,), (0,)), ((), ())), preferred_element_type=jnp.float32)
        density[n:n + 1, :] = jnp.sum(super_basis[n].astype(jnp.float32) * value, axis=0, keepdims=True)
    density_copy = pltpu.make_async_copy(density, density_out, sem.at[1])
    density_copy.start()
    density_copy.wait()
    column_copy.wait()


def fused(rows, cols, panel, tiles, tile_slot, tile_col, pole_weight, box_orbitals, box_basis, supernode_basis):
    blocks, parts, shard_rows, width = panel.shape[1:]
    tile_count, _, block, _ = tiles.shape
    boxes, orbs = box_orbitals.shape
    points = box_basis.shape[2]
    half = block // cols
    peers = rows * cols
    capacity = 2 * boxes * orbs // peers
    pieces = blocks // 2
    dma = pltpu.SemaphoreType.DMA
    bf16, f32 = jnp.bfloat16, jnp.float32
    hbm = pl.BlockSpec(memory_space=pl.ANY)
    vmem = pl.BlockSpec(memory_space=pltpu.VMEM)
    late = 2 * cols * capacity
    results = pl.pallas_call(
        functools.partial(kernel, rows, cols),
        name="pole_step",
        out_shape=(
            pltpu.VMEM((BR_DEV, 2, half, width), f32),
            pltpu.VMEM((boxes, width, points), f32),
            pltpu.VMEM((2 * cols, capacity, width), bf16),
            pltpu.VMEM((boxes, late, points), bf16),
            pltpu.VMEM(supernode_basis.shape, bf16),
        ),
        in_specs=[hbm] * 8,
        out_specs=(vmem,) * 5,
        scratch_shapes=[
            pltpu.SMEM(tile_slot.shape, jnp.int32),
            pltpu.SMEM(tile_col.shape, jnp.int32),
            pltpu.SMEM(pole_weight.shape, f32),
        ] + [pltpu.VMEM((2, blocks, parts, shard_rows, width), bf16)] * 4 + [
            pltpu.VMEM(tiles.shape, bf16),
            pltpu.VMEM(box_basis.shape, bf16),
            pltpu.VMEM((cols, rows, boxes, orbs), jnp.int32),
            pltpu.VMEM((BR_DEV, block, 2 * width), f32),
            pltpu.VMEM((BR_DEV, half, 2 * width), f32),
            pltpu.VMEM((BR_DEV, half, width), f32),
            pltpu.VMEM((BR_DEV, half, width), f32),
            pltpu.VMEM((BR_DEV, half, width), f32),
            pltpu.VMEM((peers * capacity, BR_DEV * half), bf16),
            pltpu.VMEM((boxes, peers * capacity - late, points), bf16),
            pltpu.VMEM((boxes, peers, orbs), f32),
            pltpu.VMEM((boxes, peers, orbs), f32),
            pltpu.VMEM((peers, capacity, width), bf16),
            pltpu.VMEM((peers, capacity, width), bf16),
            dma((8,)),
            dma((3, 4, pieces)),
            dma((4, 2, pieces)),
            pltpu.SemaphoreType.REGULAR((2,)),
            dma((2, 2)),
            dma((peers,)),
            dma((peers,)),
            dma((peers,)),
            dma((peers,)),
        ],
        compiler_params=pltpu.CompilerParams(
            collective_id=0, has_side_effects=True, vmem_limit_bytes=56 * 1024 * 1024),
    )(tile_slot, tile_col, pole_weight, panel, tiles, box_orbitals, box_basis, supernode_basis)
    return pl.pallas_call(
        deliver,
        name="deliver",
        out_shape=(
            jax.ShapeDtypeStruct((BR_DEV, 2, half, width), f32),
            jax.ShapeDtypeStruct((boxes, points), f32),
        ),
        in_specs=[vmem] * 5,
        out_specs=(hbm, hbm),
        scratch_shapes=[pltpu.VMEM((boxes, points), f32), dma((2,))],
        compiler_params=pltpu.CompilerParams(vmem_limit_bytes=8 * 1024 * 1024),
    )(*results)


def plain(panel, tiles, tile_slot, tile_col, pole_weight, box_orbitals, box_basis, supernode_basis):
    gathered = lax.all_gather(panel, "row", axis=3, tiled=True)
    blocks = gathered[0]
    selector = (tile_col[:, None] == jnp.arange(blocks.shape[0], dtype=jnp.int32)[None, :]).astype(
        jnp.bfloat16
    )
    chosen = jnp.einsum(
        "tj,jcbs->tcbs", selector, blocks, preferred_element_type=jnp.float32
    ).astype(jnp.bfloat16)
    real_part = jnp.einsum(
        "tab,tbs->tas", tiles[:, 0], chosen[:, 0], preferred_element_type=jnp.float32
    )
    real_part = real_part - jnp.einsum(
        "tab,tbs->tas", tiles[:, 1], chosen[:, 1], preferred_element_type=jnp.float32
    )
    imag_part = jnp.einsum(
        "tab,tbs->tas", tiles[:, 0], chosen[:, 1], preferred_element_type=jnp.float32
    )
    imag_part = imag_part + jnp.einsum(
        "tab,tbs->tas", tiles[:, 1], chosen[:, 0], preferred_element_type=jnp.float32
    )
    products = jnp.stack([real_part, imag_part], axis=1)
    partial_value = jnp.stack(
        [
            jnp.sum(jnp.where((tile_slot == slot_row)[:, None, None, None], products, 0.0), axis=0)
            for slot_row in range(BR_DEV)
        ]
    )
    summed = lax.psum_scatter(partial_value, "col", scatter_dimension=2, tiled=True)
    inverse_column = -summed
    density_local = (
        pole_weight[0] * inverse_column[:, 1] + pole_weight[1] * inverse_column[:, 0]
    ).astype(jnp.bfloat16)
    columns = density_local.shape[2]
    density_local = density_local.reshape(-1, columns)
    block_width = tiles.shape[2]
    col_count = lax.axis_size("col")
    half_rows = block_width // col_count
    wanted = box_orbitals.reshape(-1)
    wanted_total = wanted.shape[0]
    block_index = wanted // block_width
    within = wanted % block_width
    source = block_index // BR_DEV * col_count + within // half_rows
    local_row = block_index % BR_DEV * half_rows + within % half_rows
    start_rows = jnp.zeros((wanted_total, columns), jnp.bfloat16)
    shards = lax.all_gather(density_local[None], ("row", "col"), axis=0, tiled=True)
    count = shards.shape[0]
    inside = (source >= 0) & (source < count)
    clipped = jnp.clip(source, 0, count - 1)
    fetched = shards[clipped, local_row]
    picked = jnp.where(inside[:, None], fetched, start_rows)
    picked = picked.reshape(box_basis.shape[0], box_basis.shape[1], columns)
    projected = jnp.einsum("nas,nap->nsp", picked, box_basis, preferred_element_type=jnp.float32)
    density = jnp.sum(supernode_basis.astype(jnp.float32) * projected, axis=1)
    return (inverse_column, density)


def solution(mesh):
    rows, cols = mesh.shape["row"], mesh.shape["col"]

    def local(panel, *rest):
        if cols == 2 and rows == 8 and panel.shape[1] % 8 == 0 and 2 * panel.shape[3] % panel.shape[4] == 0:
            return fused(rows, cols, panel, *rest)
        return plain(panel, *rest)

    return jax.shard_map(
        local,
        mesh=mesh,
        in_specs=(
            P(("pole", "col"), None, None, "row", None),
            P(("pole", "row", "col"), None, None, None),
            P(("pole", "row", "col")),
            P(("pole", "row", "col")),
            P("pole"),
            P(("pole", "row", "col"), None),
            P(("pole", "row", "col"), None, None),
            P(("pole", "row", "col"), None, None),
        ),
        out_specs=(P(("pole", "row"), None, "col", None), P(("pole", "row", "col"), None)),
        check_vma=False,
    )
```
